128 devices in a mesh: mat: 8 (over x, core), frac: 16 (over z, y).
Axes of the slice: x: 4, y: 4, z: 4, core: 2. Of those that a mesh axis runs over, the one named last changes fastest.
Arguments:
- pressure_start: float32 [128, 1024, 256], P('mat', 'frac'), may hold values from -6 to 6
- face_trans: float32 [3, 128, 1024, 256], P(None, 'mat', 'frac'), may hold values from 0.2 to 2
- cell_coef: float32 [128, 1024, 256], P('mat', 'frac'), may hold values from 0.05 to 0.5
- matrix_source: float32 [128, 1024, 256], P('mat', 'frac'), may hold values from -6 to 6
- mortar_owner: int32 [65536, 1], P(('mat', 'frac')), may hold values from 0 to 127; in each aligned block of 512 rows (0 to 511, 512 to 1023, ...) at most 8 rows name the same one
- mortar_cell: int32 [65536], P(('mat', 'frac')), may hold values from 0 to 262143
- mortar_frac: int32 [65536], P(('mat', 'frac')), may hold values from 0 to 16383
- mortar_kappa: float32 [65536], P(('mat', 'frac')), may hold values from 0.5 to 2
- tiles: float32 [128, 4, 128, 128], P('frac'), may hold values from -0.25 to 0.25
- tile_cols: int32 [128, 4], P('frac'), may hold values from 0 to 127
- frac_diag: float32 [16384], P('frac'), may hold values from 4 to 8
- frac_source: float32 [16384], P('frac'), may hold values from -6 to 6
- fracture_start: float32 [16384], P('frac'), may hold values from -6 to 6
Outputs:
- pressure: float32 [128, 1024, 256], P('mat', 'frac')
- fracture: float32 [16384], P('frac')
- flux: float32 [65536], P(('mat', 'frac'))
The draws below stay inside these ranges and needn't reach their ends.
Inputs may be any that keep to these rules, and one draw needn't show every extreme that they name: `mortar_owner`: among the 512 mortar cells of one device, at most 8 name the same owner, and in some devices some owner is named exactly 8 times.
All inputs are finite; a program needn't handle non-finite values.
Results may differ from the reference program's by a relative error of at most 0.00015.
Values sent between devices are 32-bit elements; how exact they have to be, the bound alone decides.
No kernel may reach another device: no remote copies, remote signals or barrier semaphores. Data moves between devices by JAX's collectives and lax.ppermute only.
A program may use at most 128 MiB of HBM per device.

```python
import math
import jax
import jax.numpy as jnp
import numpy as np
from jax import lax

CX = 16
CY = 64
CZ = 256
MORT_DEV = 512
B = 128
TILES = 4
SWEEPS = 2
CG_ITERS = 3
OUTER = 2
NX = 128
NY = 1024
CELLS = 262144
NB = 128
NF = 16384
M = 65536
CAP = 8
N_MAT = 8
N_FRAC = 16
DEVICES = 128


def set_ends(values, key, low, high):
    longest = values.shape.index(max(values.shape))
    spots = []
    for shift in (0, 1):
        where = [jax.random.randint(jax.random.fold_in(key, axis), (), 0, length) for axis, length in enumerate(values.shape)]
        where[longest] = (where[longest] + shift) % values.shape[longest]
        spots.append(tuple(where))
    return values.at[spots[0]].set(low).at[spots[1]].set(high)


def block_levels(own_key, shape, pieces, smallest, top_value):
    level = 1.0
    for dim, parts in pieces:
        draws = jax.random.uniform(jax.random.fold_in(jax.random.fold_in(own_key, 6), dim), (parts,), jnp.float32, smallest / len(pieces), top_value / len(pieces))
        level = level * jnp.repeat(jnp.exp(draws), shape[dim] // parts).reshape((-1,) + (1,) * (len(shape) - 1 - dim))
    return level


def shared_out(rng, own, number, rows, amount, top, most, slope):
    order = jax.random.permutation(rng, amount)
    crowded, ordinary = shares(amount, rows * top, most, slope, True), shares(amount, rows * top, most, slope, False)
    places = jnp.arange(amount)

    def named(lengths, turn):
        used = int((lengths > 0).sum())
        fixed = max(1, used // 4)
        moved = fixed + (places - fixed + turn * (used - fixed)) % max(1, amount - fixed)
        return jnp.zeros((amount,), jnp.int32).at[order[jnp.where(places < fixed, places, moved)]].set(jnp.asarray(lengths, jnp.int32))

    lengths = jnp.where(number % 4 == 0, named(crowded, number // 4), named(ordinary, number - number // 4 - 1))
    mixed = jax.random.permutation(jax.random.fold_in(own, 3), amount)
    donor, taker = mixed[0:amount // 2 * 2:2], mixed[1:amount // 2 * 2:2]
    slack = jnp.minimum(lengths[donor] - 1, most - lengths[taker]) // 2
    slack = jnp.where((donor == order[0]) | (taker == order[0]) | (lengths[taker] == 0), 0, jnp.maximum(slack, 0))
    moved = jax.random.randint(jax.random.fold_in(own, 4), (amount // 2,), 0, 1 << 20) % (slack + 1)
    lengths = lengths.at[donor].add(-moved).at[taker].add(moved)
    labels = jnp.searchsorted(jnp.cumsum(lengths), jnp.arange(rows * top), side="right").astype(jnp.int32)
    grid = labels.reshape(top, rows).T
    grid = grid[jax.random.permutation(jax.random.fold_in(own, 1), rows)]
    turn = jax.random.randint(jax.random.fold_in(own, 2), (rows, 1), 0, top)
    return jnp.take_along_axis(grid, (jnp.arange(top)[None, :] + turn) % top, axis=1)


def shares(count, total, limit, lean, full):
    portions = [(1 << 20) // math.isqrt(standing ** lean) + 1 for standing in range(1, count + 1)]
    largest = limit if full else min(limit, max(-(-total // count), total * portions[0] // sum(portions)))
    least = 1 if total - largest >= count - 1 else 0
    given, surplus = [largest] + [least] * (count - 1), total - largest - least * (count - 1)
    while surplus > 0:
        movable = [i for i in range(1, count) if given[i] < largest] or [i for i in range(1, count) if given[i] < limit]
        whole, left = sum([portions[i] for i in movable]), surplus
        for i in movable:
            addition = min(limit - given[i], max(1, left * portions[i] // whole), surplus)
            given[i] = given[i] + addition
            surplus = surplus - addition
    return np.array(given)


def normal_values(rng, extent, scale, limit, split=(), dtype=jnp.bfloat16):
    values = scale * jax.random.normal(rng, extent, jnp.float32)
    if split:
        values = values * block_levels(rng, extent, split, -0.22, 0.18)
    return jnp.clip(values, -limit, limit).astype(dtype)


def setup_inputs(seed: int = 0) -> dict:
    seeds = jax.random.split(jax.random.key(seed), 14)
    pressure_start = normal_values(seeds[0], (NX, NY, CZ), 1.0, 6.0, ((0, 8), (1, 16)), jnp.float32)
    face_trans = jnp.clip(jnp.exp(math.log(2.0) - 2.3025851 * jax.random.uniform(seeds[1], (3, NX, NY, CZ), jnp.float32) ** block_levels(seeds[1], (3, NX, NY, CZ), ((1, 8), (2, 16)), -0.2, 0.2)), 0.2, 2.0)
    cell_coef = jnp.clip(jnp.exp(math.log(0.5) - 2.3025851 * jax.random.uniform(seeds[2], (NX, NY, CZ), jnp.float32) ** block_levels(seeds[2], (NX, NY, CZ), ((0, 8), (1, 16)), -0.2, 0.2)), 0.05, 0.5)
    matrix_source = normal_values(seeds[3], (NX, NY, CZ), 1.0, 6.0, ((0, 8), (1, 16)), jnp.float32)
    mortar_owner_keys = jax.random.split(jax.random.fold_in(seeds[4], 1), M // MORT_DEV)
    mortar_owner_turns = jax.random.permutation(jax.random.fold_in(seeds[4], 3), M // MORT_DEV)
    mortar_owner = jax.vmap(lambda own, number: shared_out(jax.random.fold_in(seeds[4], 2), own, number, MORT_DEV, DEVICES, 1, CAP, 2))(mortar_owner_keys, mortar_owner_turns).reshape((M, 1))
    mortar_cell = set_ends(jax.random.randint(seeds[5], (M,), 0, CELLS), jax.random.fold_in(seeds[5], 1), 0, CELLS - 1).astype(jnp.int32)
    mortar_frac = set_ends(jax.random.randint(seeds[6], (M,), 0, NF), jax.random.fold_in(seeds[6], 1), 0, NF - 1).astype(jnp.int32)
    mortar_kappa = jnp.clip(jnp.exp(math.log(2.0) - 1.3862944 * jax.random.uniform(seeds[7], (M,), jnp.float32) ** block_levels(seeds[7], (M,), ((0, 128),), -0.2, 0.2)), 0.5, 2.0)
    tiles = normal_values(seeds[8], (NB, TILES, B, B), (TILES * B) ** -0.5, 0.25, ((0, 16),), jnp.float32)
    tile_cols = set_ends(jax.random.randint(seeds[9], (NB, TILES), 0, NB), jax.random.fold_in(seeds[9], 1), 0, NB - 1).astype(jnp.int32)
    frac_diag = jnp.clip(jnp.exp(math.log(8.0) - 0.6931472 * jax.random.uniform(seeds[10], (NF,), jnp.float32) ** block_levels(seeds[10], (NF,), ((0, 16),), -0.2, 0.2)), 4.0, 8.0)
    frac_source = normal_values(seeds[11], (NF,), 1.0, 6.0, ((0, 16),), jnp.float32)
    fracture_start = normal_values(seeds[12], (NF,), 1.0, 6.0, ((0, 16),), jnp.float32)
    return {"pressure_start": pressure_start, "face_trans": face_trans, "cell_coef": cell_coef, "matrix_source": matrix_source, "mortar_owner": mortar_owner, "mortar_cell": mortar_cell, "mortar_frac": mortar_frac, "mortar_kappa": mortar_kappa, "tiles": tiles, "tile_cols": tile_cols, "frac_diag": frac_diag, "frac_source": frac_source, "fracture_start": fracture_start}


relax_weight = 0.8


def shift_next(values, along):
    padding = [(0, 0)] * values.ndim
    padding[along] = (0, 1)
    return lax.slice_in_dim(jnp.pad(values, padding), 1, values.shape[along] + 1, axis=along)


def shift_prev(values, along):
    padding = [(0, 0)] * values.ndim
    padding[along] = (1, 0)
    return lax.slice_in_dim(jnp.pad(values, padding), 0, values.shape[along], axis=along)


def relax_grid(pressure, face_trans, cell_coef, matrix_source, source):
    tx_low = shift_prev(face_trans[0], 0)
    ty_low = shift_prev(face_trans[1], 1)
    tz_low = shift_prev(face_trans[2], 2)
    diagonal = cell_coef + face_trans[0] + tx_low + face_trans[1] + ty_low + face_trans[2] + tz_low
    applied = (diagonal * pressure - face_trans[0] * shift_next(pressure, 0) - tx_low * shift_prev(pressure, 0)
               - face_trans[1] * shift_next(pressure, 1) - ty_low * shift_prev(pressure, 1)
               - face_trans[2] * shift_next(pressure, 2) - tz_low * shift_prev(pressure, 2))
    return pressure + relax_weight * (matrix_source + source - applied) / diagonal


def fracture_apply(vector, tiles, tile_cols, frac_diag):
    size_b = tiles.shape[2]
    blocks = vector.reshape(-1, size_b)
    forward = jnp.einsum("rtij,rtj->ri", tiles, blocks[tile_cols], precision=lax.Precision.HIGHEST)
    backward = jnp.einsum("rtij,ri->rtj", tiles, blocks, precision=lax.Precision.HIGHEST)
    spread = jnp.zeros_like(blocks).at[tile_cols.reshape(-1)].add(backward.reshape(-1, size_b))
    return frac_diag * vector + 0.5 * (forward + spread).reshape(-1)


def reference(pressure_start, face_trans, cell_coef, matrix_source, mortar_owner, mortar_cell, mortar_frac, mortar_kappa, tiles, tile_cols, frac_diag, frac_source, fracture_start):
    cells = CX * CY * CZ
    pressure = pressure_start
    fracture = fracture_start
    place = mortar_owner[:, 0].astype(jnp.int32) * cells + mortar_cell.astype(jnp.int32)
    flux = jnp.zeros(mortar_kappa.shape, jnp.float32)
    for outer_no in range(OUTER):
        by_device = pressure.reshape(N_MAT, CX, N_FRAC, CY, CZ).transpose(0, 2, 1, 3, 4).reshape(-1)
        trace = by_device[place]
        flux = mortar_kappa * (trace - fracture[mortar_frac])
        load = jnp.zeros(fracture.shape, jnp.float32).at[mortar_frac].add(flux)
        target = frac_source + load
        residual = target - fracture_apply(fracture, tiles, tile_cols, frac_diag)
        direction = residual
        norm_now = jnp.sum(residual * residual)
        for step in range(CG_ITERS):
            image = fracture_apply(direction, tiles, tile_cols, frac_diag)
            alpha = norm_now / jnp.sum(direction * image)
            fracture = fracture + alpha * direction
            residual = residual - alpha * image
            norm_next = jnp.sum(residual * residual)
            direction = residual + (norm_next / norm_now) * direction
            norm_now = norm_next
        landed = jnp.zeros(by_device.shape, jnp.float32).at[place].add(flux)
        source = landed.reshape(N_MAT, N_FRAC, CX, CY, CZ).transpose(0, 2, 1, 3, 4).reshape(pressure.shape)
        for sweep_no in range(SWEEPS):
            pressure = relax_grid(pressure, face_trans, cell_coef, matrix_source, source)
    return pressure, fracture, flux
```

```python
import jax
import jax.numpy as jnp
from jax import lax
from jax.sharding import PartitionSpec as P

SWEEPS = 2
CG_ITERS = 3
OUTER = 2


relax_weight = 0.8


def with_halo(block, sides, width):
    for axis, dim in sides:
        count = lax.axis_size(axis)
        forward = [(i, i + 1) for i in range(count - 1)]
        backward = [(target, source) for source, target in forward]
        low = lax.ppermute(
            lax.slice_in_dim(block, block.shape[dim] - width, None, axis=dim), axis, forward
        )
        high = lax.ppermute(lax.slice_in_dim(block, 0, width, axis=dim), axis, backward)
        block = jnp.concatenate([low, block, high], axis=dim)
    return block


def copy_for_each(x, axis):
    length = lax.axis_size(axis)
    return lax.all_to_all(jnp.broadcast_to(x[None], (length, *x.shape)), axis, 0, 0, tiled=True)


def in_order(blocks, dim):
    lengths = list(blocks.shape[1:])
    lengths[dim] *= blocks.shape[0]
    return jnp.moveaxis(blocks, 0, dim).reshape(lengths)


def gather_directly(x, axis, dim):
    blocks = copy_for_each(x, axis)
    return in_order(blocks, dim)


def split_up(x, dim, length):
    lengths = x.shape
    blocks = x.reshape(*lengths[:dim], length, lengths[dim] // length, *lengths[dim + 1 :])
    return jnp.moveaxis(blocks, dim, 0)


def summed_on_arrival(x, axis, dim):
    length = lax.axis_size(axis)
    blocks = lax.all_to_all(split_up(x, dim, length), axis, 0, 0, tiled=True)
    return jnp.sum(blocks, axis=0)


def of_everyone(x, axis):
    return copy_for_each(x, axis).sum(axis=0)


def in_one(arrays, axis):
    ends = [0]
    for a in arrays:
        ends.append(ends[-1] + a.size)
    running = of_everyone(jnp.concatenate([a.ravel() for a in arrays]), axis)
    return tuple((running[b:e].reshape(a.shape) for a, b, e in zip(arrays, ends, ends[1:])))


def shift_next(values, along):
    padding = [(0, 0)] * values.ndim
    padding[along] = (0, 1)
    return lax.slice_in_dim(jnp.pad(values, padding), 1, values.shape[along] + 1, axis=along)


def shift_prev(values, along):
    padding = [(0, 0)] * values.ndim
    padding[along] = (1, 0)
    return lax.slice_in_dim(jnp.pad(values, padding), 0, values.shape[along], axis=along)


def relax(padded, coef_part, source_part, inside):
    centre = padded[1:-1, 1:-1]
    tx_here = coef_part[0, 1:-1, 1:-1]
    tx_low = coef_part[0, :-2, 1:-1]
    ty_here = coef_part[1, 1:-1, 1:-1]
    ty_low = coef_part[1, 1:-1, :-2]
    tz_here = coef_part[2, 1:-1, 1:-1]
    tz_low = shift_prev(tz_here, 2)
    cell_part = coef_part[3, 1:-1, 1:-1]
    base_part = coef_part[4, 1:-1, 1:-1]
    diagonal = cell_part + tx_here + tx_low + ty_here + ty_low + tz_here + tz_low
    diagonal = jnp.where(inside, diagonal, 1.0)
    applied = (
        diagonal * centre
        - tx_here * padded[2:, 1:-1]
        - tx_low * padded[:-2, 1:-1]
        - ty_here * padded[1:-1, 2:]
        - ty_low * padded[1:-1, :-2]
        - tz_here * shift_next(centre, 2)
        - tz_low * shift_prev(centre, 2)
    )
    updated = centre + relax_weight * (base_part + source_part - applied) / diagonal
    return jnp.where(inside, updated, 0.0)


def body(
    pressure_start,
    face_trans,
    cell_coef,
    matrix_source,
    mortar_owner,
    mortar_cell,
    mortar_frac,
    mortar_kappa,
    tiles,
    tile_cols,
    frac_diag,
    frac_source,
    fracture_start,
):
    width_x, width_y, depth_z = pressure_start.shape
    cells = width_x * width_y * depth_z
    mat_count = lax.axis_size("mat")
    frac_count = lax.axis_size("frac")
    devices = mat_count * frac_count
    row_mat = lax.axis_index("mat")
    row_frac = lax.axis_index("frac")
    size_b = tiles.shape[2]
    coefs = jnp.concatenate([face_trans, cell_coef[None], matrix_source[None]], 0)
    coef_ext = with_halo(coefs, (("mat", 1), ("frac", 2)), SWEEPS)
    owner = mortar_owner[:, 0]
    mortar_count = owner.shape[0]
    capacity = max(2, 2 * mortar_count // devices)
    rows = jnp.arange(mortar_count, dtype=jnp.int32)
    earlier = (owner[:, None] == owner[None, :]) & (rows[None, :] < rows[:, None])
    slot = jnp.sum(earlier.astype(jnp.int32), axis=1)
    place = owner * capacity + slot
    index_slots = (
        jnp.full((devices * capacity,), cells, jnp.int32)
        .at[place]
        .set(mortar_cell)
        .reshape(devices, capacity)
    )
    asked = lax.all_to_all(index_slots, ("mat", "frac"), split_axis=0, concat_axis=0, tiled=True)
    asked_safe = jnp.minimum(asked, cells - 1)

    def fracture_apply(vector):
        whole = gather_directly(vector, "frac", 0)
        blocks = whole.reshape(-1, size_b)
        forward = jnp.einsum(
            "rtij,rtj->ri", tiles, blocks[tile_cols], precision=lax.Precision.HIGHEST
        )
        backward = jnp.einsum(
            "rtij,ri->rtj", tiles, vector.reshape(-1, size_b), precision=lax.Precision.HIGHEST
        )
        spread = jnp.zeros_like(blocks).at[tile_cols.reshape(-1)].add(backward.reshape(-1, size_b))
        returned = summed_on_arrival(spread, "frac", 0)
        return frac_diag * vector + 0.5 * (forward + returned).reshape(-1)

    def two_products(residual, image):
        return in_one((jnp.sum(residual * residual), jnp.sum(residual * image)), "frac")

    def solve_fracture(fracture, target):
        residual = target - fracture_apply(fracture)
        image = fracture_apply(residual)
        norm_now, product = two_products(residual, image)
        alpha = norm_now / product
        direction, along_image = (residual, image)
        for step in range(CG_ITERS):
            fracture = fracture + alpha * direction
            residual = residual - alpha * along_image
            if step + 1 < CG_ITERS:
                image = fracture_apply(residual)
                norm_next, product = two_products(residual, image)
                ratio = norm_next / norm_now
                alpha = norm_next / (product - ratio * norm_next / alpha)
                direction = residual + ratio * direction
                along_image = image + ratio * along_image
                norm_now = norm_next
        return fracture

    pressure = pressure_start
    fracture = fracture_start
    flux = jnp.zeros(mortar_kappa.shape, jnp.float32)
    for outer_no in range(OUTER):
        local_values = pressure.reshape(-1)[asked_safe]
        returned = lax.all_to_all(
            local_values, ("mat", "frac"), split_axis=0, concat_axis=0, tiled=True
        )
        trace = returned.reshape(-1)[place]
        fracture_whole = lax.all_gather(fracture, "frac", axis=0, tiled=True)
        flux = mortar_kappa * (trace - fracture_whole[mortar_frac])
        landed = jax.ops.segment_sum(flux, mortar_frac, num_segments=fracture_whole.shape[0])
        rows_part = summed_on_arrival(landed, "frac", 0)
        load = lax.psum(rows_part, "mat")
        fracture = solve_fracture(fracture, frac_source + load)
        flux_slots = (
            jnp.zeros((devices * capacity,), jnp.float32)
            .at[place]
            .set(flux)
            .reshape(devices, capacity)
        )
        arrived = lax.all_to_all(
            flux_slots, ("mat", "frac"), split_axis=0, concat_axis=0, tiled=True
        )
        source = jax.ops.segment_sum(
            arrived.reshape(-1), asked_safe.reshape(-1), num_segments=cells
        ).reshape(pressure.shape)
        stacked = with_halo(jnp.stack([pressure, source]), (("mat", 1), ("frac", 2)), SWEEPS)
        current = stacked[0]
        source_ext = stacked[1]
        for sweep_no in range(SWEEPS):
            span_x = current.shape[0]
            span_y = current.shape[1]
            coef_part = coef_ext[:, sweep_no : sweep_no + span_x, sweep_no : sweep_no + span_y]
            source_part = source_ext[
                sweep_no + 1 : sweep_no + span_x - 1, sweep_no + 1 : sweep_no + span_y - 1
            ]
            offset = SWEEPS - sweep_no - 1
            global_x = row_mat * width_x - offset + jnp.arange(span_x - 2)
            global_y = row_frac * width_y - offset + jnp.arange(span_y - 2)
            keep_x = (global_x >= 0) & (global_x < width_x * mat_count)
            keep_y = (global_y >= 0) & (global_y < width_y * frac_count)
            current = relax(
                current, coef_part, source_part, (keep_x[:, None] & keep_y[None, :])[:, :, None]
            )
        pressure = current
    return (pressure, fracture, flux)


def solution(mesh):
    in_specs = (
        P("mat", "frac", None),
        P(None, "mat", "frac", None),
        P("mat", "frac", None),
        P("mat", "frac", None),
        P(("mat", "frac"), None),
        P(("mat", "frac")),
        P(("mat", "frac")),
        P(("mat", "frac")),
        P("frac", None, None, None),
        P("frac", None),
        P("frac"),
        P("frac"),
        P("frac"),
    )
    out_specs = (P("mat", "frac", None), P("frac"), P(("mat", "frac")))
    return jax.shard_map(body, mesh=mesh, in_specs=in_specs, out_specs=out_specs, check_vma=False)
```

```python
import functools

import jax
import jax.numpy as jnp
from jax import lax
from jax.experimental import pallas as pl
from jax.experimental.pallas import tpu as pltpu
from jax.sharding import PartitionSpec as P

WEIGHT = 0.8
CAP = 8
LANES = 128
F32 = jnp.float32
BF16 = jnp.bfloat16
VMEM = pl.BlockSpec(memory_space=pltpu.VMEM)
SMEM = pl.BlockSpec(memory_space=pltpu.SMEM)
X, Y, Z, HI, LO, KAPPA, COLS = (CAP * i for i in range(7))


def shape(*dims, dtype=F32):
    return jax.ShapeDtypeStruct(dims, dtype)


def call(body, outs, in_specs, flops=1e6, nbytes=1e6, scratch=(), name=None, **more):
    return pl.pallas_call(
        body,
        out_shape=outs,
        in_specs=in_specs,
        scratch_shapes=scratch,
        compiler_params=pltpu.CompilerParams(vmem_limit_bytes=32 << 20),
        cost_estimate=pl.CostEstimate(
            flops=int(flops), bytes_accessed=int(nbytes), transcendentals=0
        ),
        name=name,
        **more,
    )


def iota(dims, dim):
    return lax.broadcasted_iota(jnp.int32, dims, dim)


def ones_where(mask):
    return jnp.where(mask, 1.0, 0.0).astype(BF16)


def split(v):
    top = v.astype(BF16)
    rest = v - top.astype(F32)
    middle = rest.astype(BF16)
    low = (rest - middle.astype(F32)).astype(BF16)
    return jnp.concatenate([top, middle, low], axis=1)


def pick(chosen, v):
    width = v.shape[1]
    out = jnp.dot(chosen, split(v), preferred_element_type=F32)
    return out[:, :width] + out[:, width : 2 * width] + out[:, 2 * width :]


def total(v):
    return jnp.sum(jnp.sum(v, axis=1, keepdims=True), axis=0, keepdims=True)


def row_sums(v):
    return jnp.sum(v.T, axis=0, keepdims=True)


def as_column(row):
    return jnp.broadcast_to(row, (LANES, LANES)).T


def pack_body(at, cols, owner_col, owner, cell, frac, kappa, x_own, send, slot_out, blocks):
    count = owner.shape[1]
    mine = at[0]
    own = owner[...]
    earlier = (owner_col[...] == own) & (iota((count, count), 0) < iota((count, count), 1))
    slot = jnp.sum(jnp.where(earlier, 1, 0), axis=0, keepdims=True)
    slot_out[...] = slot
    here = iota((CAP, count), 0) == slot
    c, f = cell[...], frac[...]
    k = kappa[...]
    top = k.astype(BF16).astype(F32)
    middle = (k - top).astype(BF16).astype(F32)
    low = k - top - middle
    whole = [c >> 14, (c >> 8) & 63, c & 255, f >> 7, f & 127]
    rows = [jnp.where(here, v.astype(F32), 0.0) for v in whole]
    rows = jnp.concatenate([*rows, jnp.where(here, top, 0.0), jnp.zeros((LANES - 6 * CAP, count), F32)], axis=0)
    chosen = ones_where(iota((LANES, count), 0) == own)
    nt = functools.partial(
        lax.dot_general,
        dimension_numbers=(((1,), (1,)), ((), ())),
        preferred_element_type=F32,
    )

    def kappas(v):
        return jnp.concatenate(
            [
                jnp.zeros((KAPPA, count), F32),
                jnp.where(here, v, 0.0),
                jnp.zeros((LANES - 6 * CAP, count), F32),
            ],
            axis=0,
        ).astype(BF16)

    message = nt(chosen, rows.astype(BF16)) + nt(chosen, kappas(middle)) + nt(chosen, kappas(low))
    lane = iota((1, LANES), 1)
    extra = jnp.zeros((1, LANES), F32)
    for t in range(cols.shape[1]):
        extra = jnp.where(lane == COLS + t, cols[mine, t].astype(F32), extra)
    blocks[...] = jnp.broadcast_to(x_own[pl.ds(mine, 1), :], (LANES, LANES))
    send[pl.ds(0, LANES, stride=2), :] = blocks[...]
    send[pl.ds(1, LANES, stride=2), :] = message + extra


def by_slot(message, k):
    x = message[:, X + k : X + k + 1].astype(jnp.int32)
    y = message[:, Y + k : Y + k + 1].astype(jnp.int32)
    z = message[:, Z + k : Z + k + 1].astype(jnp.int32)
    hi = message[:, HI + k : HI + k + 1].astype(jnp.int32)
    lo = message[:, LO + k : LO + k + 1].astype(jnp.int32)
    return x * 64 + y, z, hi, lo, message[:, KAPPA + k : KAPPA + k + 1]


def traces(message, pressure, gathered):
    rows, depth = pressure.shape
    chosen = jnp.concatenate(
        [ones_where(iota((LANES, rows), 1) == by_slot(message, k)[0]) for k in range(CAP)], axis=0
    )
    gathered[...] = pick(chosen, pressure)
    lane = iota((LANES, LANES), 1)
    out = jnp.zeros((LANES, LANES), F32)
    for k in range(CAP):
        z = by_slot(message, k)[1]
        part = gathered[k * LANES : (k + 1) * LANES, :]
        value = jnp.sum(jnp.where(iota((LANES, depth), 1) == z, part, 0.0), axis=1, keepdims=True)
        out = jnp.where(lane == k, value, out)
    return out


def at_mortar(message, x):
    chosen = jnp.concatenate(
        [ones_where(iota((LANES, LANES), 1) == by_slot(message, k)[2]) for k in range(CAP)], axis=0
    )
    found = pick(chosen, x)
    lane = iota((LANES, LANES), 1)
    out = jnp.zeros((LANES, LANES), F32)
    for k in range(CAP):
        part = found[k * LANES : (k + 1) * LANES, :]
        value = jnp.sum(jnp.where(lane == by_slot(message, k)[3], part, 0.0), axis=1, keepdims=True)
        out = jnp.where(lane == k, value, out)
    return out


def onto_fracture(message, *values):
    flipped = message.T
    hi = jnp.concatenate([flipped[HI + k : HI + k + 1, :] for k in range(CAP)], axis=1)
    chosen = ones_where(iota((LANES, CAP * LANES), 0) == hi.astype(jnp.int32))
    lane = iota((LANES, LANES), 1)
    wide = []
    for v in values:
        spread = [
            jnp.where(lane == by_slot(message, k)[3], v[:, k : k + 1], 0.0) for k in range(CAP)
        ]
        wide.append(jnp.concatenate(spread, axis=0))
    return [pick(chosen, v) for v in wide]


def kappa_of(message):
    lane = iota((LANES, LANES), 1)
    out = jnp.zeros((LANES, LANES), F32)
    for k in range(CAP):
        out = jnp.where(lane == k, message[:, KAPPA + k : KAPPA + k + 1], out)
    return out


def first_body(
    at, cols, got, pressure, tiles, diag, source, send, x_out, trace_out, flux_out, gathered, part
):
    mine, shard = at[0], at[1]
    groups = LANES // CAP
    for m in range(CAP):
        x_out[pl.ds(m, groups, stride=CAP), :] = got[
            pl.ds(2 * m * groups, groups, stride=2), :
        ]
    message = got[pl.ds(1, LANES, stride=2), :]
    trace = traces(message, pressure[...], gathered)
    kappa = kappa_of(message)
    flux = kappa * (trace - at_mortar(message, x_out[...]))
    load, weight = onto_fracture(message, flux, kappa)
    part[...] = load
    row = CAP * shard + mine
    x_row = x_out[pl.ds(row, 1), :]
    x_col = as_column(x_row)
    mixed = jnp.zeros((LANES, LANES), F32)
    for t in range(cols.shape[1]):
        tile = tiles[0, t]
        mixed += tile * x_out[pl.ds(cols[mine, t], 1), :]
        back = jnp.sum(tile * x_col, axis=0, keepdims=True)
        part[pl.ds(cols[mine, t], 1), :] -= 0.5 * back
    part[pl.ds(row, 1), :] += source[pl.ds(mine, 1), :] - (
        diag[pl.ds(mine, 1), :] * x_row + 0.5 * row_sums(mixed)
    )
    send[pl.ds(0, LANES, stride=2), :] = part[...]
    send[pl.ds(1, LANES, stride=2), :] = weight
    trace_out[...] = trace
    flux_out[...] = flux


def source_body(got, flux, base, rhs):
    message = got[pl.ds(1, LANES, stride=2), :]
    rows, depth = base.shape
    flipped = message.T
    cell_row = jnp.concatenate(
        [flipped[X + k : X + k + 1, :] * 64 + flipped[Y + k : Y + k + 1, :] for k in range(CAP)],
        axis=1,
    )
    chosen = ones_where(iota((rows, CAP * LANES), 0) == cell_row.astype(jnp.int32))
    spread = jnp.concatenate(
        [
            jnp.where(iota((LANES, depth), 1) == by_slot(message, k)[1], flux[:, k : k + 1], 0.0)
            for k in range(CAP)
        ],
        axis=0,
    )
    rhs[...] = base[...] + pick(chosen, spread)


def second_body(got, pressure, trace, trace_out, send, gathered):
    message = got[pl.ds(1, LANES, stride=2), :]
    now = traces(message, pressure[...], gathered)
    trace_out[...] = now
    [change] = onto_fracture(message, kappa_of(message) * (now - trace[...]))
    for m in range(send.shape[0] // LANES):
        send[m * LANES : (m + 1) * LANES, :] = change


def flux_body(got, trace, x, flux):
    message = got[pl.ds(1, LANES, stride=2), :]
    flux[...] = kappa_of(message) * (trace[...] - at_mortar(message, x[...]))


def home_body(got, owner, slot, flux):
    count = owner.shape[1]
    values = got[...].T[:CAP, :]
    chosen = ones_where(iota((LANES, count), 0) == owner[...])
    top = values.astype(BF16).astype(F32)
    middle = (values - top).astype(BF16).astype(F32)
    stacked = jnp.concatenate([top, middle, values - top - middle, jnp.zeros_like(top)], axis=0)
    found = jnp.dot(stacked.astype(BF16), chosen, preferred_element_type=F32)
    found = found[:CAP] + found[CAP : 2 * CAP] + found[2 * CAP : 3 * CAP]
    here = iota((CAP, count), 0) == slot[...]
    flux[...] = jnp.sum(jnp.where(here, found, 0.0), axis=0, keepdims=True)


def sum_body(got, send):
    for i in range(2):
        mine = jnp.sum(got[pl.ds(i, LANES, stride=2), :], axis=0, keepdims=True)
        send[pl.ds(i, LANES, stride=2), :] = jnp.broadcast_to(mine, (LANES, LANES))


def columns_body(got, chosen, *, shards, rows, tiles):
    flipped = got[pl.ds(1, LANES, stride=2), :].T[COLS : COLS + CAP, :]
    count = shards * rows * tiles
    tile = iota((LANES, count), 1)
    sender = (tile // tiles) % rows * shards + tile // (rows * tiles)
    moved = jnp.dot(
        jnp.concatenate([flipped, flipped], axis=0).astype(BF16),
        ones_where(iota((LANES, count), 0) == sender),
        preferred_element_type=F32,
    )[:CAP]
    here = iota((CAP, count), 0) == iota((CAP, count), 1) % tiles
    column = jnp.sum(jnp.where(here, moved, 0.0), axis=0, keepdims=True).astype(jnp.int32)
    chosen[...] = ones_where(iota((LANES, count), 0) == column)


def products(at, cols, d, tiles, diag, block):
    shard = at[1]
    rows, per_row = cols.shape
    for r in range(rows):
        d_row = d[pl.ds(CAP * shard + r, 1), :]
        d_col = as_column(d_row)
        mixed = jnp.zeros((LANES, LANES), F32)
        for t in range(per_row):
            tile = tiles[per_row * r + t]
            mixed += tile * d[pl.ds(cols[r, t], 1), :]
            back = jnp.sum(tile * d_col, axis=0, keepdims=True)
            block[rows + per_row * r + t : rows + per_row * r + t + 1, :] = 0.5 * back
        block[r : r + 1, :] = diag[r : r + 1, :] * d_row + 0.5 * row_sums(mixed)


def image_of(got, chosen, step, rows, tiles):
    shards = got.shape[0] // step
    own = jnp.concatenate([got[s * step : s * step + rows, :] for s in range(shards)], axis=0)
    back = jnp.concatenate(
        [got[s * step + rows : s * step + rows + tiles, :] for s in range(shards)], axis=0
    )
    return own + pick(chosen[...], back)


def start_body(at, cols, got, tiles, diag, r_out, weight_out, send, block):
    r_out[...] = got[pl.ds(0, LANES, stride=2), :]
    weight_out[...] = got[pl.ds(1, LANES, stride=2), :]
    products(at, cols, r_out, tiles, diag, block)
    size = block.shape[0]
    for s in range(send.shape[0] // size):
        send[s * size : (s + 1) * size, :] = block[...]


def step_body(at, cols, got, x, r, d, chosen, tiles, diag, *rest, ride, last):
    rows, per_row = cols.shape
    size = rows * (1 + per_row)
    shards = LANES // rows
    extra = list(rest)
    change = extra.pop(0) if ride == "reduce" else None
    x_before, weight = (extra.pop(0), extra.pop(0)) if ride == "next" else (None, None)
    x_out, r_out, d_out, send, block = extra
    got_step = got.shape[0] // shards
    image = image_of(got, chosen, got_step, rows, rows * per_row)
    old = d[...]
    norm = total(r[...] * r[...])
    alpha = norm / total(old * image)
    x_new = x[...] + alpha * old
    r_new = r[...] - alpha * image
    x_out[...] = x_new
    if ride == "next":
        moved = jnp.concatenate(
            [got[s * got_step + size : (s + 1) * got_step, :] for s in range(shards)], axis=0
        )
        r_new = r_new + moved - weight[...] * (x_new - x_before[...])
        d_out[...] = r_new
    else:
        d_out[...] = r_new + (total(r_new * r_new) / norm) * old
    r_out[...] = r_new
    if last:
        shard = at[1]
        lanes = jnp.zeros((1, LANES), F32)
        for i in range(rows):
            d_row = d_out[pl.ds(CAP * shard + i, 1), :]
            mixed = jnp.zeros((LANES, LANES), F32)
            for t in range(per_row):
                mixed += tiles[per_row * i + t] * d_out[pl.ds(cols[i, t], 1), :]
            lanes += diag[i : i + 1, :] * d_row * d_row
            lanes += jnp.sum(mixed * as_column(d_row), axis=0, keepdims=True)
        send[...] = jnp.broadcast_to(lanes, send.shape)
        return
    products(at, cols, d_out, tiles, diag, block)
    send_step = send.shape[0] // shards
    if ride == "gather":
        own = jnp.zeros((rows, LANES), F32)
        for s in range(shards):
            own += got[s * got_step + size : (s + 1) * got_step, :]
    if ride == "reduce":
        sums = jnp.zeros((LANES, LANES), F32)
        for m in range(change.shape[0] // LANES):
            sums += change[m * LANES : (m + 1) * LANES, :]
    for s in range(shards):
        send[s * send_step : s * send_step + size, :] = block[...]
        if ride == "gather":
            send[s * send_step + size : (s + 1) * send_step, :] = own
        if ride == "reduce":
            send[s * send_step + size : (s + 1) * send_step, :] = sums[
                s * rows : (s + 1) * rows, :
            ]


def final_body(at, got, x, r, d, out):
    alpha = total(r[...] * r[...]) / total(got[...])
    here = pl.ds(pl.multiple_of(CAP * at[1], CAP), CAP)
    out[...] = x[here, :] + alpha * d[here, :]


def edges_body(px0, px1, py0, py1, tx1, ty1, x_up, x_down, y_up, y_down):
    wide = px0.shape[1]
    x_up[:wide, :] = px1[0]
    x_up[wide:, :] = tx1[0, 0]
    x_down[...] = px0[0]
    deep = py0.shape[0]
    y_up[:deep, :] = py1[:, 7, :]
    y_up[deep:, :] = ty1[0, :, 7, :]
    y_down[...] = py0[:, 0, :]


def edges(pressure, trans):
    nx, ny, nz = pressure.shape
    y_last = ny // 8 - 1
    return pl.pallas_call(
        edges_body,
        grid=(1,),
        out_shape=(shape(2 * ny, nz), shape(ny, nz), shape(2 * nx, nz), shape(nx, nz)),
        in_specs=[
            pl.BlockSpec((1, ny, nz), lambda i: (0, 0, 0)),
            pl.BlockSpec((1, ny, nz), lambda i: (nx - 1, 0, 0)),
            pl.BlockSpec((nx, 8, nz), lambda i: (0, 0, 0)),
            pl.BlockSpec((nx, 8, nz), lambda i: (0, y_last, 0)),
            pl.BlockSpec((1, 1, ny, nz), lambda i: (0, nx - 1, 0, 0)),
            pl.BlockSpec((1, nx, 8, nz), lambda i: (1, 0, y_last, 0)),
        ],
        out_specs=(VMEM,) * 4,
        compiler_params=pltpu.CompilerParams(vmem_limit_bytes=16 << 20),
        name="edges",
    )(pressure, pressure, pressure, pressure, trans, trans)


def sweep_body(
    p, x_low, x_high, y_low, y_high, tx_low, ty_low, trans, cell, rhs, *rest, first, last
):
    rest = list(rest)
    weight = None if first else rest.pop(0)
    out = rest.pop(0)
    weight_out = rest.pop(0) if first else None
    carry, carry_t = rest.pop(), rest.pop()
    step = pl.program_id(0)
    many = out.shape[0]
    ny, nz = out.shape[1:]
    nx = p.shape[0]
    zero_row = iota((ny, nz), 0)
    lane = iota((ny, nz), 1)

    @pl.when(step == 0)
    def _():
        carry[...] = tx_low[...] * (x_low[...] - p[0])
        carry_t[...] = tx_low[...]

    for i in range(many):
        at = step * many + i
        here = p[at]
        after = jnp.where(at + 1 < nx, p[jnp.minimum(at + 1, nx - 1)], x_high[...])
        tx, ty, tz = trans[0, i], trans[1, i], trans[2, i]
        fx = tx * (here - after)
        y_next = jnp.where(zero_row == ny - 1, y_high[pl.ds(at, 1), :], pltpu.roll(here, ny - 1, 0))
        fy = ty * (here - y_next)
        ty_edge = ty_low[pl.ds(at, 1), :]
        fy_edge = ty_edge * (y_low[pl.ds(at, 1), :] - here[:1])
        fy_low = jnp.where(zero_row == 0, fy_edge, pltpu.roll(fy, 1, 0))
        z_next = jnp.where(lane == nz - 1, 0.0, pltpu.roll(here, nz - 1, 1))
        fz = tz * (here - z_next)
        fz_low = jnp.where(lane == 0, 0.0, pltpu.roll(fz, 1, 1))
        if first:
            ty_before = jnp.where(zero_row == 0, ty_edge, pltpu.roll(ty, 1, 0))
            tz_before = jnp.where(lane == 0, 0.0, pltpu.roll(tz, 1, 1))
            diagonal = cell[i] + tx + carry_t[...] + ty + ty_before + tz + tz_before
            w = WEIGHT / diagonal
            weight_out[i] = w
            carry_t[...] = tx
        else:
            w = weight[i]
        applied = cell[i] * here + fx - carry[...] + fy - fy_low + fz - fz_low
        carry[...] = fx
        out[i] = here + w * (rhs[i] - applied)
    if not last:
        x_up, x_down, y_up, y_down = rest

        @pl.when(step == 0)
        def _():
            x_down[...] = out[0]

        @pl.when(step == pl.num_programs(0) - 1)
        def _():
            x_up[...] = out[many - 1]

        for i in range(many):
            y_down[pl.ds(step * many + i, 1), :] = out[i, :1, :]
            y_up[pl.ds(step * many + i, 1), :] = out[i, ny - 1 :, :]


def sweep(p, halo, lows, trans, cell, rhs, weight=None, last=False, many=4):
    nx, ny, nz = p.shape
    whole = pl.BlockSpec((nx, ny, nz), lambda i: (0, 0, 0))
    part = pl.BlockSpec((many, ny, nz), lambda i: (i, 0, 0))
    x_face = pl.BlockSpec((ny, nz), lambda i: (0, 0))
    y_face = pl.BlockSpec((nx, nz), lambda i: (0, 0))
    first = weight is None
    out_shape, out_specs = [shape(nx, ny, nz)], [part]
    if first:
        out_shape.append(shape(nx, ny, nz))
        out_specs.append(part)
    if not last:
        out_shape += [shape(ny, nz)] * 2 + [shape(nx, nz)] * 2
        out_specs += [x_face, x_face, y_face, y_face]
    operands = [p, *halo, *lows, trans, cell, rhs] + ([] if first else [weight])
    return pl.pallas_call(
        functools.partial(sweep_body, first=first, last=last),
        grid=(nx // many,),
        out_shape=tuple(out_shape),
        in_specs=[whole, x_face, x_face, y_face, y_face, x_face, y_face]
        + [pl.BlockSpec((3, many, ny, nz), lambda i: (0, i, 0, 0)), part, part]
        + ([] if first else [part]),
        out_specs=tuple(out_specs),
        scratch_shapes=[pltpu.VMEM((ny, nz), F32)] * 2,
        compiler_params=pltpu.CompilerParams(vmem_limit_bytes=32 << 20),
        cost_estimate=pl.CostEstimate(flops=6_000_000, bytes_accessed=8 << 20, transcendentals=0),
        name="sweep",
    )(*operands)


def shifted(x_up, x_down, y_up, y_down, mats, shards):
    def move(v, axis, count, by):
        pairs = [(i, i + by) for i in range(count) if 0 <= i + by < count]
        return lax.ppermute(v, axis, pairs)

    return (
        move(x_up, "mat", mats, 1),
        move(x_down, "mat", mats, -1),
        move(y_up, "frac", shards, 1),
        move(y_down, "frac", shards, -1),
    )


def body(
    pressure_start,
    face_trans,
    cell_coef,
    matrix_source,
    mortar_owner,
    mortar_cell,
    mortar_frac,
    mortar_kappa,
    tiles,
    tile_cols,
    frac_diag,
    frac_source,
    fracture_start,
):
    nx, ny, nz = pressure_start.shape
    mats, shards = lax.axis_size("mat"), lax.axis_size("frac")
    rows, per_row = tile_cols.shape
    count = mortar_cell.shape[0]
    size = rows * (1 + per_row)
    at = jnp.stack([lax.axis_index("mat"), lax.axis_index("frac")]).astype(jnp.int32)
    everyone = functools.partial(
        lax.all_to_all, axis_name=("mat", "frac"), split_axis=0, concat_axis=0, tiled=True
    )
    over_frac = functools.partial(
        lax.all_to_all, axis_name="frac", split_axis=0, concat_axis=0, tiled=True
    )
    over_mat = functools.partial(
        lax.all_to_all, axis_name="mat", split_axis=0, concat_axis=0, tiled=True
    )
    square = shape(LANES, LANES)
    owner = mortar_owner.reshape(1, count)
    flat = (nx * ny, nz)
    tile_list = tiles.reshape(rows * per_row, LANES, LANES)
    diag = frac_diag.reshape(rows, LANES)
    square_scratch = pltpu.VMEM((LANES, LANES), F32)
    gathered = pltpu.VMEM((CAP * LANES, nz), F32)
    block = pltpu.VMEM((size, LANES), F32)

    send, slot = call(
        pack_body,
        (shape(2 * LANES, LANES), shape(1, count, dtype=jnp.int32)),
        [SMEM, SMEM] + [VMEM] * 6,
        scratch=[square_scratch],
        name="pack",
    )(
        at,
        tile_cols,
        mortar_owner,
        owner,
        mortar_cell.reshape(1, count),
        mortar_frac.reshape(1, count),
        mortar_kappa.reshape(1, count),
        fracture_start.reshape(rows, LANES),
    )
    got = everyone(send)

    x_low, x_high, y_low, y_high = shifted(
        *edges(pressure_start, face_trans), mats, shards
    )
    lows = (x_low[ny:], y_low[nx:])
    halo = (x_low[:ny], x_high, y_low[:nx], y_high)

    send, x_start, trace, flux = pl.pallas_call(
        first_body,
        out_shape=(shape(2 * LANES, LANES), square, square, square),
        grid_spec=pltpu.PrefetchScalarGridSpec(
            num_scalar_prefetch=2,
            grid=(1,),
            in_specs=[
                VMEM,
                VMEM,
                pl.BlockSpec(
                    (1, per_row, LANES, LANES), lambda i, at, cols: (at[0], 0, 0, 0)
                ),
                VMEM,
                VMEM,
            ],
            out_specs=(VMEM,) * 4,
            scratch_shapes=[gathered, square_scratch],
        ),
        compiler_params=pltpu.CompilerParams(vmem_limit_bytes=32 << 20),
        name="first",
    )(at, tile_cols, got, pressure_start.reshape(flat), tiles, diag, frac_source.reshape(rows, LANES))
    reduced = everyone(send)
    send = call(sum_body, shape(2 * LANES, LANES), [VMEM], name="sums")(reduced)
    residuals = everyone(send)

    base = matrix_source.reshape(flat)

    def with_source(flux):
        return call(source_body, shape(*flat), [VMEM] * 3, flops=2e9, nbytes=2 << 20, name="source")(
            got, flux, base
        ).reshape(nx, ny, nz)

    chosen = call(
        functools.partial(columns_body, shards=shards, rows=rows, tiles=per_row),
        shape(LANES, shards * rows * per_row, dtype=BF16),
        [VMEM],
        name="columns",
    )(got)
    rhs = with_source(flux)
    pressure, weight, *sides = sweep(
        pressure_start, halo, lows, face_trans, cell_coef, rhs
    )
    pressure, *sides = sweep(
        pressure, shifted(*sides, mats, shards), lows, face_trans, cell_coef, rhs, weight
    )
    halo = shifted(*sides, mats, shards)
    trace, send = call(
        second_body,
        (square, shape(mats * LANES, LANES)),
        [VMEM] * 3,
        flops=2e9,
        nbytes=2 << 20,
        scratch=[gathered],
        name="second",
    )(got, pressure.reshape(flat), trace)
    change = over_mat(send)

    r, sums, send = call(
        start_body,
        (square, square, shape(shards * size, LANES)),
        [SMEM, SMEM] + [VMEM] * 3,
        scratch=[block],
        name="start",
    )(at, tile_cols, residuals, tile_list, diag)
    x, d = x_start, r

    def step(arrived, x, r, d, *more, ride=None, last=False):
        length = LANES if last else shards * (size + (rows if ride in ("reduce", "gather") else 0))
        if last:
            length = shards
        return call(
            functools.partial(step_body, ride=ride, last=last),
            (square, square, square, shape(length, LANES)),
            [SMEM, SMEM] + [VMEM] * (7 + len(more)),
            scratch=[block],
            name="step",
        )(at, tile_cols, arrived, x, r, d, chosen, tile_list, diag, *more)

    x, r, d, send = step(over_frac(send), x, r, d, change, ride="reduce")
    x, r, d, send = step(over_frac(send), x, r, d, ride="gather")
    x, r, d, send = step(over_frac(send), x, r, d, x_start, sums, ride="next")

    flux = call(flux_body, square, [VMEM] * 3, name="flux")(got, trace, x)
    rhs = with_source(flux)
    pressure, *sides = sweep(pressure, halo, lows, face_trans, cell_coef, rhs, weight)
    [pressure] = sweep(
        pressure, shifted(*sides, mats, shards), lows, face_trans, cell_coef, rhs, weight, last=True
    )
    flux_out = call(home_body, shape(1, count), [VMEM] * 3, name="home")(
        everyone(flux), owner, slot
    )

    x, r, d, send = step(over_frac(send), x, r, d)
    x, r, d, send = step(over_frac(send), x, r, d, last=True)
    fracture = call(final_body, shape(rows, LANES), [SMEM] + [VMEM] * 4, name="final")(
        at, over_frac(send), x, r, d
    )
    return pressure, fracture.reshape(rows * LANES), flux_out.reshape(count)


def solution(mesh):
    in_specs = (
        P("mat", "frac", None),
        P(None, "mat", "frac", None),
        P("mat", "frac", None),
        P("mat", "frac", None),
        P(("mat", "frac"), None),
        P(("mat", "frac")),
        P(("mat", "frac")),
        P(("mat", "frac")),
        P("frac", None, None, None),
        P("frac", None),
        P("frac"),
        P("frac"),
        P("frac"),
    )
    out_specs = (P("mat", "frac", None), P("frac"), P(("mat", "frac")))
    return jax.shard_map(body, mesh=mesh, in_specs=in_specs, out_specs=out_specs, check_vma=False)
```

```python
import functools

import jax
import jax.numpy as jnp
from jax import lax
from jax.experimental import pallas as pl
from jax.experimental.pallas import tpu as pltpu
from jax.sharding import PartitionSpec as P

WEIGHT = 0.8
CAP = 8
LANES = 128
F32 = jnp.float32
BF16 = jnp.bfloat16
SMEM = pl.BlockSpec(memory_space=pltpu.SMEM)
RAW = pl.BlockSpec(memory_space=pltpu.HBM)
X, Y, Z, HI, LO, KAPPA, COLS = (CAP * i for i in range(7))


def shape(*dims, dtype=F32):
    return pltpu.HBM(dims, dtype)


def in_hbm(x):
    return pltpu.with_memory_space_constraint(x, pltpu.HBM)


def whole(dims):
    return pl.BlockSpec(dims, lambda i: (0,) * len(dims), pipeline_mode=pl.Buffered(1))


def params():
    return pltpu.CompilerParams(vmem_limit_bytes=32 << 20)


def call(body, outs, *operands, scalars=(), raw=(), scratch=(), flops=1e6, nbytes=1e6, name=None):
    single = not isinstance(outs, tuple)
    outs = (outs,) if single else outs
    result = pl.pallas_call(
        body,
        grid=(1,),
        out_shape=outs,
        in_specs=[SMEM] * len(scalars) + [RAW] * len(raw) + [whole(v.shape) for v in operands],
        out_specs=tuple(
            pl.BlockSpec(v.shape, lambda i, n=len(v.shape): (0,) * n) for v in outs
        ),
        scratch_shapes=scratch,
        compiler_params=params(),
        cost_estimate=pl.CostEstimate(
            flops=int(flops), bytes_accessed=int(nbytes), transcendentals=0
        ),
        name=name,
    )(*scalars, *(in_hbm(v) for v in (*raw, *operands)))
    return result[0] if single else result


def iota(dims, dim):
    return lax.broadcasted_iota(jnp.int32, dims, dim)


def ones_where(mask):
    return jnp.where(mask, 1.0, 0.0).astype(BF16)


def split(v):
    top = v.astype(BF16)
    rest = v - top.astype(F32)
    middle = rest.astype(BF16)
    low = (rest - middle.astype(F32)).astype(BF16)
    return jnp.concatenate([top, middle, low], axis=1)


def pick(chosen, v):
    width = v.shape[1]
    out = jnp.dot(chosen, split(v), preferred_element_type=F32)
    return out[:, :width] + out[:, width : 2 * width] + out[:, 2 * width :]


def total(v):
    return jnp.sum(jnp.sum(v, axis=1, keepdims=True), axis=0, keepdims=True)


def row_sums(v):
    return jnp.sum(v.T, axis=0, keepdims=True)


def as_column(row):
    return jnp.broadcast_to(row, (LANES, LANES)).T


def pack_body(at, cols, owner_col, owner, cell, frac, kappa, x_own, send, slot_out, blocks):
    count = owner.shape[1]
    mine = at[0]
    own = owner[...]
    earlier = (owner_col[...] == own) & (iota((count, count), 0) < iota((count, count), 1))
    slot = jnp.sum(jnp.where(earlier, 1, 0), axis=0, keepdims=True)
    slot_out[...] = slot
    here = iota((CAP, count), 0) == slot
    c, f = cell[...], frac[...]
    k = kappa[...]
    top = k.astype(BF16).astype(F32)
    middle = (k - top).astype(BF16).astype(F32)
    low = k - top - middle
    whole = [c >> 14, (c >> 8) & 63, c & 255, f >> 7, f & 127]
    rows = [jnp.where(here, v.astype(F32), 0.0) for v in whole]
    rows = jnp.concatenate([*rows, jnp.where(here, top, 0.0), jnp.zeros((LANES - 6 * CAP, count), F32)], axis=0)
    chosen = ones_where(iota((LANES, count), 0) == own)
    nt = functools.partial(
        lax.dot_general,
        dimension_numbers=(((1,), (1,)), ((), ())),
        preferred_element_type=F32,
    )

    def kappas(v):
        return jnp.concatenate(
            [
                jnp.zeros((KAPPA, count), F32),
                jnp.where(here, v, 0.0),
                jnp.zeros((LANES - 6 * CAP, count), F32),
            ],
            axis=0,
        ).astype(BF16)

    message = nt(chosen, rows.astype(BF16)) + nt(chosen, kappas(middle)) + nt(chosen, kappas(low))
    lane = iota((1, LANES), 1)
    extra = jnp.zeros((1, LANES), F32)
    for t in range(cols.shape[1]):
        extra = jnp.where(lane == COLS + t, cols[mine, t].astype(F32), extra)
    blocks[...] = jnp.broadcast_to(x_own[pl.ds(mine, 1), :], (LANES, LANES))
    send[pl.ds(0, LANES, stride=2), :] = blocks[...]
    send[pl.ds(1, LANES, stride=2), :] = message + extra


def by_slot(message, k):
    x = message[:, X + k : X + k + 1].astype(jnp.int32)
    y = message[:, Y + k : Y + k + 1].astype(jnp.int32)
    z = message[:, Z + k : Z + k + 1].astype(jnp.int32)
    hi = message[:, HI + k : HI + k + 1].astype(jnp.int32)
    lo = message[:, LO + k : LO + k + 1].astype(jnp.int32)
    return x * 64 + y, z, hi, lo, message[:, KAPPA + k : KAPPA + k + 1]


def traces(message, pressure, gathered):
    rows, depth = pressure.shape
    chosen = jnp.concatenate(
        [ones_where(iota((LANES, rows), 1) == by_slot(message, k)[0]) for k in range(CAP)], axis=0
    )
    gathered[...] = pick(chosen, pressure)
    lane = iota((LANES, LANES), 1)
    out = jnp.zeros((LANES, LANES), F32)
    for k in range(CAP):
        z = by_slot(message, k)[1]
        part = gathered[k * LANES : (k + 1) * LANES, :]
        value = jnp.sum(jnp.where(iota((LANES, depth), 1) == z, part, 0.0), axis=1, keepdims=True)
        out = jnp.where(lane == k, value, out)
    return out


def at_mortar(message, x):
    chosen = jnp.concatenate(
        [ones_where(iota((LANES, LANES), 1) == by_slot(message, k)[2]) for k in range(CAP)], axis=0
    )
    found = pick(chosen, x)
    lane = iota((LANES, LANES), 1)
    out = jnp.zeros((LANES, LANES), F32)
    for k in range(CAP):
        part = found[k * LANES : (k + 1) * LANES, :]
        value = jnp.sum(jnp.where(lane == by_slot(message, k)[3], part, 0.0), axis=1, keepdims=True)
        out = jnp.where(lane == k, value, out)
    return out


def onto_fracture(message, *values):
    flipped = message.T
    hi = jnp.concatenate([flipped[HI + k : HI + k + 1, :] for k in range(CAP)], axis=1)
    chosen = ones_where(iota((LANES, CAP * LANES), 0) == hi.astype(jnp.int32))
    lane = iota((LANES, LANES), 1)
    wide = []
    for v in values:
        spread = [
            jnp.where(lane == by_slot(message, k)[3], v[:, k : k + 1], 0.0) for k in range(CAP)
        ]
        wide.append(jnp.concatenate(spread, axis=0))
    return [pick(chosen, v) for v in wide]


def kappa_of(message):
    lane = iota((LANES, LANES), 1)
    out = jnp.zeros((LANES, LANES), F32)
    for k in range(CAP):
        out = jnp.where(lane == k, message[:, KAPPA + k : KAPPA + k + 1], out)
    return out


def first_body(
    at,
    cols,
    tiles_all,
    got,
    pressure,
    diag,
    source,
    send,
    x_out,
    trace_out,
    flux_out,
    gathered,
    part,
    tiles,
    arrived,
):
    mine, shard = at[0], at[1]
    per_row = cols.shape[1]
    fetch = pltpu.make_async_copy(tiles_all.at[pl.ds(per_row * mine, per_row)], tiles, arrived)
    fetch.start()
    groups = LANES // CAP
    for m in range(CAP):
        x_out[pl.ds(m, groups, stride=CAP), :] = got[
            pl.ds(2 * m * groups, groups, stride=2), :
        ]
    message = got[pl.ds(1, LANES, stride=2), :]
    trace = traces(message, pressure[...], gathered)
    kappa = kappa_of(message)
    flux = kappa * (trace - at_mortar(message, x_out[...]))
    load, weight = onto_fracture(message, flux, kappa)
    part[...] = load
    row = CAP * shard + mine
    x_row = x_out[pl.ds(row, 1), :]
    x_col = as_column(x_row)
    mixed = jnp.zeros((LANES, LANES), F32)
    fetch.wait()
    for t in range(per_row):
        tile = tiles[t]
        mixed += tile * x_out[pl.ds(cols[mine, t], 1), :]
        back = jnp.sum(tile * x_col, axis=0, keepdims=True)
        part[pl.ds(cols[mine, t], 1), :] -= 0.5 * back
    part[pl.ds(row, 1), :] += source[pl.ds(mine, 1), :] - (
        diag[pl.ds(mine, 1), :] * x_row + 0.5 * row_sums(mixed)
    )
    send[pl.ds(0, LANES, stride=2), :] = part[...]
    send[pl.ds(1, LANES, stride=2), :] = weight
    trace_out[...] = trace
    flux_out[...] = flux


def source_body(got, flux, base, rhs):
    message = got[pl.ds(1, LANES, stride=2), :]
    rows, depth = base.shape
    flipped = message.T
    cell_row = jnp.concatenate(
        [flipped[X + k : X + k + 1, :] * 64 + flipped[Y + k : Y + k + 1, :] for k in range(CAP)],
        axis=1,
    )
    chosen = ones_where(iota((rows, CAP * LANES), 0) == cell_row.astype(jnp.int32))
    spread = jnp.concatenate(
        [
            jnp.where(iota((LANES, depth), 1) == by_slot(message, k)[1], flux[:, k : k + 1], 0.0)
            for k in range(CAP)
        ],
        axis=0,
    )
    rhs[...] = base[...] + pick(chosen, spread)


def second_source_body(got, trace, x, base, rhs):
    message = got[pl.ds(1, LANES, stride=2), :]
    flux = kappa_of(message) * (trace[...] - at_mortar(message, x[...]))
    source_body(got, flux, base, rhs)


def second_body(got, pressure, trace, trace_out, send, gathered):
    message = got[pl.ds(1, LANES, stride=2), :]
    now = traces(message, pressure[...], gathered)
    trace_out[...] = now
    [change] = onto_fracture(message, kappa_of(message) * (now - trace[...]))
    for m in range(send.shape[0] // LANES):
        send[m * LANES : (m + 1) * LANES, :] = change


def home_body(got, owner, slot, frac, kappa, x, flux):
    count = owner.shape[1]

    def found(values, chosen):
        top = values.astype(BF16).astype(F32)
        middle = (values - top).astype(BF16).astype(F32)
        parts = jnp.concatenate([top, middle, values - top - middle], axis=0)
        if parts.shape[0] % 16:
            parts = jnp.concatenate([parts, jnp.zeros_like(top)], axis=0)
        out = jnp.dot(parts.astype(BF16), chosen, preferred_element_type=F32)
        n = values.shape[0]
        return out[:n] + out[n : 2 * n] + out[2 * n : 3 * n]

    traces_all = found(got[...].T[:CAP, :], ones_where(iota((LANES, count), 0) == owner[...]))
    here = iota((CAP, count), 0) == slot[...]
    trace = jnp.sum(jnp.where(here, traces_all, 0.0), axis=0, keepdims=True)
    f = frac[...]
    x_all = found(x[...].T, ones_where(iota((LANES, count), 0) == f >> 7))
    here = iota((LANES, count), 0) == (f & 127)
    x_there = jnp.sum(jnp.where(here, x_all, 0.0), axis=0, keepdims=True)
    flux[...] = kappa[...] * (trace - x_there)


def sum_body(got, send):
    for i in range(2):
        mine = jnp.sum(got[pl.ds(i, LANES, stride=2), :], axis=0, keepdims=True)
        send[pl.ds(i, LANES, stride=2), :] = jnp.broadcast_to(mine, (LANES, LANES))


def columns_body(got, chosen, *, shards, rows, tiles):
    flipped = got[pl.ds(1, LANES, stride=2), :].T[COLS : COLS + CAP, :]
    count = shards * rows * tiles
    tile = iota((LANES, count), 1)
    sender = (tile // tiles) % rows * shards + tile // (rows * tiles)
    moved = jnp.dot(
        jnp.concatenate([flipped, flipped], axis=0).astype(BF16),
        ones_where(iota((LANES, count), 0) == sender),
        preferred_element_type=F32,
    )[:CAP]
    here = iota((CAP, count), 0) == iota((CAP, count), 1) % tiles
    column = jnp.sum(jnp.where(here, moved, 0.0), axis=0, keepdims=True).astype(jnp.int32)
    chosen[...] = ones_where(iota((LANES, count), 0) == column)


def products(at, cols, d, tiles, diag, block):
    shard = at[1]
    rows, per_row = cols.shape
    for r in range(rows):
        d_row = d[pl.ds(CAP * shard + r, 1), :]
        d_col = as_column(d_row)
        mixed = jnp.zeros((LANES, LANES), F32)
        for t in range(per_row):
            tile = tiles[per_row * r + t]
            mixed += tile * d[pl.ds(cols[r, t], 1), :]
            back = jnp.sum(tile * d_col, axis=0, keepdims=True)
            block[rows + per_row * r + t : rows + per_row * r + t + 1, :] = 0.5 * back
        block[r : r + 1, :] = diag[r : r + 1, :] * d_row + 0.5 * row_sums(mixed)


def image_of(got, chosen, step, rows, tiles):
    shards = got.shape[0] // step
    own = jnp.concatenate([got[s * step : s * step + rows, :] for s in range(shards)], axis=0)
    back = jnp.concatenate(
        [got[s * step + rows : s * step + rows + tiles, :] for s in range(shards)], axis=0
    )
    return own + pick(chosen[...], back)


def start_body(at, cols, tiles_all, got, diag, r_out, weight_out, send, block, tiles, arrived):
    fetch = pltpu.make_async_copy(tiles_all, tiles, arrived)
    fetch.start()
    r_out[...] = got[pl.ds(0, LANES, stride=2), :]
    weight_out[...] = got[pl.ds(1, LANES, stride=2), :]
    fetch.wait()
    products(at, cols, r_out, tiles, diag, block)
    size = block.shape[0]
    for s in range(send.shape[0] // size):
        send[s * size : (s + 1) * size, :] = block[...]


def step_body(at, cols, tiles_all, got, x, r, d, chosen, diag, *rest, ride, last):
    rows, per_row = cols.shape
    size = rows * (1 + per_row)
    shards = LANES // rows
    extra = list(rest)
    change = extra.pop(0) if ride == "reduce" else None
    x_before, weight = (extra.pop(0), extra.pop(0)) if ride == "next" else (None, None)
    x_out, r_out, d_out, send, block, tiles, arrived = extra
    fetch = pltpu.make_async_copy(tiles_all, tiles, arrived)
    fetch.start()
    got_step = got.shape[0] // shards
    image = image_of(got, chosen, got_step, rows, rows * per_row)
    old = d[...]
    norm = total(r[...] * r[...])
    alpha = norm / total(old * image)
    x_new = x[...] + alpha * old
    r_new = r[...] - alpha * image
    x_out[...] = x_new
    if ride == "next":
        moved = jnp.concatenate(
            [got[s * got_step + size : (s + 1) * got_step, :] for s in range(shards)], axis=0
        )
        r_new = r_new + moved - weight[...] * (x_new - x_before[...])
        d_out[...] = r_new
    else:
        d_out[...] = r_new + (total(r_new * r_new) / norm) * old
    r_out[...] = r_new
    fetch.wait()
    if last:
        shard = at[1]
        lanes = jnp.zeros((1, LANES), F32)
        for i in range(rows):
            d_row = d_out[pl.ds(CAP * shard + i, 1), :]
            mixed = jnp.zeros((LANES, LANES), F32)
            for t in range(per_row):
                mixed += tiles[per_row * i + t] * d_out[pl.ds(cols[i, t], 1), :]
            lanes += diag[i : i + 1, :] * d_row * d_row
            lanes += jnp.sum(mixed * as_column(d_row), axis=0, keepdims=True)
        send[...] = jnp.broadcast_to(lanes, send.shape)
        return
    products(at, cols, d_out, tiles, diag, block)
    send_step = send.shape[0] // shards
    if ride == "gather":
        own = jnp.zeros((rows, LANES), F32)
        for s in range(shards):
            own += got[s * got_step + size : (s + 1) * got_step, :]
    if ride == "reduce":
        sums = jnp.zeros((LANES, LANES), F32)
        for m in range(change.shape[0] // LANES):
            sums += change[m * LANES : (m + 1) * LANES, :]
    for s in range(shards):
        send[s * send_step : s * send_step + size, :] = block[...]
        if ride == "gather":
            send[s * send_step + size : (s + 1) * send_step, :] = own
        if ride == "reduce":
            send[s * send_step + size : (s + 1) * send_step, :] = sums[
                s * rows : (s + 1) * rows, :
            ]


def final_body(at, got, x, r, d, out):
    alpha = total(r[...] * r[...]) / total(got[...])
    here = pl.ds(pl.multiple_of(CAP * at[1], CAP), CAP)
    out[...] = x[here, :] + alpha * d[here, :]


def even(at, dim):
    return (at[dim] & 1) == 0


def edges_body(at, px0, px1, py0, py1, tx1, ty1, xa, xb, ya, yb):
    wide, deep = px0.shape[1], py0.shape[0]
    low, high = px0[0], px1[0]
    xa[:wide, :] = jnp.where(even(at, 0), high, low)
    xb[:wide, :] = jnp.where(even(at, 0), low, high)
    xa[wide:, :] = tx1[0, 0]
    xb[wide:, :] = tx1[0, 0]
    low, high = py0[:, 0, :], py1[:, 7, :]
    ya[:deep, :] = jnp.where(even(at, 1), high, low)
    yb[:deep, :] = jnp.where(even(at, 1), low, high)
    ya[deep:, :] = ty1[0, :, 7, :]
    yb[deep:, :] = ty1[0, :, 7, :]


def edges(at, pressure, trans):
    nx, ny, nz = pressure.shape
    y_last = ny // 8 - 1
    out = [(2 * ny, nz)] * 2 + [(2 * nx, nz)] * 2
    pressure, trans = in_hbm(pressure), in_hbm(trans)
    return pl.pallas_call(
        edges_body,
        grid=(1,),
        out_shape=tuple(shape(*v) for v in out),
        in_specs=[
            SMEM,
            pl.BlockSpec((1, ny, nz), lambda i: (0, 0, 0)),
            pl.BlockSpec((1, ny, nz), lambda i: (nx - 1, 0, 0)),
            pl.BlockSpec((nx, 8, nz), lambda i: (0, 0, 0)),
            pl.BlockSpec((nx, 8, nz), lambda i: (0, y_last, 0)),
            pl.BlockSpec((1, 1, ny, nz), lambda i: (0, nx - 1, 0, 0)),
            pl.BlockSpec((1, nx, 8, nz), lambda i: (1, 0, y_last, 0)),
        ],
        out_specs=tuple(pl.BlockSpec(v, lambda i: (0, 0)) for v in out),
        compiler_params=params(),
        name="edges",
    )(at, pressure, pressure, pressure, pressure, trans, trans)


def sweep_body(
    at, p, xa, xb, ya, yb, cxa, cxb, cya, cyb, trans, cell, rhs, *rest, first, last
):
    rest = list(rest)
    weight = None if first else rest.pop(0)
    out = rest.pop(0)
    weight_out = rest.pop(0) if first else None
    carry_t = rest.pop() if first else None
    carry = rest.pop()
    step = pl.program_id(0)
    steps = pl.num_programs(0)
    many, ny, nz = out.shape
    nx = p.shape[0]
    row = iota((ny, nz), 0)
    lane = iota((ny, nz), 1)
    x_even, y_even = even(at, 0), even(at, 1)

    @pl.when(step == 0)
    def _():
        tx_low = jnp.where(x_even, cxb[ny:, :], cxa[ny:, :])
        carry[...] = tx_low * (jnp.where(x_even, xb[:ny, :], xa[:ny, :]) - p[0])
        if first:
            carry_t[...] = tx_low

    for i in range(many):
        here_at = step * many + i
        here = p[here_at]
        if i + 1 < many:
            after = p[here_at + 1]
        else:
            x_high = jnp.where(x_even, xa[:ny, :], xb[:ny, :])
            after = jnp.where(step + 1 < steps, p[jnp.minimum(here_at + 1, nx - 1)], x_high)
        one = pl.ds(here_at, 1)
        edge = pl.ds(nx + here_at, 1)
        y_low = jnp.where(y_even, yb[one, :], ya[one, :])
        y_high = jnp.where(y_even, ya[one, :], yb[one, :])
        ty_edge = jnp.where(y_even, cyb[edge, :], cya[edge, :])
        tx, ty, tz = trans[0, i], trans[1, i], trans[2, i]
        fx = tx * (here - after)
        y_next = jnp.where(row == ny - 1, y_high, pltpu.roll(here, ny - 1, 0))
        fy = ty * (here - y_next)
        fy_low = jnp.where(row == 0, ty_edge * (y_low - here[:1]), pltpu.roll(fy, 1, 0))
        z_next = jnp.where(lane == nz - 1, 0.0, pltpu.roll(here, nz - 1, 1))
        fz = tz * (here - z_next)
        fz_low = jnp.where(lane == 0, 0.0, pltpu.roll(fz, 1, 1))
        if first:
            ty_before = jnp.where(row == 0, ty_edge, pltpu.roll(ty, 1, 0))
            tz_before = jnp.where(lane == 0, 0.0, pltpu.roll(tz, 1, 1))
            diagonal = cell[i] + tx + carry_t[...] + ty + ty_before + tz + tz_before
            w = WEIGHT / diagonal
            weight_out[i] = w
            carry_t[...] = tx
        else:
            w = weight[i]
        applied = cell[i] * here + fx - carry[...] + fy - fy_low + fz - fz_low
        carry[...] = fx
        out[i] = here + w * (rhs[i] - applied)
    if last:
        return
    xa_out, xb_out, ya_out, yb_out = rest
    start, end = step == 0, step == steps - 1

    @pl.when(start & x_even)
    def _():
        xb_out[...] = out[0]

    @pl.when(start & ~x_even)
    def _():
        xa_out[...] = out[0]

    @pl.when(end & x_even)
    def _():
        xa_out[...] = out[many - 1]

    @pl.when(end & ~x_even)
    def _():
        xb_out[...] = out[many - 1]

    for i in range(many):
        one = pl.ds(step * many + i, 1)
        low, high = out[i, :1, :], out[i, ny - 1 :, :]
        ya_out[one, :] = jnp.where(y_even, high, low)
        yb_out[one, :] = jnp.where(y_even, low, high)


def sweep(at, p, halo, faces, trans, cell, rhs, weight=None, last=False, many=4):
    nx, ny, nz = p.shape
    part = pl.BlockSpec((many, ny, nz), lambda i: (i, 0, 0))
    x_face = pl.BlockSpec((ny, nz), lambda i: (0, 0))
    y_face = pl.BlockSpec((nx, nz), lambda i: (0, 0))
    first = weight is None
    out_shape, out_specs = [shape(nx, ny, nz)], [part]
    if first:
        out_shape.append(shape(nx, ny, nz))
        out_specs.append(part)
    if not last:
        out_shape += [shape(ny, nz)] * 2 + [shape(nx, nz)] * 2
        out_specs += [x_face, x_face, y_face, y_face]
    operands = [p, *halo, *faces, trans, cell, rhs] + ([] if first else [weight])
    return pl.pallas_call(
        functools.partial(sweep_body, first=first, last=last),
        grid=(nx // many,),
        out_shape=tuple(out_shape),
        in_specs=[SMEM]
        + [whole(v.shape) for v in (p, *halo, *faces)]
        + [pl.BlockSpec((3, many, ny, nz), lambda i: (0, i, 0, 0)), part, part]
        + ([] if first else [part]),
        out_specs=tuple(out_specs),
        scratch_shapes=[pltpu.VMEM((ny, nz), F32)] * (2 if first else 1),
        compiler_params=params(),
        cost_estimate=pl.CostEstimate(flops=6_000_000, bytes_accessed=8 << 20, transcendentals=0),
        name="sweep",
    )(at, *(in_hbm(v) for v in operands))


def swapped(xa, xb, ya, yb, mats, shards):
    def swap(v, axis, count, low):
        pairs = [(i, i + 1) for i in range(low, count - 1, 2)]
        return lax.ppermute(v, axis, pairs + [(b, a) for a, b in pairs])

    return (
        swap(xa, "mat", mats, 0),
        swap(xb, "mat", mats, 1),
        swap(ya, "frac", shards, 0),
        swap(yb, "frac", shards, 1),
    )


def body(
    pressure_start,
    face_trans,
    cell_coef,
    matrix_source,
    mortar_owner,
    mortar_cell,
    mortar_frac,
    mortar_kappa,
    tiles,
    tile_cols,
    frac_diag,
    frac_source,
    fracture_start,
):
    nx, ny, nz = pressure_start.shape
    mats, shards = lax.axis_size("mat"), lax.axis_size("frac")
    rows, per_row = tile_cols.shape
    count = mortar_cell.shape[0]
    size = rows * (1 + per_row)
    at = jnp.stack([lax.axis_index("mat"), lax.axis_index("frac")]).astype(jnp.int32)
    everyone = functools.partial(
        lax.all_to_all, axis_name=("mat", "frac"), split_axis=0, concat_axis=0, tiled=True
    )
    over_frac = functools.partial(
        lax.all_to_all, axis_name="frac", split_axis=0, concat_axis=0, tiled=True
    )
    over_mat = functools.partial(
        lax.all_to_all, axis_name="mat", split_axis=0, concat_axis=0, tiled=True
    )
    square = shape(LANES, LANES)
    owner = mortar_owner.reshape(1, count)
    frac, kappa = mortar_frac.reshape(1, count), mortar_kappa.reshape(1, count)
    flat = (nx * ny, nz)
    tile_list = tiles.reshape(rows * per_row, LANES, LANES)
    diag = frac_diag.reshape(rows, LANES)
    square_scratch = pltpu.VMEM((LANES, LANES), F32)
    gathered = pltpu.VMEM((CAP * LANES, nz), F32)
    block = pltpu.VMEM((size, LANES), F32)
    tile_scratch = [
        pltpu.VMEM((rows * per_row, LANES, LANES), F32),
        pltpu.SemaphoreType.DMA(()),
    ]
    scalars = (at, tile_cols)

    send, slot = call(
        pack_body,
        (shape(2 * LANES, LANES), shape(1, count, dtype=jnp.int32)),
        mortar_owner,
        owner,
        mortar_cell.reshape(1, count),
        frac,
        kappa,
        fracture_start.reshape(rows, LANES),
        scalars=scalars,
        scratch=[square_scratch],
        name="pack",
    )
    got = everyone(send)

    faces = swapped(*edges(at, pressure_start, face_trans), mats, shards)

    send, x_start, trace, flux = call(
        first_body,
        (shape(2 * LANES, LANES), square, square, square),
        got,
        pressure_start.reshape(flat),
        diag,
        frac_source.reshape(rows, LANES),
        scalars=scalars,
        raw=(tile_list,),
        scratch=[
            gathered,
            square_scratch,
            pltpu.VMEM((per_row, LANES, LANES), F32),
            pltpu.SemaphoreType.DMA(()),
        ],
        flops=2e9,
        name="first",
    )
    reduced = everyone(send)
    base = matrix_source.reshape(flat)
    rhs = call(source_body, shape(*flat), got, flux, base, flops=2e9, name="source")
    rhs = rhs.reshape(nx, ny, nz)
    pressure, weight, *sides = sweep(
        at, pressure_start, faces, faces, face_trans, cell_coef, rhs
    )
    sides = swapped(*sides, mats, shards)

    send = call(sum_body, shape(2 * LANES, LANES), reduced, name="sums")
    send, pressure = lax.optimization_barrier((send, pressure))
    residuals = everyone(send)
    chosen = call(
        functools.partial(columns_body, shards=shards, rows=rows, tiles=per_row),
        shape(LANES, shards * rows * per_row, dtype=BF16),
        got,
        name="columns",
    )
    pressure, *sides = sweep(at, pressure, sides, faces, face_trans, cell_coef, rhs, weight)

    r, sums, send = call(
        start_body,
        (square, square, shape(shards * size, LANES)),
        residuals,
        diag,
        scalars=scalars,
        raw=(tile_list,),
        scratch=[block, *tile_scratch],
        name="start",
    )
    x, d = x_start, r
    send, pressure = lax.optimization_barrier((send, pressure))
    arrived = over_frac(send)
    trace, change = call(
        second_body,
        (square, shape(mats * LANES, LANES)),
        got,
        pressure.reshape(flat),
        trace,
        scratch=[gathered],
        flops=2e9,
        name="second",
    )
    change = over_mat(change)

    def step(arrived, x, r, d, *more, ride=None, last=False):
        length = shards * (size + (rows if ride in ("reduce", "gather") else 0))
        return call(
            functools.partial(step_body, ride=ride, last=last),
            (square, square, square, shape(shards if last else length, LANES)),
            arrived,
            x,
            r,
            d,
            chosen,
            diag,
            *more,
            scalars=scalars,
            raw=(tile_list,),
            scratch=[block, *tile_scratch],
            name="step",
        )

    x, r, d, send = step(arrived, x, r, d, change, ride="reduce")
    send, trace, sides = lax.optimization_barrier((send, trace, sides))
    arrived = over_frac(send)
    sides = swapped(*sides, mats, shards)

    x, r, d, send = step(arrived, x, r, d, ride="gather")
    send, home = lax.optimization_barrier((send, trace))
    arrived = over_frac(send)
    home = everyone(home)

    x, r, d, send = step(arrived, x, r, d, x_start, sums, ride="next")
    x_flux = x
    arrived = over_frac(send)
    rhs = call(
        second_source_body, shape(*flat), got, trace, x_flux, base, flops=2e9, name="source"
    ).reshape(nx, ny, nz)
    pressure, *sides = sweep(at, pressure, sides, faces, face_trans, cell_coef, rhs, weight)

    x, r, d, send = step(arrived, x, r, d)
    send, sides, home = lax.optimization_barrier((send, sides, home))
    arrived = over_frac(send)
    sides = swapped(*sides, mats, shards)
    flux = call(
        home_body, shape(1, count), home, owner, slot, frac, kappa, x_flux, name="home"
    )

    x, r, d, send = step(arrived, x, r, d, last=True)
    send, pressure, flux = lax.optimization_barrier((send, pressure, flux))
    arrived = over_frac(send)
    [pressure] = sweep(
        at, pressure, sides, faces, face_trans, cell_coef, rhs, weight, last=True
    )
    fracture = call(
        final_body, shape(rows, LANES), arrived, x, r, d, scalars=(at,), name="final"
    )
    return pressure, fracture.reshape(rows * LANES), flux.reshape(count)


def solution(mesh):
    in_specs = (
        P("mat", "frac", None),
        P(None, "mat", "frac", None),
        P("mat", "frac", None),
        P("mat", "frac", None),
        P(("mat", "frac"), None),
        P(("mat", "frac")),
        P(("mat", "frac")),
        P(("mat", "frac")),
        P("frac", None, None, None),
        P("frac", None),
        P("frac"),
        P("frac"),
        P("frac"),
    )
    out_specs = (P("mat", "frac", None), P("frac"), P(("mat", "frac")))
    return jax.shard_map(body, mesh=mesh, in_specs=in_specs, out_specs=out_specs, check_vma=False)
```

```python
import functools
import math

import jax
import jax.numpy as jnp
from jax import lax
from jax.experimental import pallas as pl
from jax.experimental.pallas import tpu as pltpu
from jax.sharding import PartitionSpec as P

WEIGHT = 0.8
CAP = 8
LANES = 128
LARGE = 1 << 18
F32 = jnp.float32
BF16 = jnp.bfloat16
SMEM = pl.BlockSpec(memory_space=pltpu.SMEM)
VMEM = pl.BlockSpec(memory_space=pltpu.VMEM)
RAW = pl.BlockSpec(memory_space=pltpu.HBM)
X, Y, Z, HI, LO, KAPPA, COLS = (CAP * i for i in range(7))


def shape(*dims, dtype=F32):
    if math.prod(dims) >= LARGE:
        return pltpu.HBM(dims, dtype)
    return jax.ShapeDtypeStruct(dims, dtype)


def sent(*dims):
    return pltpu.HBM(dims, F32)


def in_hbm(x, least=LARGE):
    if x.size < least:
        return x
    return pltpu.with_memory_space_constraint(x, pltpu.HBM)


def on_chip(v):
    return isinstance(v, jax.ShapeDtypeStruct) and math.prod(v.shape) < LARGE


def whole(dims):
    return pl.BlockSpec(dims, lambda i: (0,) * len(dims), pipeline_mode=pl.Buffered(1))


def params():
    return pltpu.CompilerParams(vmem_limit_bytes=32 << 20)


def call(
    body, outs, *operands, scalars=(), raw=(), resident=(), side=(), scratch=(), flops=1e6, nbytes=1e6, name=None, least=LARGE
):
    single = not isinstance(outs, tuple)
    outs = (outs,) if single else outs
    result = pl.pallas_call(
        body,
        grid=(1,),
        out_shape=outs,
        in_specs=[SMEM] * len(scalars) + [RAW] * len(raw) + [VMEM] * len(resident) + [VMEM if v.size < least else whole(v.shape) for v in operands]
        + [whole(v.shape) for v in side],
        out_specs=tuple(
            VMEM if on_chip(v) else pl.BlockSpec(v.shape, lambda i, n=len(v.shape): (0,) * n)
            for v in outs
        ),
        scratch_shapes=scratch,
        compiler_params=params(),
        cost_estimate=pl.CostEstimate(
            flops=int(flops), bytes_accessed=int(nbytes), transcendentals=0
        ),
        name=name,
    )(
        *scalars,
        *(in_hbm(v, least) for v in raw),
        *resident,
        *(in_hbm(v, least) for v in operands),
        *(in_hbm(v, 1) for v in side),
    )
    return result[0] if single else result


def iota(dims, dim):
    return lax.broadcasted_iota(jnp.int32, dims, dim)


def ones_where(mask):
    return jnp.where(mask, 1.0, 0.0).astype(BF16)


def halves(v):
    top = v.astype(BF16)
    return jnp.concatenate([top, (v - top.astype(F32)).astype(BF16)], axis=1)


def pick_rounded(chosen, v):
    width = v.shape[1]
    out = jnp.dot(chosen, halves(v), preferred_element_type=F32)
    return out[:, :width] + out[:, width:]


def split(v):
    top = v.astype(BF16)
    rest = v - top.astype(F32)
    middle = rest.astype(BF16)
    low = (rest - middle.astype(F32)).astype(BF16)
    return jnp.concatenate([top, middle, low], axis=1)


def pick(chosen, v):
    width = v.shape[1]
    out = jnp.dot(chosen, split(v), preferred_element_type=F32)
    return out[:, :width] + out[:, width : 2 * width] + out[:, 2 * width :]


def total(v):
    return jnp.sum(jnp.sum(v, axis=1, keepdims=True), axis=0, keepdims=True)


def row_sums(v):
    return jnp.sum(v.T, axis=0, keepdims=True)


def as_column(row):
    return jnp.broadcast_to(row, (LANES, LANES)).T


def pack_body(at, cols, owner, cell, frac, kappa, x_own, send, slot_out, blocks):
    count = owner.shape[1]
    mine = at[0]
    own = owner[...]
    slot = jnp.zeros((1, count), jnp.int32)
    for first in range(0, count, LANES):
        column = jnp.broadcast_to(own[:, first : first + LANES], (LANES, LANES)).T
        column = jnp.concatenate([column] * (count // LANES), axis=1)
        before = iota((LANES, count), 0) + first < iota((LANES, count), 1)
        slot += jnp.sum(jnp.where((column == own) & before, 1, 0), axis=0, keepdims=True)
    slot_out[...] = slot
    here = iota((CAP, count), 0) == slot
    c, f = cell[...], frac[...]
    k = kappa[...]
    top = k.astype(BF16).astype(F32)
    middle = (k - top).astype(BF16).astype(F32)
    low = k - top - middle
    whole = [c >> 14, (c >> 8) & 63, c & 255, f >> 7, f & 127]
    rows = [jnp.where(here, v.astype(F32), 0.0) for v in whole]
    rows = jnp.concatenate([*rows, jnp.where(here, top, 0.0), jnp.zeros((LANES - 6 * CAP, count), F32)], axis=0)
    chosen = ones_where(iota((LANES, count), 0) == own)
    nt = functools.partial(
        lax.dot_general,
        dimension_numbers=(((1,), (1,)), ((), ())),
        preferred_element_type=F32,
    )

    def kappas(v):
        return jnp.concatenate(
            [
                jnp.zeros((KAPPA, count), F32),
                jnp.where(here, v, 0.0),
                jnp.zeros((LANES - 6 * CAP, count), F32),
            ],
            axis=0,
        ).astype(BF16)

    message = nt(chosen, rows.astype(BF16)) + nt(chosen, kappas(middle)) + nt(chosen, kappas(low))
    lane = iota((1, LANES), 1)
    extra = jnp.zeros((1, LANES), F32)
    for t in range(cols.shape[0]):
        extra = jnp.where(lane == COLS + t, cols[t, mine].astype(F32), extra)
    blocks[...] = jnp.broadcast_to(x_own[pl.ds(mine, 1), :], (LANES, LANES))
    send[pl.ds(0, LANES, stride=2), :] = blocks[...]
    send[pl.ds(1, LANES, stride=2), :] = message + extra


def by_slot(message, k):
    x = message[:, X + k : X + k + 1].astype(jnp.int32)
    y = message[:, Y + k : Y + k + 1].astype(jnp.int32)
    z = message[:, Z + k : Z + k + 1].astype(jnp.int32)
    hi = message[:, HI + k : HI + k + 1].astype(jnp.int32)
    lo = message[:, LO + k : LO + k + 1].astype(jnp.int32)
    return x * 64 + y, z, hi, lo, message[:, KAPPA + k : KAPPA + k + 1]


def in_parts(source, target, arrived):
    parts = arrived.shape[0]
    each = source.shape[0] // parts
    copies = []
    for i in range(parts):
        part = pl.ds(i * each, each)
        copies.append(
            pltpu.make_async_copy(source.at[part], target.at[part], arrived.at[i])
        )
        copies[-1].start()
    return copies


def traces(message, pressure_all, pressure, here, gathered):
    copies = in_parts(pressure_all, pressure, here)
    rows, depth = pressure.shape
    chosen = jnp.concatenate(
        [ones_where(iota((LANES, rows), 1) == by_slot(message, k)[0]) for k in range(CAP)], axis=0
    )
    for copy in copies:
        copy.wait()
    gathered[...] = pick_rounded(chosen, pressure[...])
    lane = iota((LANES, LANES), 1)
    out = jnp.zeros((LANES, LANES), F32)
    for k in range(CAP):
        z = by_slot(message, k)[1]
        part = gathered[k * LANES : (k + 1) * LANES, :]
        value = jnp.sum(jnp.where(iota((LANES, depth), 1) == z, part, 0.0), axis=1, keepdims=True)
        out = jnp.where(lane == k, value, out)
    return out


def at_mortar(message, x):
    chosen = jnp.concatenate(
        [ones_where(iota((LANES, LANES), 1) == by_slot(message, k)[2]) for k in range(CAP)], axis=0
    )
    found = pick(chosen, x)
    lane = iota((LANES, LANES), 1)
    out = jnp.zeros((LANES, LANES), F32)
    for k in range(CAP):
        part = found[k * LANES : (k + 1) * LANES, :]
        value = jnp.sum(jnp.where(lane == by_slot(message, k)[3], part, 0.0), axis=1, keepdims=True)
        out = jnp.where(lane == k, value, out)
    return out


def onto_fracture(message, *values):
    flipped = message.T
    hi = jnp.concatenate([flipped[HI + k : HI + k + 1, :] for k in range(CAP)], axis=1)
    chosen = ones_where(iota((LANES, CAP * LANES), 0) == hi.astype(jnp.int32))
    lane = iota((LANES, LANES), 1)
    wide = []
    for v in values:
        spread = [
            jnp.where(lane == by_slot(message, k)[3], v[:, k : k + 1], 0.0) for k in range(CAP)
        ]
        wide.append(jnp.concatenate(spread, axis=0))
    return [pick(chosen, v) for v in wide]


def kappa_of(message):
    lane = iota((LANES, LANES), 1)
    out = jnp.zeros((LANES, LANES), F32)
    for k in range(CAP):
        out = jnp.where(lane == k, message[:, KAPPA + k : KAPPA + k + 1], out)
    return out


def first_body(
    at,
    cols,
    tiles_all,
    pressure_all,
    got,
    diag,
    source,
    send,
    x_out,
    trace_out,
    flux_out,
    message_out,
    gathered,
    part,
    tiles,
    arrived,
    pressure,
    here,
):
    mine, shard = at[0], at[1]
    per_row = cols.shape[0]
    fetch = pltpu.make_async_copy(tiles_all.at[pl.ds(per_row * mine, per_row)], tiles, arrived)
    fetch.start()
    groups = LANES // CAP
    for m in range(CAP):
        x_out[pl.ds(m, groups, stride=CAP), :] = got[
            pl.ds(2 * m * groups, groups, stride=2), :
        ]
    message = got[pl.ds(1, LANES, stride=2), :]
    message_out[...] = message
    trace = traces(message, pressure_all, pressure, here, gathered)
    kappa = kappa_of(message)
    flux = kappa * (trace - at_mortar(message, x_out[...]))
    load, weight = onto_fracture(message, flux, kappa)
    part[...] = load
    row = CAP * shard + mine
    x_row = x_out[pl.ds(row, 1), :]
    x_col = as_column(x_row)
    mixed = jnp.zeros((LANES, LANES), F32)
    fetch.wait()
    for t in range(per_row):
        tile = tiles[t]
        mixed += tile * x_out[pl.ds(cols[t, mine], 1), :]
        back = jnp.sum(tile * x_col, axis=0, keepdims=True)
        part[pl.ds(cols[t, mine], 1), :] -= 0.5 * back
    part[pl.ds(row, 1), :] += source[pl.ds(mine, 1), :] - (
        diag[pl.ds(mine, 1), :] * x_row + 0.5 * row_sums(mixed)
    )
    send[pl.ds(0, LANES, stride=2), :] = part[...]
    send[pl.ds(1, LANES, stride=2), :] = weight
    trace_out[...] = trace
    flux_out[...] = flux


def spread_flux(message, values, spread, cell_row, depth):
    flipped = message.T
    for k in range(CAP):
        z = by_slot(message, k)[1]
        placed = jnp.where(iota((LANES, depth), 1) == z, values[:, k : k + 1], 0.0)
        spread[k * LANES : (k + 1) * LANES, :] = halves(placed)
        cell_row[:, k * LANES : (k + 1) * LANES] = (
            flipped[X + k : X + k + 1, :] * 64 + flipped[Y + k : Y + k + 1, :]
        ).astype(jnp.int32)


def sources(rows, step, spread, cell_row):
    depth = spread.shape[1] // 2
    row = iota((rows, CAP * LANES), 0) + step * rows
    chosen = ones_where(row == cell_row[...])
    out = jnp.dot(chosen, spread[...], preferred_element_type=F32)
    return out[:, :depth] + out[:, depth:]


def second_body(pressure_all, message, trace, trace_out, send, gathered, pressure, here, change):
    message = message[...]
    now = traces(message, pressure_all, pressure, here, gathered)
    trace_out[...] = now
    change[...] = onto_fracture(message, kappa_of(message) * (now - trace[...]))[0]
    mats = CAP
    each = LANES // mats
    for m in range(mats):
        part = slice(m * each, (m + 1) * each)
        send[2 * m * each : (2 * m + 1) * each, :] = change[part, :]
        send[(2 * m + 1) * each : (2 * m + 2) * each, :] = now[part, :]


def home_body(got, owner, slot, frac, kappa, x, flux, *, mats):
    count = owner.shape[1]

    def found(values, chosen):
        top = values.astype(BF16).astype(F32)
        middle = (values - top).astype(BF16).astype(F32)
        parts = jnp.concatenate([top, middle, values - top - middle], axis=0)
        if parts.shape[0] % 16:
            parts = jnp.concatenate([parts, jnp.zeros_like(top)], axis=0)
        out = jnp.dot(parts.astype(BF16), chosen, preferred_element_type=F32)
        n = values.shape[0]
        return out[:n] + out[n : 2 * n] + out[2 * n : 3 * n]

    shards = LANES // mats
    own = owner[...]
    source = (own & (shards - 1)) * mats + own // shards
    traces_all = found(got[...].T[:CAP, :], ones_where(iota((LANES, count), 0) == source))
    here = iota((CAP, count), 0) == slot[...]
    trace = jnp.sum(jnp.where(here, traces_all, 0.0), axis=0, keepdims=True)
    f = frac[...]
    x_all = found(x[...].T, ones_where(iota((LANES, count), 0) == f >> 7))
    here = iota((LANES, count), 0) == (f & 127)
    x_there = jnp.sum(jnp.where(here, x_all, 0.0), axis=0, keepdims=True)
    flux[...] = kappa[...] * (trace - x_there)


def sum_body(got, send):
    for i in range(2):
        mine = jnp.sum(got[pl.ds(i, LANES, stride=2), :], axis=0, keepdims=True)
        send[pl.ds(i, LANES, stride=2), :] = jnp.broadcast_to(mine, (LANES, LANES))


def columns_body(got, chosen, *, shards, rows, tiles):
    flipped = got[pl.ds(1, LANES, stride=2), :].T[COLS : COLS + CAP, :]
    count = shards * rows * tiles
    tile = iota((LANES, count), 1)
    sender = (tile // tiles) % rows * shards + tile // (rows * tiles)
    moved = jnp.dot(
        jnp.concatenate([flipped, flipped], axis=0).astype(BF16),
        ones_where(iota((LANES, count), 0) == sender),
        preferred_element_type=F32,
    )[:CAP]
    here = iota((CAP, count), 0) == iota((CAP, count), 1) % tiles
    column = jnp.sum(jnp.where(here, moved, 0.0), axis=0, keepdims=True).astype(jnp.int32)
    chosen[...] = ones_where(iota((LANES, count), 0) == column)


def products(at, cols, d, tiles, diag, block):
    shard = at[1]
    per_row, rows = cols.shape
    for r in range(rows):
        d_row = d[pl.ds(CAP * shard + r, 1), :]
        d_col = as_column(d_row)
        mixed = jnp.zeros((LANES, LANES), F32)
        for t in range(per_row):
            tile = tiles[per_row * r + t]
            mixed += tile * d[pl.ds(cols[t, r], 1), :]
            back = jnp.sum(tile * d_col, axis=0, keepdims=True)
            block[rows + per_row * r + t : rows + per_row * r + t + 1, :] = 0.5 * back
        block[r : r + 1, :] = diag[r : r + 1, :] * d_row + 0.5 * row_sums(mixed)


def image_of(got, chosen, step, rows, tiles):
    shards = got.shape[0] // step
    own = jnp.concatenate([got[s * step : s * step + rows, :] for s in range(shards)], axis=0)
    back = jnp.concatenate(
        [got[s * step + rows : s * step + rows + tiles, :] for s in range(shards)], axis=0
    )
    return own + pick(chosen[...], back)


def start_body(at, cols, tiles, got, diag, r_out, weight_out, send, block):
    r_out[...] = got[pl.ds(0, LANES, stride=2), :]
    weight_out[...] = got[pl.ds(1, LANES, stride=2), :]
    products(at, cols, r_out, tiles, diag, block)
    size = block.shape[0]
    for s in range(send.shape[0] // size):
        send[s * size : (s + 1) * size, :] = block[...]


def step_body(
    at, cols, tiles, got, x, r, d, chosen, diag, *rest, ride, last, faces_in, faces_out
):
    per_row, rows = cols.shape
    size = rows * (1 + per_row)
    shards = LANES // rows
    mats = rows
    extra = list(rest)
    change = extra.pop(0) if ride == "reduce" else None
    parts = [extra.pop(0) for _ in range(4)] if ride == "next" else None
    x_before, weight = (extra.pop(0), extra.pop(0)) if ride == "next" else (None, None)
    y_faces = (extra.pop(0), extra.pop(0)) if faces_out else None
    x_out, r_out, d_out, send = (extra.pop(0) for _ in range(4))
    change_out, home = (extra.pop(0), extra.pop(0)) if ride == "gather" else (None, None)
    y_halo = (extra.pop(0), extra.pop(0)) if faces_in else None
    block = extra.pop()
    got_step = got.shape[0] // shards
    shard = at[1]
    image = image_of(got, chosen, got_step, rows, rows * per_row)
    old = d[...]
    norm = total(r[...] * r[...])
    alpha = norm / total(old * image)
    x_new = x[...] + alpha * old
    r_new = r[...] - alpha * image
    x_out[...] = x_new
    if ride == "next":
        [whole_change] = extra
        k = 0
        for part in parts:
            for i in range(part.shape[0] // shards):
                place = pl.multiple_of((at[0] ^ k) * shards, shards)
                whole_change[pl.ds(place, shards), :] = part[i * shards : (i + 1) * shards, :]
                k += 1
        r_new = r_new + whole_change[...] - weight[...] * (x_new - x_before[...])
        d_out[...] = r_new
    else:
        d_out[...] = r_new + (total(r_new * r_new) / norm) * old
    r_out[...] = r_new
    if last:
        lanes = jnp.zeros((1, LANES), F32)
        for i in range(rows):
            d_row = d_out[pl.ds(CAP * shard + i, 1), :]
            mixed = jnp.zeros((LANES, LANES), F32)
            for t in range(per_row):
                mixed += tiles[per_row * i + t] * d_out[pl.ds(cols[t, i], 1), :]
            lanes += diag[i : i + 1, :] * d_row * d_row
            lanes += jnp.sum(mixed * as_column(d_row), axis=0, keepdims=True)
        send[...] = jnp.broadcast_to(lanes, send.shape)
    else:
        products(at, cols, d_out, tiles, diag, block)
        send_step = send.shape[0] // shards
        if ride == "reduce":
            found = change[:shards, :]
            for m in range(1, mats):
                found = found + change[2 * m * shards : (2 * m + 1) * shards, :]
        for s in range(shards):
            first = s * send_step
            send[first : first + size, :] = block[...]
            first += size
            if ride == "reduce":
                send[first : first + shards, :] = found
                for m in range(mats):
                    row = (2 * m + 1) * shards + s
                    send[first + shards + m : first + shards + m + 1, :] = change[row : row + 1, :]
                first += shards + mats
            if faces_out:
                face = jnp.where(shard < s, y_faces[1][...], y_faces[0][...])
                deep = face.shape[0]
                send[first : first + deep, :] = face[:, :LANES]
                send[first + deep : first + 2 * deep, :] = face[:, LANES:]
    first = size
    if ride == "gather":
        found = jnp.zeros((shards, LANES), F32)
        for s in range(shards):
            row = s * got_step + size
            found += got[row : row + shards, :]
            home[s * mats : (s + 1) * mats, :] = got[row + shards : row + shards + mats, :]
        change_out[...] = found
        first += shards + mats
    if faces_in:
        deep = y_halo[0].shape[0]
        for halo, other, there in (
            (y_halo[0], jnp.maximum(shard - 1, 0), shard > 0),
            (y_halo[1], jnp.minimum(shard + 1, shards - 1), shard < shards - 1),
        ):
            row = pl.multiple_of(other * got_step + first, 8)
            for half in range(2):
                values = got[pl.ds(row + half * deep, deep), :]
                halo[:, half * LANES : (half + 1) * LANES] = jnp.where(there, values, 0.0)


def final_body(at, got, x, r, d, out):
    alpha = total(r[...] * r[...]) / total(got[...])
    here = pl.ds(pl.multiple_of(CAP * at[1], CAP), CAP)
    out[...] = x[here, :] + alpha * d[here, :]


def even(at, dim):
    return (at[dim] & 1) == 0


def edges_body(at, px0, px1, py0, py1, tx1, ty1, xa, xb, ya, yb):
    wide, deep = px0.shape[1], py0.shape[0]
    low, high = px0[0], px1[0]
    xa[:wide, :] = jnp.where(even(at, 0), high, low)
    xb[:wide, :] = jnp.where(even(at, 0), low, high)
    xa[wide:, :] = tx1[0, 0]
    xb[wide:, :] = tx1[0, 0]
    low, high = py0[:, 0, :], py1[:, 7, :]
    ya[:deep, :] = jnp.where(even(at, 1), high, low)
    yb[:deep, :] = jnp.where(even(at, 1), low, high)
    ya[deep:, :] = ty1[0, :, 7, :]
    yb[deep:, :] = ty1[0, :, 7, :]


def edges(at, pressure, trans):
    nx, ny, nz = pressure.shape
    y_last = ny // 8 - 1
    out = [(2 * ny, nz)] * 2 + [(2 * nx, nz)] * 2
    pressure, trans = in_hbm(pressure), in_hbm(trans)
    return pl.pallas_call(
        edges_body,
        grid=(1,),
        out_shape=tuple(sent(*v) for v in out),
        in_specs=[
            SMEM,
            pl.BlockSpec((1, ny, nz), lambda i: (0, 0, 0)),
            pl.BlockSpec((1, ny, nz), lambda i: (nx - 1, 0, 0)),
            pl.BlockSpec((nx, 8, nz), lambda i: (0, 0, 0)),
            pl.BlockSpec((nx, 8, nz), lambda i: (0, y_last, 0)),
            pl.BlockSpec((1, 1, ny, nz), lambda i: (0, nx - 1, 0, 0)),
            pl.BlockSpec((1, nx, 8, nz), lambda i: (1, 0, y_last, 0)),
        ],
        out_specs=tuple(pl.BlockSpec(v, lambda i: (0, 0)) for v in out),
        compiler_params=params(),
        name="edges",
    )(at, pressure, pressure, pressure, pressure, trans, trans)


def sweep_body(
    at, xa, xb, ya, yb, cxa, cxb, cya, cyb, p, p_after, trans, cell, rhs, *rest, first, last, fluxes, y_in, y_out
):
    rest = list(rest)
    weight = None if first else rest.pop(0)
    if fluxes:
        got, values = rest.pop(0), [rest.pop(0) for _ in range(fluxes)]
    out = rest.pop(0)
    weight_out = rest.pop(0) if first else None
    rhs_out = rest.pop(0) if fluxes else None
    if fluxes:
        found, spread, cell_row = rest.pop(), rest.pop(), rest.pop()
    carry_t = rest.pop() if first else None
    carry = rest.pop()
    step = pl.program_id(0)
    steps = pl.num_programs(0)
    many, ny, nz = out.shape
    nx = ya.shape[0] if not first else ya.shape[0] // 2
    row = iota((ny, nz), 0)
    lane = iota((ny, nz), 1)
    x_even, y_even = even(at, 0), even(at, 1)

    @pl.when(step == 0)
    def _():
        if fluxes == 1:
            spread_flux(got[...], values[0][...], spread, cell_row, nz)
        if fluxes == 2:
            message = got[...]
            flux = values[0][...] - at_mortar(message, values[1][...])
            spread_flux(message, kappa_of(message) * flux, spread, cell_row, nz)
        tx_low = jnp.where(x_even, cxb[ny:, :], cxa[ny:, :])
        carry[...] = tx_low * (jnp.where(x_even, xb[:ny, :], xa[:ny, :]) - p[0])
        if first:
            carry_t[...] = tx_low

    if fluxes:
        found[...] = sources(many * ny, step, spread, cell_row)
    for i in range(many):
        here_at = step * many + i
        right = rhs[i]
        if fluxes:
            right = right + found[i * ny : (i + 1) * ny, :]
            rhs_out[i] = right
        here = p[i]
        if i + 1 < many:
            after = p[i + 1]
        else:
            x_high = jnp.where(x_even, xa[:ny, :], xb[:ny, :])
            after = jnp.where(step + 1 < steps, p_after[0], x_high)
        one = pl.ds(here_at, 1)
        edge = pl.ds(nx + here_at, 1)
        y_low, y_high = ya[one, :], yb[one, :]
        if not y_in:
            y_low, y_high = jnp.where(y_even, y_high, y_low), jnp.where(y_even, y_low, y_high)
        ty_edge = jnp.where(y_even, cyb[edge, :], cya[edge, :])
        tx, ty, tz = trans[0, i], trans[1, i], trans[2, i]
        fx = tx * (here - after)
        y_next = jnp.where(row == ny - 1, y_high, pltpu.roll(here, ny - 1, 0))
        fy = ty * (here - y_next)
        fy_low = jnp.where(row == 0, ty_edge * (y_low - here[:1]), pltpu.roll(fy, 1, 0))
        z_next = jnp.where(lane == nz - 1, 0.0, pltpu.roll(here, nz - 1, 1))
        fz = tz * (here - z_next)
        fz_low = jnp.where(lane == 0, 0.0, pltpu.roll(fz, 1, 1))
        if first:
            ty_before = jnp.where(row == 0, ty_edge, pltpu.roll(ty, 1, 0))
            tz_before = jnp.where(lane == 0, 0.0, pltpu.roll(tz, 1, 1))
            diagonal = cell[i] + tx + carry_t[...] + ty + ty_before + tz + tz_before
            w = WEIGHT / diagonal
            weight_out[i] = w
            carry_t[...] = tx
        else:
            w = weight[i]
        applied = cell[i] * here + fx - carry[...] + fy - fy_low + fz - fz_low
        carry[...] = fx
        out[i] = here + w * (right - applied)
    if last:
        return
    xa_out, xb_out, ya_out, yb_out = rest
    start, end = step == 0, step == steps - 1

    @pl.when(start & x_even)
    def _():
        xb_out[...] = out[0]

    @pl.when(start & ~x_even)
    def _():
        xa_out[...] = out[0]

    @pl.when(end & x_even)
    def _():
        xa_out[...] = out[many - 1]

    @pl.when(end & ~x_even)
    def _():
        xb_out[...] = out[many - 1]

    for i in range(many):
        one = pl.ds(step * many + i, 1)
        low, high = out[i, :1, :], out[i, ny - 1 :, :]
        if not y_out:
            low, high = jnp.where(y_even, high, low), jnp.where(y_even, low, high)
        ya_out[one, :] = low
        yb_out[one, :] = high


def sweep(at, p, halo, faces, trans, cell, rhs, weight=None, last=False, got=None, values=(), y_in=False, y_out=False, many=4):
    nx, ny, nz = p.shape
    part = pl.BlockSpec((many, ny, nz), lambda i: (i, 0, 0))
    x_face = pl.BlockSpec((ny, nz), lambda i: (0, 0))
    y_face = pl.BlockSpec((nx, nz), lambda i: (0, 0))
    first = weight is None
    out_shape, out_specs = [shape(nx, ny, nz)], [part]
    if first:
        out_shape.append(shape(nx, ny, nz))
        out_specs.append(part)
    scratch = [pltpu.VMEM((ny, nz), F32)] * (2 if first else 1)
    if values:
        out_shape.append(shape(nx, ny, nz))
        out_specs.append(part)
        scratch += [
            pltpu.VMEM((1, CAP * LANES), jnp.int32),
            pltpu.VMEM((CAP * LANES, 2 * nz), BF16),
            pltpu.VMEM((many * ny, nz), F32),
        ]
    if not last:
        out_shape += [sent(ny, nz)] * 2 + [sent(nx, nz)] * 2
        out_specs += [x_face, x_face, y_face, y_face]
    after = pl.BlockSpec(
        (1, ny, nz), lambda i: (jnp.minimum((i + 1) * many, nx - 1), 0, 0)
    )
    operands = [*halo, *faces, p, p, trans, cell, rhs] + ([] if first else [weight])
    operands += [got, *values] if values else []
    return pl.pallas_call(
        functools.partial(sweep_body, first=first, last=last, fluxes=len(values), y_in=y_in, y_out=y_out),
        grid=(nx // many,),
        out_shape=tuple(out_shape),
        in_specs=[SMEM]
        + [whole(v.shape) for v in (*halo, *faces)]
        + [part, after]
        + [pl.BlockSpec((3, many, ny, nz), lambda i: (0, i, 0, 0)), part, part]
        + ([] if first else [part])
        + ([whole(v.shape) for v in (got, *values)] if values else []),
        out_specs=tuple(out_specs),
        scratch_shapes=scratch,
        compiler_params=params(),
        cost_estimate=pl.CostEstimate(flops=6_000_000, bytes_accessed=8 << 20, transcendentals=0),
        name="sweep",
    )(at, *(in_hbm(v) for v in operands))


def swap(v, axis, count, low):
    pairs = [(i, i + 1) for i in range(low, count - 1, 2)]
    return lax.ppermute(v, axis, pairs + [(b, a) for a, b in pairs])


def swapped(xa, xb, ya, yb, mats, shards):
    return (
        swap(xa, "mat", mats, 0),
        swap(xb, "mat", mats, 1),
        swap(ya, "frac", shards, 0),
        swap(yb, "frac", shards, 1),
    )


def body(
    pressure_start,
    face_trans,
    cell_coef,
    matrix_source,
    mortar_owner,
    mortar_cell,
    mortar_frac,
    mortar_kappa,
    tiles,
    tile_cols,
    frac_diag,
    frac_source,
    fracture_start,
):
    nx, ny, nz = pressure_start.shape
    mats, shards = lax.axis_size("mat"), lax.axis_size("frac")
    rows, per_row = tile_cols.shape
    count = mortar_cell.shape[0]
    size = rows * (1 + per_row)
    at = jnp.stack([lax.axis_index("mat"), lax.axis_index("frac")]).astype(jnp.int32)
    everyone = functools.partial(
        lax.all_to_all, axis_name=("mat", "frac"), split_axis=0, concat_axis=0, tiled=True
    )
    over_frac = functools.partial(
        lax.all_to_all, axis_name="frac", split_axis=0, concat_axis=0, tiled=True
    )
    over_mat = functools.partial(
        lax.all_to_all, axis_name="mat", split_axis=0, concat_axis=0, tiled=True
    )
    square = shape(LANES, LANES)
    owner = mortar_owner.reshape(1, count)
    frac, kappa = mortar_frac.reshape(1, count), mortar_kappa.reshape(1, count)
    flat = (nx * ny, nz)
    tile_list = tiles.reshape(rows * per_row, LANES, LANES)
    diag = frac_diag.reshape(rows, LANES)
    square_scratch = pltpu.VMEM((LANES, LANES), F32)
    gathered = pltpu.VMEM((CAP * LANES, nz), F32)
    block = pltpu.VMEM((size, LANES), F32)
    scalars = (at, tile_cols.T)
    fetch_scratch = [pltpu.VMEM(flat, F32), pltpu.SemaphoreType.DMA((8,))]

    send, slot = call(
        pack_body,
        (sent(2 * LANES, LANES), pltpu.HBM((1, count), jnp.int32)),
        owner,
        mortar_cell.reshape(1, count),
        frac,
        kappa,
        fracture_start.reshape(rows, LANES),
        scalars=scalars,
        scratch=[square_scratch],
        name="pack",
        least=1,
    )
    send, edges_at = lax.optimization_barrier((send, at))
    got = everyone(send)

    faces = swapped(*edges(edges_at, pressure_start, face_trans), mats, shards)
    got, *faces = lax.optimization_barrier((got, *faces))

    send, x_start, trace, flux, message = call(
        first_body,
        (sent(2 * LANES, LANES), square, *[sent(LANES, LANES)] * 3),
        got,
        diag,
        frac_source.reshape(rows, LANES),
        scalars=scalars,
        raw=(tile_list, pressure_start.reshape(flat)),
        scratch=[
            gathered,
            square_scratch,
            pltpu.VMEM((per_row, LANES, LANES), F32),
            pltpu.SemaphoreType.DMA(()),
            *fetch_scratch,
        ],
        flops=2e9,
        name="first",
    )
    reduced = everyone(send)
    pressure, weight, rhs, *sides = sweep(
        at, pressure_start, faces, faces, face_trans, cell_coef, matrix_source, got=message, values=(flux,)
    )
    sides = swapped(*sides, mats, shards)

    send = call(sum_body, sent(2 * LANES, LANES), reduced, name="sums")
    send, pressure = lax.optimization_barrier((send, pressure))
    residuals = everyone(send)
    chosen = call(
        functools.partial(columns_body, shards=shards, rows=rows, tiles=per_row),
        shape(LANES, shards * rows * per_row, dtype=BF16),
        got,
        name="columns",
    )
    pressure, *sides = sweep(
        at, pressure, sides, faces, face_trans, cell_coef, rhs, weight, y_out=True
    )

    r, sums, send = call(
        start_body,
        (square, sent(LANES, LANES), sent(shards * size, LANES)),
        residuals,
        diag,
        scalars=scalars,
        resident=(tile_list,),
        scratch=[block],
        name="start",
    )
    x, d = x_start, r
    send, pressure = lax.optimization_barrier((send, pressure))
    arrived = over_frac(send)
    trace, change = call(
        second_body,
        (sent(LANES, LANES), sent(2 * LANES, LANES)),
        side=(message, trace),
        raw=(pressure.reshape(flat),),
        scratch=[gathered, *fetch_scratch, square_scratch],
        flops=2e9,
        name="second",
    )

    arrived, change = lax.optimization_barrier((arrived, change))
    change = over_mat(change)
    arrived, change = lax.optimization_barrier((arrived, change))

    def step(arrived, x, r, d, *more, ride=None, last=False, faces_in=False, faces=(), side=()):
        length = size + (shards + mats if ride == "reduce" else 0) + (2 * nx if faces else 0)
        outs = [square, square, square, sent(shards * (1 if last else length), LANES)]
        if ride == "gather":
            outs += [sent(shards, LANES), sent(LANES, LANES)]
        if faces_in:
            outs += [sent(nx, nz)] * 2
        return call(
            functools.partial(
                step_body, ride=ride, last=last, faces_in=faces_in, faces_out=bool(faces)
            ),
            tuple(outs),
            arrived,
            x,
            r,
            d,
            chosen,
            diag,
            *more,
            side=(*side, *faces),
            scalars=scalars,
            resident=(tile_list,),
            scratch=([square_scratch] if ride == "next" else []) + [block],
            name="step",
        )

    def swapped_mat(xa, xb):
        return swap(xa, "mat", mats, 0), swap(xb, "mat", mats, 1)

    x, r, d, send = step(arrived, x, r, d, change, ride="reduce")
    send, trace, *x_sides = lax.optimization_barrier((send, trace, *sides[:2]))
    arrived = over_frac(send)
    x_sides = swapped_mat(*x_sides)
    arrived, *x_sides = lax.optimization_barrier((arrived, *x_sides))

    x, r, d, send, change, home = step(arrived, x, r, d, ride="gather", faces=sides[2:])
    arrived = over_frac(send)
    parts = [change]
    for hop in (1, 2, 4):
        mine = jnp.concatenate(parts, axis=0) if hop > 1 else change
        parts.append(lax.ppermute(mine, "mat", [(i, i ^ hop) for i in range(mats)]))

    x, r, d, send, *y_sides = step(
        arrived, x, r, d, faces_in=True, ride="next", side=(*parts, x_start, sums))
    x_flux = x
    arrived = over_frac(send)
    pressure, rhs, *sides = sweep(
        at,
        pressure,
        (*x_sides, *y_sides),
        faces,
        face_trans,
        cell_coef,
        matrix_source,
        weight,
        got=message,
        values=(trace, x_flux),
        y_in=True,
        y_out=True,
    )
    arrived, pressure, *sides = lax.optimization_barrier((arrived, pressure, *sides))
    x, r, d, send = step(arrived, x, r, d, faces=sides[2:])
    send, home, *sides = lax.optimization_barrier((send, home, *sides[:2]))
    arrived = over_frac(send)
    x_sides = swapped_mat(*sides)
    flux = call(
        functools.partial(home_body, mats=mats),
        shape(1, count),
        side=(home, owner, slot, frac, kappa, x_flux),
        name="home",
    )
    arrived, flux, *x_sides = lax.optimization_barrier((arrived, flux, *x_sides))
    x, r, d, send, *y_sides = step(arrived, x, r, d, last=True, faces_in=True)
    send, pressure, flux = lax.optimization_barrier((send, pressure, flux))
    arrived = over_frac(send)
    [pressure] = sweep(
        at,
        pressure,
        (*x_sides, *y_sides),
        faces,
        face_trans,
        cell_coef,
        rhs,
        weight,
        last=True,
        y_in=True,
    )
    fracture = call(
        final_body, shape(rows, LANES), arrived, x, r, d, scalars=(at,), name="final"
    )
    return pressure, fracture.reshape(rows * LANES), flux.reshape(count)


def solution(mesh):
    in_specs = (
        P("mat", "frac", None),
        P(None, "mat", "frac", None),
        P("mat", "frac", None),
        P("mat", "frac", None),
        P(("mat", "frac"), None),
        P(("mat", "frac")),
        P(("mat", "frac")),
        P(("mat", "frac")),
        P("frac", None, None, None),
        P("frac", None),
        P("frac"),
        P("frac"),
        P("frac"),
    )
    out_specs = (P("mat", "frac", None), P("frac"), P(("mat", "frac")))
    return jax.shard_map(body, mesh=mesh, in_specs=in_specs, out_specs=out_specs, check_vma=False)
```

```python
import functools
import math

import jax
import jax.numpy as jnp
from jax import lax
from jax.experimental import pallas as pl
from jax.experimental.pallas import tpu as pltpu
from jax.sharding import PartitionSpec as P

WEIGHT = 0.8
CAP = 8
LANES = 128
LARGE = 1 << 18
F32 = jnp.float32
BF16 = jnp.bfloat16
SMEM = pl.BlockSpec(memory_space=pltpu.SMEM)
VMEM = pl.BlockSpec(memory_space=pltpu.VMEM)
RAW = pl.BlockSpec(memory_space=pltpu.HBM)
X, Y, Z, HI, LO, KAPPA, COLS = (CAP * i for i in range(7))


def shape(*dims, dtype=F32):
    if math.prod(dims) >= LARGE:
        return pltpu.HBM(dims, dtype)
    return jax.ShapeDtypeStruct(dims, dtype)


def sent(*dims):
    return pltpu.HBM(dims, F32)


def in_hbm(x, least=LARGE):
    if x.size < least:
        return x
    return pltpu.with_memory_space_constraint(x, pltpu.HBM)


def on_chip(v):
    return isinstance(v, jax.ShapeDtypeStruct) and math.prod(v.shape) < LARGE


def whole(dims):
    return pl.BlockSpec(dims, lambda i: (0,) * len(dims), pipeline_mode=pl.Buffered(1))


def params():
    return pltpu.CompilerParams(vmem_limit_bytes=32 << 20)


def call(
    body, outs, *operands, scalars=(), raw=(), resident=(), side=(), scratch=(), flops=1e6, nbytes=1e6, name=None, least=LARGE
):
    single = not isinstance(outs, tuple)
    outs = (outs,) if single else outs
    result = pl.pallas_call(
        body,
        grid=(1,),
        out_shape=outs,
        in_specs=[SMEM] * len(scalars) + [RAW] * len(raw) + [VMEM] * len(resident) + [VMEM if v.size < least else whole(v.shape) for v in operands]
        + [whole(v.shape) for v in side],
        out_specs=tuple(
            VMEM if on_chip(v) else pl.BlockSpec(v.shape, lambda i, n=len(v.shape): (0,) * n)
            for v in outs
        ),
        scratch_shapes=scratch,
        compiler_params=params(),
        cost_estimate=pl.CostEstimate(
            flops=int(flops), bytes_accessed=int(nbytes), transcendentals=0
        ),
        name=name,
    )(
        *scalars,
        *(in_hbm(v, least) for v in raw),
        *resident,
        *(in_hbm(v, least) for v in operands),
        *(in_hbm(v, 1) for v in side),
    )
    return result[0] if single else result


def iota(dims, dim):
    return lax.broadcasted_iota(jnp.int32, dims, dim)


def ones_where(mask):
    return jnp.where(mask, 1.0, 0.0).astype(BF16)


def halves(v):
    top = v.astype(BF16)
    return jnp.concatenate([top, (v - top.astype(F32)).astype(BF16)], axis=1)


def pick_rounded(chosen, v):
    width = v.shape[1]
    out = jnp.dot(chosen, halves(v), preferred_element_type=F32)
    return out[:, :width] + out[:, width:]


def split(v):
    top = v.astype(BF16)
    rest = v - top.astype(F32)
    middle = rest.astype(BF16)
    low = (rest - middle.astype(F32)).astype(BF16)
    return jnp.concatenate([top, middle, low], axis=1)


def pick(chosen, v):
    width = v.shape[1]
    out = jnp.dot(chosen, split(v), preferred_element_type=F32)
    return out[:, :width] + out[:, width : 2 * width] + out[:, 2 * width :]


def total(v):
    return jnp.sum(jnp.sum(v, axis=1, keepdims=True), axis=0, keepdims=True)


def row_sums(v):
    return jnp.sum(v.T, axis=0, keepdims=True)


def as_column(row):
    return jnp.broadcast_to(row, (LANES, LANES)).T


def pack_body(at, cols, owner, cell, frac, kappa, x_own, send, slot_out, blocks):
    count = owner.shape[1]
    mine = at[0]
    own = owner[...]
    slot = jnp.zeros((1, count), jnp.int32)
    for first in range(0, count, LANES):
        column = jnp.broadcast_to(own[:, first : first + LANES], (LANES, LANES)).T
        column = jnp.concatenate([column] * (count // LANES), axis=1)
        before = iota((LANES, count), 0) + first < iota((LANES, count), 1)
        slot += jnp.sum(jnp.where((column == own) & before, 1, 0), axis=0, keepdims=True)
    slot_out[...] = slot
    here = iota((CAP, count), 0) == slot
    c, f = cell[...], frac[...]
    k = kappa[...]
    top = k.astype(BF16).astype(F32)
    middle = (k - top).astype(BF16).astype(F32)
    low = k - top - middle
    whole = [c >> 14, (c >> 8) & 63, c & 255, f >> 7, f & 127]
    rows = [jnp.where(here, v.astype(F32), 0.0) for v in whole]
    rows = jnp.concatenate([*rows, jnp.where(here, top, 0.0), jnp.zeros((LANES - 6 * CAP, count), F32)], axis=0)
    chosen = ones_where(iota((LANES, count), 0) == own)
    nt = functools.partial(
        lax.dot_general,
        dimension_numbers=(((1,), (1,)), ((), ())),
        preferred_element_type=F32,
    )

    def kappas(v):
        return jnp.concatenate(
            [
                jnp.zeros((KAPPA, count), F32),
                jnp.where(here, v, 0.0),
                jnp.zeros((LANES - 6 * CAP, count), F32),
            ],
            axis=0,
        ).astype(BF16)

    message = nt(chosen, rows.astype(BF16)) + nt(chosen, kappas(middle)) + nt(chosen, kappas(low))
    lane = iota((1, LANES), 1)
    extra = jnp.zeros((1, LANES), F32)
    for t in range(cols.shape[0]):
        extra = jnp.where(lane == COLS + t, cols[t, mine].astype(F32), extra)
    blocks[...] = jnp.broadcast_to(x_own[pl.ds(mine, 1), :], (LANES, LANES))
    send[pl.ds(0, LANES, stride=2), :] = blocks[...]
    send[pl.ds(1, LANES, stride=2), :] = message + extra


def by_slot(message, k):
    x = message[:, X + k : X + k + 1].astype(jnp.int32)
    y = message[:, Y + k : Y + k + 1].astype(jnp.int32)
    z = message[:, Z + k : Z + k + 1].astype(jnp.int32)
    hi = message[:, HI + k : HI + k + 1].astype(jnp.int32)
    lo = message[:, LO + k : LO + k + 1].astype(jnp.int32)
    return x * 64 + y, z, hi, lo, message[:, KAPPA + k : KAPPA + k + 1]


def in_parts(source, target, arrived):
    parts = arrived.shape[0]
    each = source.shape[0] // parts
    copies = []
    for i in range(parts):
        part = pl.ds(i * each, each)
        copies.append(
            pltpu.make_async_copy(source.at[part], target.at[part], arrived.at[i])
        )
        copies[-1].start()
    return copies


def traces(message, pressure_all, pressure, here, gathered):
    copies = in_parts(pressure_all, pressure, here)
    rows, depth = pressure.shape
    chosen = jnp.concatenate(
        [ones_where(iota((LANES, rows), 1) == by_slot(message, k)[0]) for k in range(CAP)], axis=0
    )
    for copy in copies:
        copy.wait()
    gathered[...] = pick_rounded(chosen, pressure[...])
    lane = iota((LANES, LANES), 1)
    out = jnp.zeros((LANES, LANES), F32)
    for k in range(CAP):
        z = by_slot(message, k)[1]
        part = gathered[k * LANES : (k + 1) * LANES, :]
        value = jnp.sum(jnp.where(iota((LANES, depth), 1) == z, part, 0.0), axis=1, keepdims=True)
        out = jnp.where(lane == k, value, out)
    return out


def at_mortar(message, x):
    chosen = jnp.concatenate(
        [ones_where(iota((LANES, LANES), 1) == by_slot(message, k)[2]) for k in range(CAP)], axis=0
    )
    found = pick(chosen, x)
    lane = iota((LANES, LANES), 1)
    out = jnp.zeros((LANES, LANES), F32)
    for k in range(CAP):
        part = found[k * LANES : (k + 1) * LANES, :]
        value = jnp.sum(jnp.where(lane == by_slot(message, k)[3], part, 0.0), axis=1, keepdims=True)
        out = jnp.where(lane == k, value, out)
    return out


def onto_fracture(message, *values):
    flipped = message.T
    hi = jnp.concatenate([flipped[HI + k : HI + k + 1, :] for k in range(CAP)], axis=1)
    chosen = ones_where(iota((LANES, CAP * LANES), 0) == hi.astype(jnp.int32))
    lane = iota((LANES, LANES), 1)
    wide = []
    for v in values:
        spread = [
            jnp.where(lane == by_slot(message, k)[3], v[:, k : k + 1], 0.0) for k in range(CAP)
        ]
        wide.append(jnp.concatenate(spread, axis=0))
    return [pick(chosen, v) for v in wide]


def kappa_of(message):
    lane = iota((LANES, LANES), 1)
    out = jnp.zeros((LANES, LANES), F32)
    for k in range(CAP):
        out = jnp.where(lane == k, message[:, KAPPA + k : KAPPA + k + 1], out)
    return out


def first_body(
    at,
    cols,
    tiles_all,
    pressure_all,
    got,
    diag,
    source,
    send,
    x_out,
    trace_out,
    flux_out,
    message_out,
    gathered,
    part,
    tiles,
    arrived,
    pressure,
    here,
):
    mine, shard = at[0], at[1]
    per_row = cols.shape[0]
    fetch = pltpu.make_async_copy(tiles_all.at[pl.ds(per_row * mine, per_row)], tiles, arrived)
    fetch.start()
    groups = LANES // CAP
    for m in range(CAP):
        x_out[pl.ds(m, groups, stride=CAP), :] = got[
            pl.ds(2 * m * groups, groups, stride=2), :
        ]
    message = got[pl.ds(1, LANES, stride=2), :]
    message_out[...] = message
    trace = traces(message, pressure_all, pressure, here, gathered)
    kappa = kappa_of(message)
    flux = kappa * (trace - at_mortar(message, x_out[...]))
    load, weight = onto_fracture(message, flux, kappa)
    part[...] = load
    row = CAP * shard + mine
    x_row = x_out[pl.ds(row, 1), :]
    x_col = as_column(x_row)
    mixed = jnp.zeros((LANES, LANES), F32)
    fetch.wait()
    for t in range(per_row):
        tile = tiles[t]
        mixed += tile * x_out[pl.ds(cols[t, mine], 1), :]
        back = jnp.sum(tile * x_col, axis=0, keepdims=True)
        part[pl.ds(cols[t, mine], 1), :] -= 0.5 * back
    part[pl.ds(row, 1), :] += source[pl.ds(mine, 1), :] - (
        diag[pl.ds(mine, 1), :] * x_row + 0.5 * row_sums(mixed)
    )
    send[pl.ds(0, LANES, stride=2), :] = part[...]
    send[pl.ds(1, LANES, stride=2), :] = weight
    trace_out[...] = trace
    flux_out[...] = flux


def spread_flux(message, values, spread, cell_row, depth):
    flipped = message.T
    for k in range(CAP):
        z = by_slot(message, k)[1]
        placed = jnp.where(iota((LANES, depth), 1) == z, values[:, k : k + 1], 0.0)
        spread[k * LANES : (k + 1) * LANES, :] = halves(placed)
        cell_row[:, k * LANES : (k + 1) * LANES] = (
            flipped[X + k : X + k + 1, :] * 64 + flipped[Y + k : Y + k + 1, :]
        ).astype(jnp.int32)


def sources(rows, step, spread, cell_row):
    depth = spread.shape[1] // 2
    row = iota((rows, CAP * LANES), 0) + step * rows
    chosen = ones_where(row == cell_row[...])
    out = jnp.dot(chosen, spread[...], preferred_element_type=F32)
    return out[:, :depth] + out[:, depth:]


def second_body(pressure_all, message, trace, trace_out, send, gathered, pressure, here, change):
    message = message[...]
    now = traces(message, pressure_all, pressure, here, gathered)
    trace_out[...] = now
    change[...] = onto_fracture(message, kappa_of(message) * (now - trace[...]))[0]
    mats = CAP
    each = LANES // mats
    for m in range(mats):
        part = slice(m * each, (m + 1) * each)
        send[2 * m * each : (2 * m + 1) * each, :] = change[part, :]
        send[(2 * m + 1) * each : (2 * m + 2) * each, :] = now[part, :]


def home_body(got, owner, slot, frac, kappa, x, flux, *, mats):
    count = owner.shape[1]

    def found(values, chosen):
        top = values.astype(BF16).astype(F32)
        middle = (values - top).astype(BF16).astype(F32)
        parts = jnp.concatenate([top, middle, values - top - middle], axis=0)
        if parts.shape[0] % 16:
            parts = jnp.concatenate([parts, jnp.zeros_like(top)], axis=0)
        out = jnp.dot(parts.astype(BF16), chosen, preferred_element_type=F32)
        n = values.shape[0]
        return out[:n] + out[n : 2 * n] + out[2 * n : 3 * n]

    shards = LANES // mats
    own = owner[...]
    source = (own & (shards - 1)) * mats + own // shards
    traces_all = found(got[...].T[:CAP, :], ones_where(iota((LANES, count), 0) == source))
    here = iota((CAP, count), 0) == slot[...]
    trace = jnp.sum(jnp.where(here, traces_all, 0.0), axis=0, keepdims=True)
    f = frac[...]
    x_all = found(x[...].T, ones_where(iota((LANES, count), 0) == f >> 7))
    here = iota((LANES, count), 0) == (f & 127)
    x_there = jnp.sum(jnp.where(here, x_all, 0.0), axis=0, keepdims=True)
    flux[...] = kappa[...] * (trace - x_there)


def sum_body(got, send):
    for i in range(2):
        mine = jnp.sum(got[pl.ds(i, LANES, stride=2), :], axis=0, keepdims=True)
        send[pl.ds(i, LANES, stride=2), :] = jnp.broadcast_to(mine, (LANES, LANES))


def columns_body(got, chosen, *, shards, rows, tiles):
    flipped = got[pl.ds(1, LANES, stride=2), :].T[COLS : COLS + CAP, :]
    count = shards * rows * tiles
    tile = iota((LANES, count), 1)
    sender = (tile // tiles) % rows * shards + tile // (rows * tiles)
    moved = jnp.dot(
        jnp.concatenate([flipped, flipped], axis=0).astype(BF16),
        ones_where(iota((LANES, count), 0) == sender),
        preferred_element_type=F32,
    )[:CAP]
    here = iota((CAP, count), 0) == iota((CAP, count), 1) % tiles
    column = jnp.sum(jnp.where(here, moved, 0.0), axis=0, keepdims=True).astype(jnp.int32)
    chosen[...] = ones_where(iota((LANES, count), 0) == column)


def products(at, cols, d, tiles, diag, block):
    shard = at[1]
    per_row, rows = cols.shape
    for r in range(rows):
        d_row = d[pl.ds(CAP * shard + r, 1), :]
        d_col = as_column(d_row)
        mixed = jnp.zeros((LANES, LANES), F32)
        for t in range(per_row):
            tile = tiles[per_row * r + t]
            mixed += tile * d[pl.ds(cols[t, r], 1), :]
            back = jnp.sum(tile * d_col, axis=0, keepdims=True)
            block[rows + per_row * r + t : rows + per_row * r + t + 1, :] = 0.5 * back
        block[r : r + 1, :] = diag[r : r + 1, :] * d_row + 0.5 * row_sums(mixed)


def image_of(got, chosen, step, rows, tiles):
    shards = got.shape[0] // step
    own = jnp.concatenate([got[s * step : s * step + rows, :] for s in range(shards)], axis=0)
    back = jnp.concatenate(
        [got[s * step + rows : s * step + rows + tiles, :] for s in range(shards)], axis=0
    )
    return own + pick(chosen[...], back)


def start_body(at, cols, tiles, got, diag, r_out, weight_out, send, block):
    r_out[...] = got[pl.ds(0, LANES, stride=2), :]
    weight_out[...] = got[pl.ds(1, LANES, stride=2), :]
    products(at, cols, r_out, tiles, diag, block)
    size = block.shape[0]
    for s in range(send.shape[0] // size):
        send[s * size : (s + 1) * size, :] = block[...]


def step_body(
    at, cols, tiles, got, chosen, diag, *rest, ride, last, faces_in, faces_out
):
    per_row, rows = cols.shape
    size = rows * (1 + per_row)
    shards = LANES // rows
    mats = rows
    extra = list(rest)
    change = extra.pop(0) if ride == "reduce" else None
    parts = [extra.pop(0) for _ in range(3)] if ride == "next" else None
    x, r, d = (extra.pop(0) for _ in range(3))
    if ride == "next":
        parts.insert(0, extra.pop(0))
    x_before, weight = (extra.pop(0), extra.pop(0)) if ride == "next" else (None, None)
    y_faces = (extra.pop(0), extra.pop(0)) if faces_out else None
    x_out, r_out, d_out, send = (extra.pop(0) for _ in range(4))
    change_out, home = (extra.pop(0), extra.pop(0)) if ride == "gather" else (None, None)
    y_halo = (extra.pop(0), extra.pop(0)) if faces_in else None
    block = extra.pop()
    got_step = got.shape[0] // shards
    shard = at[1]
    image = image_of(got, chosen, got_step, rows, rows * per_row)
    old = d[...]
    norm = total(r[...] * r[...])
    alpha = norm / total(old * image)
    x_new = x[...] + alpha * old
    r_new = r[...] - alpha * image
    x_out[...] = x_new
    if ride == "next":
        [whole_change] = extra
        k = 0
        for part in parts:
            for i in range(part.shape[0] // shards):
                place = pl.multiple_of((at[0] ^ k) * shards, shards)
                whole_change[pl.ds(place, shards), :] = part[i * shards : (i + 1) * shards, :]
                k += 1
        r_new = r_new + whole_change[...] - weight[...] * (x_new - x_before[...])
        d_out[...] = r_new
    else:
        d_out[...] = r_new + (total(r_new * r_new) / norm) * old
    r_out[...] = r_new
    if last:
        lanes = jnp.zeros((1, LANES), F32)
        for i in range(rows):
            d_row = d_out[pl.ds(CAP * shard + i, 1), :]
            mixed = jnp.zeros((LANES, LANES), F32)
            for t in range(per_row):
                mixed += tiles[per_row * i + t] * d_out[pl.ds(cols[t, i], 1), :]
            lanes += diag[i : i + 1, :] * d_row * d_row
            lanes += jnp.sum(mixed * as_column(d_row), axis=0, keepdims=True)
        send[...] = jnp.broadcast_to(lanes, send.shape)
    else:
        products(at, cols, d_out, tiles, diag, block)
        send_step = send.shape[0] // shards
        if ride == "reduce":
            found = change[:shards, :]
            for m in range(1, mats):
                found = found + change[2 * m * shards : (2 * m + 1) * shards, :]
        for s in range(shards):
            first = s * send_step
            send[first : first + size, :] = block[...]
            first += size
            if ride == "reduce":
                send[first : first + shards, :] = found
                for m in range(mats):
                    row = (2 * m + 1) * shards + s
                    send[first + shards + m : first + shards + m + 1, :] = change[row : row + 1, :]
                first += shards + mats
            if faces_out:
                face = jnp.where(shard < s, y_faces[1][...], y_faces[0][...])
                deep = face.shape[0]
                send[first : first + deep, :] = face[:, :LANES]
                send[first + deep : first + 2 * deep, :] = face[:, LANES:]
    first = size
    if ride == "gather":
        found = jnp.zeros((shards, LANES), F32)
        for s in range(shards):
            row = s * got_step + size
            found += got[row : row + shards, :]
            home[s * mats : (s + 1) * mats, :] = got[row + shards : row + shards + mats, :]
        change_out[...] = found
        first += shards + mats
    if faces_in:
        deep = y_halo[0].shape[0]
        for halo, other, there in (
            (y_halo[0], jnp.maximum(shard - 1, 0), shard > 0),
            (y_halo[1], jnp.minimum(shard + 1, shards - 1), shard < shards - 1),
        ):
            row = pl.multiple_of(other * got_step + first, 8)
            for half in range(2):
                values = got[pl.ds(row + half * deep, deep), :]
                halo[:, half * LANES : (half + 1) * LANES] = jnp.where(there, values, 0.0)


def final_body(at, got, x, r, d, out):
    alpha = total(r[...] * r[...]) / total(got[...])
    here = pl.ds(pl.multiple_of(CAP * at[1], CAP), CAP)
    out[...] = x[here, :] + alpha * d[here, :]


def even(at, dim):
    return (at[dim] & 1) == 0


def edges_body(at, px0, px1, py0, py1, tx1, ty1, xa, xb, ya, yb):
    wide, deep = px0.shape[1], py0.shape[0]
    low, high = px0[0], px1[0]
    xa[:wide, :] = jnp.where(even(at, 0), high, low)
    xb[:wide, :] = jnp.where(even(at, 0), low, high)
    xa[wide:, :] = tx1[0, 0]
    xb[wide:, :] = tx1[0, 0]
    low, high = py0[:, 0, :], py1[:, 7, :]
    ya[:deep, :] = jnp.where(even(at, 1), high, low)
    yb[:deep, :] = jnp.where(even(at, 1), low, high)
    ya[deep:, :] = ty1[0, :, 7, :]
    yb[deep:, :] = ty1[0, :, 7, :]


def edges(at, pressure, trans):
    nx, ny, nz = pressure.shape
    y_last = ny // 8 - 1
    out = [(2 * ny, nz)] * 2 + [(2 * nx, nz)] * 2
    pressure, trans = in_hbm(pressure), in_hbm(trans)
    return pl.pallas_call(
        edges_body,
        grid=(1,),
        out_shape=tuple(sent(*v) for v in out),
        in_specs=[
            SMEM,
            pl.BlockSpec((1, ny, nz), lambda i: (0, 0, 0)),
            pl.BlockSpec((1, ny, nz), lambda i: (nx - 1, 0, 0)),
            pl.BlockSpec((nx, 8, nz), lambda i: (0, 0, 0)),
            pl.BlockSpec((nx, 8, nz), lambda i: (0, y_last, 0)),
            pl.BlockSpec((1, 1, ny, nz), lambda i: (0, nx - 1, 0, 0)),
            pl.BlockSpec((1, nx, 8, nz), lambda i: (1, 0, y_last, 0)),
        ],
        out_specs=tuple(pl.BlockSpec(v, lambda i: (0, 0)) for v in out),
        compiler_params=params(),
        name="edges",
    )(at, pressure, pressure, pressure, pressure, trans, trans)


def sweep_body(
    at, xa, xb, ya, yb, cxa, cxb, cya, cyb, p, p_after, trans, cell, rhs, *rest, first, last, fluxes, y_in, y_out
):
    rest = list(rest)
    weight = None if first else rest.pop(0)
    if fluxes:
        got, values = rest.pop(0), [rest.pop(0) for _ in range(fluxes)]
    out = rest.pop(0)
    weight_out = rest.pop(0) if first else None
    rhs_out = rest.pop(0) if fluxes else None
    if fluxes:
        found, spread, cell_row = rest.pop(), rest.pop(), rest.pop()
    carry_t = rest.pop() if first else None
    carry = rest.pop()
    step = pl.program_id(0)
    steps = pl.num_programs(0)
    many, ny, nz = out.shape
    nx = ya.shape[0] if not first else ya.shape[0] // 2
    row = iota((ny, nz), 0)
    lane = iota((ny, nz), 1)
    x_even, y_even = even(at, 0), even(at, 1)

    @pl.when(step == 0)
    def _():
        if fluxes == 1:
            spread_flux(got[...], values[0][...], spread, cell_row, nz)
        if fluxes == 2:
            message = got[...]
            flux = values[0][...] - at_mortar(message, values[1][...])
            spread_flux(message, kappa_of(message) * flux, spread, cell_row, nz)
        tx_low = jnp.where(x_even, cxb[ny:, :], cxa[ny:, :])
        carry[...] = tx_low * (jnp.where(x_even, xb[:ny, :], xa[:ny, :]) - p[0])
        if first:
            carry_t[...] = tx_low

    if fluxes:
        found[...] = sources(many * ny, step, spread, cell_row)
    for i in range(many):
        here_at = step * many + i
        right = rhs[i]
        if fluxes:
            right = right + found[i * ny : (i + 1) * ny, :]
            rhs_out[i] = right
        here = p[i]
        if i + 1 < many:
            after = p[i + 1]
        else:
            x_high = jnp.where(x_even, xa[:ny, :], xb[:ny, :])
            after = jnp.where(step + 1 < steps, p_after[0], x_high)
        one = pl.ds(here_at, 1)
        edge = pl.ds(nx + here_at, 1)
        y_low, y_high = ya[one, :], yb[one, :]
        if not y_in:
            y_low, y_high = jnp.where(y_even, y_high, y_low), jnp.where(y_even, y_low, y_high)
        ty_edge = jnp.where(y_even, cyb[edge, :], cya[edge, :])
        tx, ty, tz = trans[0, i], trans[1, i], trans[2, i]
        fx = tx * (here - after)
        y_next = jnp.where(row == ny - 1, y_high, pltpu.roll(here, ny - 1, 0))
        fy = ty * (here - y_next)
        fy_low = jnp.where(row == 0, ty_edge * (y_low - here[:1]), pltpu.roll(fy, 1, 0))
        z_next = jnp.where(lane == nz - 1, 0.0, pltpu.roll(here, nz - 1, 1))
        fz = tz * (here - z_next)
        fz_low = jnp.where(lane == 0, 0.0, pltpu.roll(fz, 1, 1))
        if first:
            ty_before = jnp.where(row == 0, ty_edge, pltpu.roll(ty, 1, 0))
            tz_before = jnp.where(lane == 0, 0.0, pltpu.roll(tz, 1, 1))
            diagonal = cell[i] + tx + carry_t[...] + ty + ty_before + tz + tz_before
            w = WEIGHT / diagonal
            weight_out[i] = w
            carry_t[...] = tx
        else:
            w = weight[i]
        applied = cell[i] * here + fx - carry[...] + fy - fy_low + fz - fz_low
        carry[...] = fx
        out[i] = here + w * (right - applied)
    if last:
        return
    xa_out, xb_out, ya_out, yb_out = rest
    start, end = step == 0, step == steps - 1

    @pl.when(start & x_even)
    def _():
        xb_out[...] = out[0]

    @pl.when(start & ~x_even)
    def _():
        xa_out[...] = out[0]

    @pl.when(end & x_even)
    def _():
        xa_out[...] = out[many - 1]

    @pl.when(end & ~x_even)
    def _():
        xb_out[...] = out[many - 1]

    for i in range(many):
        one = pl.ds(step * many + i, 1)
        low, high = out[i, :1, :], out[i, ny - 1 :, :]
        if not y_out:
            low, high = jnp.where(y_even, high, low), jnp.where(y_even, low, high)
        ya_out[one, :] = low
        yb_out[one, :] = high


def sweep(at, p, halo, faces, trans, cell, rhs, weight=None, last=False, got=None, values=(), y_in=False, y_out=False, many=4):
    nx, ny, nz = p.shape
    part = pl.BlockSpec((many, ny, nz), lambda i: (i, 0, 0))
    x_face = pl.BlockSpec((ny, nz), lambda i: (0, 0))
    y_face = pl.BlockSpec((nx, nz), lambda i: (0, 0))
    first = weight is None
    out_shape, out_specs = [shape(nx, ny, nz)], [part]
    if first:
        out_shape.append(shape(nx, ny, nz))
        out_specs.append(part)
    scratch = [pltpu.VMEM((ny, nz), F32)] * (2 if first else 1)
    if values:
        out_shape.append(shape(nx, ny, nz))
        out_specs.append(part)
        scratch += [
            pltpu.VMEM((1, CAP * LANES), jnp.int32),
            pltpu.VMEM((CAP * LANES, 2 * nz), BF16),
            pltpu.VMEM((many * ny, nz), F32),
        ]
    if not last:
        out_shape += [sent(ny, nz)] * 2 + [sent(nx, nz)] * 2
        out_specs += [x_face, x_face, y_face, y_face]
    after = pl.BlockSpec(
        (1, ny, nz), lambda i: (jnp.minimum((i + 1) * many, nx - 1), 0, 0)
    )
    if y_in:
        halo = (*halo[:2], *(in_hbm(v, 1) for v in halo[2:]))
    operands = [*halo, *faces, p, p, trans, cell, rhs] + ([] if first else [weight])
    operands += [in_hbm(v, 1) for v in (got, *values)] if values else []
    return pl.pallas_call(
        functools.partial(sweep_body, first=first, last=last, fluxes=len(values), y_in=y_in, y_out=y_out),
        grid=(nx // many,),
        out_shape=tuple(out_shape),
        in_specs=[SMEM]
        + [whole(v.shape) for v in (*halo, *faces)]
        + [part, after]
        + [pl.BlockSpec((3, many, ny, nz), lambda i: (0, i, 0, 0)), part, part]
        + ([] if first else [part])
        + ([whole(v.shape) for v in (got, *values)] if values else []),
        out_specs=tuple(out_specs),
        scratch_shapes=scratch,
        compiler_params=params(),
        cost_estimate=pl.CostEstimate(flops=6_000_000, bytes_accessed=8 << 20, transcendentals=0),
        name="sweep",
    )(at, *(in_hbm(v) for v in operands))


def swap(v, axis, count, low):
    pairs = [(i, i + 1) for i in range(low, count - 1, 2)]
    return lax.ppermute(v, axis, pairs + [(b, a) for a, b in pairs])


def swapped(xa, xb, ya, yb, mats, shards):
    return (
        swap(xa, "mat", mats, 0),
        swap(xb, "mat", mats, 1),
        swap(ya, "frac", shards, 0),
        swap(yb, "frac", shards, 1),
    )


def body(
    pressure_start,
    face_trans,
    cell_coef,
    matrix_source,
    mortar_owner,
    mortar_cell,
    mortar_frac,
    mortar_kappa,
    tiles,
    tile_cols,
    frac_diag,
    frac_source,
    fracture_start,
):
    nx, ny, nz = pressure_start.shape
    mats, shards = lax.axis_size("mat"), lax.axis_size("frac")
    rows, per_row = tile_cols.shape
    count = mortar_cell.shape[0]
    size = rows * (1 + per_row)
    at = jnp.stack([lax.axis_index("mat"), lax.axis_index("frac")]).astype(jnp.int32)
    everyone = functools.partial(
        lax.all_to_all, axis_name=("mat", "frac"), split_axis=0, concat_axis=0, tiled=True
    )
    over_frac = functools.partial(
        lax.all_to_all, axis_name="frac", split_axis=0, concat_axis=0, tiled=True
    )
    over_mat = functools.partial(
        lax.all_to_all, axis_name="mat", split_axis=0, concat_axis=0, tiled=True
    )
    square = shape(LANES, LANES)
    owner = mortar_owner.reshape(1, count)
    frac, kappa = mortar_frac.reshape(1, count), mortar_kappa.reshape(1, count)
    flat = (nx * ny, nz)
    tile_list = tiles.reshape(rows * per_row, LANES, LANES)
    diag = frac_diag.reshape(rows, LANES)
    square_scratch = pltpu.VMEM((LANES, LANES), F32)
    gathered = pltpu.VMEM((CAP * LANES, nz), F32)
    block = pltpu.VMEM((size, LANES), F32)
    scalars = (at, tile_cols.T)
    fetch_scratch = [pltpu.VMEM(flat, F32), pltpu.SemaphoreType.DMA((8,))]

    send, slot = call(
        pack_body,
        (sent(2 * LANES, LANES), pltpu.HBM((1, count), jnp.int32)),
        owner,
        mortar_cell.reshape(1, count),
        frac,
        kappa,
        fracture_start.reshape(rows, LANES),
        scalars=scalars,
        scratch=[square_scratch],
        name="pack",
        least=1,
    )
    send, edges_at = lax.optimization_barrier((send, at))
    got = everyone(send)

    faces = swapped(*edges(edges_at, pressure_start, face_trans), mats, shards)

    send, x_start, trace, flux, message = call(
        first_body,
        (sent(2 * LANES, LANES), *[sent(LANES, LANES)] * 4),
        got,
        diag,
        frac_source.reshape(rows, LANES),
        scalars=scalars,
        raw=(tile_list, pressure_start.reshape(flat)),
        scratch=[
            gathered,
            square_scratch,
            pltpu.VMEM((per_row, LANES, LANES), F32),
            pltpu.SemaphoreType.DMA(()),
            *fetch_scratch,
        ],
        flops=2e9,
        name="first",
    )
    send, *faces = lax.optimization_barrier((send, *faces))
    reduced = everyone(send)
    pressure, weight, rhs, *sides = sweep(
        at, pressure_start, faces, faces, face_trans, cell_coef, matrix_source, got=message, values=(flux,)
    )
    sides = swapped(*sides, mats, shards)

    send = call(sum_body, sent(2 * LANES, LANES), reduced, name="sums")
    send, pressure = lax.optimization_barrier((send, pressure))
    residuals = everyone(send)
    chosen = call(
        functools.partial(columns_body, shards=shards, rows=rows, tiles=per_row),
        shape(LANES, shards * rows * per_row, dtype=BF16),
        got,
        name="columns",
    )
    pressure, *sides = sweep(
        at, pressure, sides, faces, face_trans, cell_coef, rhs, weight, y_out=True
    )

    r, sums, send = call(
        start_body,
        (*[sent(LANES, LANES)] * 2, sent(shards * size, LANES)),
        residuals,
        diag,
        scalars=scalars,
        resident=(tile_list,),
        scratch=[block],
        name="start",
    )
    x, d = x_start, r
    send, pressure = lax.optimization_barrier((send, pressure))
    arrived = over_frac(send)
    trace, change = call(
        second_body,
        (sent(LANES, LANES), sent(2 * LANES, LANES)),
        side=(message, trace),
        raw=(pressure.reshape(flat),),
        scratch=[gathered, *fetch_scratch, square_scratch],
        flops=2e9,
        name="second",
    )

    arrived, change = lax.optimization_barrier((arrived, change))
    change = over_mat(change)
    arrived, change = lax.optimization_barrier((arrived, change))

    def step(arrived, x, r, d, *more, ride=None, last=False, faces_in=False, faces=(), side=()):
        length = size + (shards + mats if ride == "reduce" else 0) + (2 * nx if faces else 0)
        outs = [*[sent(LANES, LANES)] * 3, sent(shards * (1 if last else length), LANES)]
        if ride == "gather":
            outs += [sent(shards, LANES), sent(LANES, LANES)]
        if faces_in:
            outs += [sent(nx, nz)] * 2
        return call(
            functools.partial(
                step_body, ride=ride, last=last, faces_in=faces_in, faces_out=bool(faces)
            ),
            tuple(outs),
            arrived,
            chosen,
            diag,
            *more,
            side=(x, r, d, *side, *faces),
            scalars=scalars,
            resident=(tile_list,),
            scratch=([square_scratch] if ride == "next" else []) + [block],
            name="step",
        )

    def swapped_mat(xa, xb):
        return swap(xa, "mat", mats, 0), swap(xb, "mat", mats, 1)

    x, r, d, send = step(arrived, x, r, d, change, ride="reduce")
    send, trace, *x_sides = lax.optimization_barrier((send, trace, *sides[:2]))
    arrived = over_frac(send)
    x_sides = swapped_mat(*x_sides)
    arrived, *x_sides = lax.optimization_barrier((arrived, *x_sides))

    x, r, d, send, change, home = step(arrived, x, r, d, ride="gather", faces=sides[2:])
    arrived = over_frac(send)
    parts = [change]
    for hop in (1, 2, 4):
        mine = jnp.concatenate(parts, axis=0) if hop > 1 else change
        parts.append(lax.ppermute(mine, "mat", [(i, i ^ hop) for i in range(mats)]))

    x, r, d, send, *y_sides = step(
        arrived, x, r, d, *parts[1:], faces_in=True, ride="next", side=(change, x_start, sums)
    )
    x_flux = x
    arrived = over_frac(send)
    pressure, rhs, *sides = sweep(
        at,
        pressure,
        (*x_sides, *y_sides),
        faces,
        face_trans,
        cell_coef,
        matrix_source,
        weight,
        got=message,
        values=(trace, x_flux),
        y_in=True,
        y_out=True,
    )
    arrived, pressure, *sides = lax.optimization_barrier((arrived, pressure, *sides))
    x, r, d, send = step(arrived, x, r, d, faces=sides[2:])
    send, home, *sides = lax.optimization_barrier((send, home, *sides[:2]))
    arrived = over_frac(send)
    x_sides = swapped_mat(*sides)
    flux = call(
        functools.partial(home_body, mats=mats),
        shape(1, count),
        side=(home, owner, slot, frac, kappa, x_flux),
        name="home",
    )
    arrived, flux, *x_sides = lax.optimization_barrier((arrived, flux, *x_sides))
    x, r, d, send, *y_sides = step(arrived, x, r, d, last=True, faces_in=True)
    send, pressure, flux = lax.optimization_barrier((send, pressure, flux))
    arrived = over_frac(send)
    [pressure] = sweep(
        at,
        pressure,
        (*x_sides, *y_sides),
        faces,
        face_trans,
        cell_coef,
        rhs,
        weight,
        last=True,
        y_in=True,
    )
    fracture = call(
        final_body, shape(rows, LANES), arrived, side=(x, r, d), scalars=(at,), name="final"
    )
    return pressure, fracture.reshape(rows * LANES), flux.reshape(count)


def solution(mesh):
    in_specs = (
        P("mat", "frac", None),
        P(None, "mat", "frac", None),
        P("mat", "frac", None),
        P("mat", "frac", None),
        P(("mat", "frac"), None),
        P(("mat", "frac")),
        P(("mat", "frac")),
        P(("mat", "frac")),
        P("frac", None, None, None),
        P("frac", None),
        P("frac"),
        P("frac"),
        P("frac"),
    )
    out_specs = (P("mat", "frac", None), P("frac"), P(("mat", "frac")))
    return jax.shard_map(body, mesh=mesh, in_specs=in_specs, out_specs=out_specs, check_vma=False)
```

```python
import functools
import math

import jax
import jax.numpy as jnp
from jax import lax
from jax.experimental import pallas as pl
from jax.experimental.pallas import tpu as pltpu
from jax.sharding import PartitionSpec as P

WEIGHT = 0.8
CAP = 8
LANES = 128
LARGE = 1 << 18
F32 = jnp.float32
BF16 = jnp.bfloat16
SMEM = pl.BlockSpec(memory_space=pltpu.SMEM)
VMEM = pl.BlockSpec(memory_space=pltpu.VMEM)
RAW = pl.BlockSpec(memory_space=pltpu.HBM)
X, Y, Z, HI, LO, KAPPA, COLS = (CAP * i for i in range(7))


def shape(*dims, dtype=F32):
    if math.prod(dims) >= LARGE:
        return pltpu.HBM(dims, dtype)
    return jax.ShapeDtypeStruct(dims, dtype)


def sent(*dims):
    return pltpu.HBM(dims, F32)


def in_hbm(x, least=LARGE):
    if x.size < least:
        return x
    return pltpu.with_memory_space_constraint(x, pltpu.HBM)


def on_chip(v):
    return isinstance(v, jax.ShapeDtypeStruct) and math.prod(v.shape) < LARGE


def whole(dims):
    return pl.BlockSpec(dims, lambda i: (0,) * len(dims), pipeline_mode=pl.Buffered(1))


def params():
    return pltpu.CompilerParams(vmem_limit_bytes=32 << 20)


def call(
    body, outs, *operands, scalars=(), raw=(), resident=(), side=(), scratch=(), flops=1e6, nbytes=1e6, name=None, least=LARGE
):
    single = not isinstance(outs, tuple)
    outs = (outs,) if single else outs
    result = pl.pallas_call(
        body,
        grid=(1,),
        out_shape=outs,
        in_specs=[SMEM] * len(scalars) + [RAW] * len(raw) + [VMEM] * len(resident) + [VMEM if v.size < least else whole(v.shape) for v in operands]
        + [whole(v.shape) for v in side],
        out_specs=tuple(
            VMEM if on_chip(v) else pl.BlockSpec(v.shape, lambda i, n=len(v.shape): (0,) * n)
            for v in outs
        ),
        scratch_shapes=scratch,
        compiler_params=params(),
        cost_estimate=pl.CostEstimate(
            flops=int(flops), bytes_accessed=int(nbytes), transcendentals=0
        ),
        name=name,
    )(
        *scalars,
        *(in_hbm(v, least) for v in raw),
        *resident,
        *(in_hbm(v, least) for v in operands),
        *(in_hbm(v, 1) for v in side),
    )
    return result[0] if single else result


def iota(dims, dim):
    return lax.broadcasted_iota(jnp.int32, dims, dim)


def ones_where(mask):
    return jnp.where(mask, 1.0, 0.0).astype(BF16)


def halves(v):
    top = v.astype(BF16)
    return jnp.concatenate([top, (v - top.astype(F32)).astype(BF16)], axis=1)


def pick_rounded(chosen, v):
    width = v.shape[1]
    out = jnp.dot(chosen, halves(v), preferred_element_type=F32)
    return out[:, :width] + out[:, width:]


def split(v):
    top = v.astype(BF16)
    rest = v - top.astype(F32)
    middle = rest.astype(BF16)
    low = (rest - middle.astype(F32)).astype(BF16)
    return jnp.concatenate([top, middle, low], axis=1)


def pick(chosen, v):
    width = v.shape[1]
    out = jnp.dot(chosen, split(v), preferred_element_type=F32)
    return out[:, :width] + out[:, width : 2 * width] + out[:, 2 * width :]


def total(v):
    return jnp.sum(jnp.sum(v, axis=1, keepdims=True), axis=0, keepdims=True)


def row_sums(v):
    return jnp.sum(v.T, axis=0, keepdims=True)


def as_column(row):
    return jnp.broadcast_to(row, (LANES, LANES)).T


def pack_body(at, cols, owner, cell, frac, kappa, x_own, send, slot_out, blocks):
    count = owner.shape[1]
    mine = at[0]
    own = owner[...]
    slot = jnp.zeros((1, count), jnp.int32)
    for first in range(0, count, LANES):
        column = jnp.broadcast_to(own[:, first : first + LANES], (LANES, LANES)).T
        column = jnp.concatenate([column] * (count // LANES), axis=1)
        before = iota((LANES, count), 0) + first < iota((LANES, count), 1)
        slot += jnp.sum(jnp.where((column == own) & before, 1, 0), axis=0, keepdims=True)
    slot_out[...] = slot
    here = iota((CAP, count), 0) == slot
    c, f = cell[...], frac[...]
    k = kappa[...]
    top = k.astype(BF16).astype(F32)
    middle = (k - top).astype(BF16).astype(F32)
    low = k - top - middle
    whole = [c >> 14, (c >> 8) & 63, c & 255, f >> 7, f & 127]
    rows = [jnp.where(here, v.astype(F32), 0.0) for v in whole]
    rows = jnp.concatenate([*rows, jnp.where(here, top, 0.0), jnp.zeros((LANES - 6 * CAP, count), F32)], axis=0)
    chosen = ones_where(iota((LANES, count), 0) == own)
    nt = functools.partial(
        lax.dot_general,
        dimension_numbers=(((1,), (1,)), ((), ())),
        preferred_element_type=F32,
    )

    def kappas(v):
        return jnp.concatenate(
            [
                jnp.zeros((KAPPA, count), F32),
                jnp.where(here, v, 0.0),
                jnp.zeros((LANES - 6 * CAP, count), F32),
            ],
            axis=0,
        ).astype(BF16)

    message = nt(chosen, rows.astype(BF16)) + nt(chosen, kappas(middle)) + nt(chosen, kappas(low))
    lane = iota((1, LANES), 1)
    extra = jnp.zeros((1, LANES), F32)
    for t in range(cols.shape[0]):
        extra = jnp.where(lane == COLS + t, cols[t, mine].astype(F32), extra)
    blocks[...] = jnp.broadcast_to(x_own[pl.ds(mine, 1), :], (LANES, LANES))
    send[pl.ds(0, LANES, stride=2), :] = blocks[...]
    send[pl.ds(1, LANES, stride=2), :] = message + extra


def by_slot(message, k):
    x = message[:, X + k : X + k + 1].astype(jnp.int32)
    y = message[:, Y + k : Y + k + 1].astype(jnp.int32)
    z = message[:, Z + k : Z + k + 1].astype(jnp.int32)
    hi = message[:, HI + k : HI + k + 1].astype(jnp.int32)
    lo = message[:, LO + k : LO + k + 1].astype(jnp.int32)
    return x * 64 + y, z, hi, lo, message[:, KAPPA + k : KAPPA + k + 1]


def in_parts(source, target, arrived):
    parts = arrived.shape[0]
    each = source.shape[0] // parts
    copies = []
    for i in range(parts):
        part = pl.ds(i * each, each)
        copies.append(
            pltpu.make_async_copy(source.at[part], target.at[part], arrived.at[i])
        )
        copies[-1].start()
    return copies


def traces(message, pressure_all, pressure, here, gathered):
    copies = in_parts(pressure_all, pressure, here)
    rows, depth = pressure.shape
    chosen = jnp.concatenate(
        [ones_where(iota((LANES, rows), 1) == by_slot(message, k)[0]) for k in range(CAP)], axis=0
    )
    for copy in copies:
        copy.wait()
    gathered[...] = pick_rounded(chosen, pressure[...])
    return at_depth(message, gathered)


def at_depth(message, gathered):
    depth = gathered.shape[1]
    lane = iota((LANES, LANES), 1)
    out = jnp.zeros((LANES, LANES), F32)
    for k in range(CAP):
        z = by_slot(message, k)[1]
        part = gathered[k * LANES : (k + 1) * LANES, :]
        value = jnp.sum(jnp.where(iota((LANES, depth), 1) == z, part, 0.0), axis=1, keepdims=True)
        out = jnp.where(lane == k, value, out)
    return out


def at_mortar(message, x):
    chosen = jnp.concatenate(
        [ones_where(iota((LANES, LANES), 1) == by_slot(message, k)[2]) for k in range(CAP)], axis=0
    )
    found = pick(chosen, x)
    lane = iota((LANES, LANES), 1)
    out = jnp.zeros((LANES, LANES), F32)
    for k in range(CAP):
        part = found[k * LANES : (k + 1) * LANES, :]
        value = jnp.sum(jnp.where(lane == by_slot(message, k)[3], part, 0.0), axis=1, keepdims=True)
        out = jnp.where(lane == k, value, out)
    return out


def onto_fracture(message, *values):
    flipped = message.T
    hi = jnp.concatenate([flipped[HI + k : HI + k + 1, :] for k in range(CAP)], axis=1)
    chosen = ones_where(iota((LANES, CAP * LANES), 0) == hi.astype(jnp.int32))
    lane = iota((LANES, LANES), 1)
    wide = []
    for v in values:
        spread = [
            jnp.where(lane == by_slot(message, k)[3], v[:, k : k + 1], 0.0) for k in range(CAP)
        ]
        wide.append(jnp.concatenate(spread, axis=0))
    return [pick(chosen, v) for v in wide]


def kappa_of(message):
    lane = iota((LANES, LANES), 1)
    out = jnp.zeros((LANES, LANES), F32)
    for k in range(CAP):
        out = jnp.where(lane == k, message[:, KAPPA + k : KAPPA + k + 1], out)
    return out


def first_body(
    at,
    cols,
    tiles_all,
    pressure_all,
    got,
    diag,
    source,
    send,
    x_out,
    trace_out,
    flux_out,
    message_out,
    gathered,
    part,
    tiles,
    arrived,
    pressure,
    here,
):
    mine, shard = at[0], at[1]
    per_row = cols.shape[0]
    fetch = pltpu.make_async_copy(tiles_all.at[pl.ds(per_row * mine, per_row)], tiles, arrived)
    fetch.start()
    groups = LANES // CAP
    for m in range(CAP):
        x_out[pl.ds(m, groups, stride=CAP), :] = got[
            pl.ds(2 * m * groups, groups, stride=2), :
        ]
    message = got[pl.ds(1, LANES, stride=2), :]
    message_out[...] = message
    trace = traces(message, pressure_all, pressure, here, gathered)
    kappa = kappa_of(message)
    flux = kappa * (trace - at_mortar(message, x_out[...]))
    load, weight = onto_fracture(message, flux, kappa)
    part[...] = load
    row = CAP * shard + mine
    x_row = x_out[pl.ds(row, 1), :]
    x_col = as_column(x_row)
    mixed = jnp.zeros((LANES, LANES), F32)
    fetch.wait()
    for t in range(per_row):
        tile = tiles[t]
        mixed += tile * x_out[pl.ds(cols[t, mine], 1), :]
        back = jnp.sum(tile * x_col, axis=0, keepdims=True)
        part[pl.ds(cols[t, mine], 1), :] -= 0.5 * back
    part[pl.ds(row, 1), :] += source[pl.ds(mine, 1), :] - (
        diag[pl.ds(mine, 1), :] * x_row + 0.5 * row_sums(mixed)
    )
    send[pl.ds(0, LANES, stride=2), :] = part[...]
    send[pl.ds(1, LANES, stride=2), :] = weight
    trace_out[...] = trace
    flux_out[...] = flux


def spread_flux(message, values, spread, cell_row, depth):
    flipped = message.T
    for k in range(CAP):
        z = by_slot(message, k)[1]
        placed = jnp.where(iota((LANES, depth), 1) == z, values[:, k : k + 1], 0.0)
        spread[k * LANES : (k + 1) * LANES, :] = halves(placed)
        cell_row[:, k * LANES : (k + 1) * LANES] = (
            flipped[X + k : X + k + 1, :] * 64 + flipped[Y + k : Y + k + 1, :]
        ).astype(jnp.int32)


def sources(rows, step, spread, cell_row):
    depth = spread.shape[1] // 2
    row = iota((rows, CAP * LANES), 0) + step * rows
    chosen = ones_where(row == cell_row[...])
    out = jnp.dot(chosen, spread[...], preferred_element_type=F32)
    return out[:, :depth] + out[:, depth:]


def second_traces(message, trace, gathered, trace_out, send):
    now = at_depth(message, gathered)
    trace_out[...] = now
    [change] = onto_fracture(message, kappa_of(message) * (now - trace))
    mats = CAP
    each = LANES // mats
    for m in range(mats):
        part = slice(m * each, (m + 1) * each)
        send[2 * m * each : (2 * m + 1) * each, :] = change[part, :]
        send[(2 * m + 1) * each : (2 * m + 2) * each, :] = now[part, :]


def home_body(got, owner, slot, frac, kappa, x, flux, *, mats):
    count = owner.shape[1]

    def found(values, chosen):
        top = values.astype(BF16).astype(F32)
        middle = (values - top).astype(BF16).astype(F32)
        parts = jnp.concatenate([top, middle, values - top - middle], axis=0)
        if parts.shape[0] % 16:
            parts = jnp.concatenate([parts, jnp.zeros_like(top)], axis=0)
        out = jnp.dot(parts.astype(BF16), chosen, preferred_element_type=F32)
        n = values.shape[0]
        return out[:n] + out[n : 2 * n] + out[2 * n : 3 * n]

    shards = LANES // mats
    own = owner[...]
    source = (own & (shards - 1)) * mats + own // shards
    traces_all = found(got[...].T[:CAP, :], ones_where(iota((LANES, count), 0) == source))
    here = iota((CAP, count), 0) == slot[...]
    trace = jnp.sum(jnp.where(here, traces_all, 0.0), axis=0, keepdims=True)
    f = frac[...]
    x_all = found(x[...].T, ones_where(iota((LANES, count), 0) == f >> 7))
    here = iota((LANES, count), 0) == (f & 127)
    x_there = jnp.sum(jnp.where(here, x_all, 0.0), axis=0, keepdims=True)
    flux[...] = kappa[...] * (trace - x_there)


def sum_body(got, send):
    for i in range(2):
        mine = jnp.sum(got[pl.ds(i, LANES, stride=2), :], axis=0, keepdims=True)
        send[pl.ds(i, LANES, stride=2), :] = jnp.broadcast_to(mine, (LANES, LANES))


def columns_body(got, chosen, *, shards, rows, tiles):
    flipped = got[pl.ds(1, LANES, stride=2), :].T[COLS : COLS + CAP, :]
    count = shards * rows * tiles
    tile = iota((LANES, count), 1)
    sender = (tile // tiles) % rows * shards + tile // (rows * tiles)
    moved = jnp.dot(
        jnp.concatenate([flipped, flipped], axis=0).astype(BF16),
        ones_where(iota((LANES, count), 0) == sender),
        preferred_element_type=F32,
    )[:CAP]
    here = iota((CAP, count), 0) == iota((CAP, count), 1) % tiles
    column = jnp.sum(jnp.where(here, moved, 0.0), axis=0, keepdims=True).astype(jnp.int32)
    chosen[...] = ones_where(iota((LANES, count), 0) == column)


def products(at, cols, d, tiles, diag, block):
    shard = at[1]
    per_row, rows = cols.shape
    for r in range(rows):
        d_row = d[pl.ds(CAP * shard + r, 1), :]
        d_col = as_column(d_row)
        mixed = jnp.zeros((LANES, LANES), F32)
        for t in range(per_row):
            tile = tiles[per_row * r + t]
            mixed += tile * d[pl.ds(cols[t, r], 1), :]
            back = jnp.sum(tile * d_col, axis=0, keepdims=True)
            block[rows + per_row * r + t : rows + per_row * r + t + 1, :] = 0.5 * back
        block[r : r + 1, :] = diag[r : r + 1, :] * d_row + 0.5 * row_sums(mixed)


def image_of(got, chosen, step, rows, tiles):
    shards = got.shape[0] // step
    own = jnp.concatenate([got[s * step : s * step + rows, :] for s in range(shards)], axis=0)
    back = jnp.concatenate(
        [got[s * step + rows : s * step + rows + tiles, :] for s in range(shards)], axis=0
    )
    return own + pick(chosen[...], back)


def start_body(at, cols, tiles, got, diag, r_out, weight_out, send, block):
    r_out[...] = got[pl.ds(0, LANES, stride=2), :]
    weight_out[...] = got[pl.ds(1, LANES, stride=2), :]
    products(at, cols, r_out, tiles, diag, block)
    size = block.shape[0]
    for s in range(send.shape[0] // size):
        send[s * size : (s + 1) * size, :] = block[...]


def step_body(
    at, cols, tiles, got, chosen, diag, *rest, ride, last, faces_in, faces_out
):
    per_row, rows = cols.shape
    size = rows * (1 + per_row)
    shards = LANES // rows
    mats = rows
    extra = list(rest)
    change = extra.pop(0) if ride == "reduce" else None
    parts = [extra.pop(0) for _ in range(mats // 2)] if ride == "next" else None
    x, r, d = (extra.pop(0) for _ in range(3))
    if ride == "next":
        parts.insert(0, extra.pop(0))
    x_before, weight = (extra.pop(0), extra.pop(0)) if ride == "next" else (None, None)
    y_faces = (extra.pop(0), extra.pop(0)) if faces_out else None
    x_out, r_out, d_out, send = (extra.pop(0) for _ in range(4))
    change_out, home = (extra.pop(0), extra.pop(0)) if ride == "gather" else (None, None)
    y_halo = (extra.pop(0), extra.pop(0)) if faces_in else None
    block = extra.pop()
    got_step = got.shape[0] // shards
    shard = at[1]
    image = image_of(got, chosen, got_step, rows, rows * per_row)
    old = d[...]
    norm = total(r[...] * r[...])
    alpha = norm / total(old * image)
    x_new = x[...] + alpha * old
    r_new = r[...] - alpha * image
    x_out[...] = x_new
    if ride == "next":
        [whole_change] = extra
        k = 0
        for part in parts:
            for i in range(part.shape[0] // shards):
                place = pl.multiple_of((at[0] ^ k) * shards, shards)
                whole_change[pl.ds(place, shards), :] = part[i * shards : (i + 1) * shards, :]
                k += 1
        r_new = r_new + whole_change[...] - weight[...] * (x_new - x_before[...])
        d_out[...] = r_new
    else:
        d_out[...] = r_new + (total(r_new * r_new) / norm) * old
    r_out[...] = r_new
    if last:
        lanes = jnp.zeros((1, LANES), F32)
        for i in range(rows):
            d_row = d_out[pl.ds(CAP * shard + i, 1), :]
            mixed = jnp.zeros((LANES, LANES), F32)
            for t in range(per_row):
                mixed += tiles[per_row * i + t] * d_out[pl.ds(cols[t, i], 1), :]
            lanes += diag[i : i + 1, :] * d_row * d_row
            lanes += jnp.sum(mixed * as_column(d_row), axis=0, keepdims=True)
        send[...] = jnp.broadcast_to(lanes, send.shape)
    else:
        products(at, cols, d_out, tiles, diag, block)
        send_step = send.shape[0] // shards
        if ride == "reduce":
            found = change[:shards, :]
            for m in range(1, mats):
                found = found + change[2 * m * shards : (2 * m + 1) * shards, :]
        for s in range(shards):
            first = s * send_step
            send[first : first + size, :] = block[...]
            first += size
            if ride == "reduce":
                send[first : first + shards, :] = found
                for m in range(mats):
                    row = (2 * m + 1) * shards + s
                    send[first + shards + m : first + shards + m + 1, :] = change[row : row + 1, :]
                first += shards + mats
            if faces_out:
                face = jnp.where(shard < s, y_faces[1][...], y_faces[0][...])
                deep = face.shape[0]
                send[first : first + deep, :] = face[:, :LANES]
                send[first + deep : first + 2 * deep, :] = face[:, LANES:]
    first = size
    if ride == "gather":
        found = jnp.zeros((shards, LANES), F32)
        for s in range(shards):
            row = s * got_step + size
            found += got[row : row + shards, :]
            home[s * mats : (s + 1) * mats, :] = got[row + shards : row + shards + mats, :]
        change_out[...] = found
        first += shards + mats
    if faces_in:
        deep = y_halo[0].shape[0]
        for halo, other, there in (
            (y_halo[0], jnp.maximum(shard - 1, 0), shard > 0),
            (y_halo[1], jnp.minimum(shard + 1, shards - 1), shard < shards - 1),
        ):
            row = pl.multiple_of(other * got_step + first, 8)
            for half in range(2):
                values = got[pl.ds(row + half * deep, deep), :]
                halo[:, half * LANES : (half + 1) * LANES] = jnp.where(there, values, 0.0)


def final_body(at, got, x, r, d, out):
    alpha = total(r[...] * r[...]) / total(got[...])
    here = pl.ds(pl.multiple_of(CAP * at[1], CAP), CAP)
    out[...] = x[here, :] + alpha * d[here, :]


def even(at, dim):
    return (at[dim] & 1) == 0


def edges_body(at, px0, px1, py0, py1, tx1, ty1, xa, xb, ya, yb):
    wide, deep = px0.shape[1], py0.shape[0]
    low, high = px0[0], px1[0]
    xa[:wide, :] = jnp.where(even(at, 0), high, low)
    xb[:wide, :] = jnp.where(even(at, 0), low, high)
    xa[wide:, :] = tx1[0, 0]
    xb[wide:, :] = tx1[0, 0]
    low, high = py0[:, 0, :], py1[:, 7, :]
    ya[:deep, :] = jnp.where(even(at, 1), high, low)
    yb[:deep, :] = jnp.where(even(at, 1), low, high)
    ya[deep:, :] = ty1[0, :, 7, :]
    yb[deep:, :] = ty1[0, :, 7, :]


def edges(at, pressure, trans):
    nx, ny, nz = pressure.shape
    y_last = ny // 8 - 1
    out = [(2 * ny, nz)] * 2 + [(2 * nx, nz)] * 2
    pressure, trans = in_hbm(pressure), in_hbm(trans)
    return pl.pallas_call(
        edges_body,
        grid=(1,),
        out_shape=tuple(sent(*v) for v in out),
        in_specs=[
            SMEM,
            pl.BlockSpec((1, ny, nz), lambda i: (0, 0, 0)),
            pl.BlockSpec((1, ny, nz), lambda i: (nx - 1, 0, 0)),
            pl.BlockSpec((nx, 8, nz), lambda i: (0, 0, 0)),
            pl.BlockSpec((nx, 8, nz), lambda i: (0, y_last, 0)),
            pl.BlockSpec((1, 1, ny, nz), lambda i: (0, nx - 1, 0, 0)),
            pl.BlockSpec((1, nx, 8, nz), lambda i: (1, 0, y_last, 0)),
        ],
        out_specs=tuple(pl.BlockSpec(v, lambda i: (0, 0)) for v in out),
        compiler_params=params(),
        name="edges",
    )(at, pressure, pressure, pressure, pressure, trans, trans)


def sweep_body(
    at,
    xa,
    xb,
    ya,
    yb,
    cxa,
    cxb,
    cya,
    cyb,
    p,
    p_after,
    trans,
    rhs,
    *rest,
    first,
    last,
    fluxes,
    gather,
    y_in,
    y_out,
):
    rest = list(rest)
    cell = rest.pop(0) if first else None
    weight = None if first else rest.pop(0)
    if fluxes or gather:
        got, values = rest.pop(0), [rest.pop(0) for _ in range(fluxes + gather)]
    out = rest.pop(0)
    weight_out = rest.pop(0) if first else None
    rhs_out = rest.pop(0) if fluxes else None
    trace_out, cuts = (rest.pop(0), rest.pop(0)) if gather else (None, None)
    gathered = rest.pop() if gather else None
    if fluxes:
        found, spread, cell_row = rest.pop(), rest.pop(), rest.pop()
    carry_t = rest.pop() if first else None
    carry = rest.pop()
    step = pl.program_id(0)
    steps = pl.num_programs(0)
    many, ny, nz = out.shape
    nx = ya.shape[0] if not first else ya.shape[0] // 2
    row = iota((ny, nz), 0)
    lane = iota((ny, nz), 1)
    x_even, y_even = even(at, 0), even(at, 1)

    @pl.when(step == 0)
    def _():
        if fluxes == 1:
            spread_flux(got[...], values[0][...], spread, cell_row, nz)
        if fluxes == 2:
            message = got[...]
            flux = values[0][...] - at_mortar(message, values[1][...])
            spread_flux(message, kappa_of(message) * flux, spread, cell_row, nz)
        tx_low = jnp.where(x_even, cxb[ny:, :], cxa[ny:, :])
        carry[...] = tx_low * jnp.where(x_even, xb[:ny, :], xa[:ny, :])
        if first:
            carry_t[...] = tx_low

    if fluxes:
        found[...] = sources(many * ny, step, spread, cell_row)
    for i in range(many):
        here_at = step * many + i
        right = rhs[i]
        if fluxes:
            right = right + found[i * ny : (i + 1) * ny, :]
            rhs_out[i] = right
        here = p[i]
        if i + 1 < many:
            after = p[i + 1]
        else:
            x_high = jnp.where(x_even, xa[:ny, :], xb[:ny, :])
            after = jnp.where(step + 1 < steps, p_after[0], x_high)
        one = pl.ds(here_at, 1)
        edge = pl.ds(nx + here_at, 1)
        y_low, y_high = ya[one, :], yb[one, :]
        if not y_in:
            y_low, y_high = jnp.where(y_even, y_high, y_low), jnp.where(y_even, y_low, y_high)
        ty_edge = jnp.where(y_even, cyb[edge, :], cya[edge, :])
        tx, ty, tz = trans[0, i], trans[1, i], trans[2, i]
        y_next = jnp.where(row == ny - 1, y_high, pltpu.roll(here, ny - 1, 0))
        y_prev = jnp.where(row == 0, ty_edge * y_low, pltpu.roll(ty * here, 1, 0))
        z_next = jnp.where(lane == nz - 1, 0.0, pltpu.roll(here, nz - 1, 1))
        z_prev = jnp.where(lane == 0, 0.0, pltpu.roll(tz * here, 1, 1))
        if first:
            ty_before = jnp.where(row == 0, ty_edge, pltpu.roll(ty, 1, 0))
            tz_before = jnp.where(lane == 0, 0.0, pltpu.roll(tz, 1, 1))
            diagonal = cell[i] + tx + carry_t[...] + ty + ty_before + tz + tz_before
            w = WEIGHT / diagonal
            weight_out[i] = w
            carry_t[...] = tx
        else:
            w = weight[i]
        around = (tx * after + carry[...]) + (ty * y_next + y_prev) + (tz * z_next + z_prev)
        carry[...] = tx * here
        out[i] = (1.0 - WEIGHT) * here + w * (right + around)
    if gather:
        message = got[...]
        rows = iota((LANES, many * ny), 1) + step * (many * ny)
        chosen = jnp.concatenate(
            [ones_where(rows == by_slot(message, k)[0]) for k in range(CAP)], axis=0
        )
        planes = jnp.concatenate([out[i] for i in range(many)], axis=0)
        found = pick_rounded(chosen, planes)

        @pl.when(step == 0)
        def _():
            gathered[...] = found

        @pl.when(step > 0)
        def _():
            gathered[...] += found

        @pl.when(step == steps - 1)
        def _():
            second_traces(message, values[0][...], gathered, trace_out, cuts)

    if last:
        return
    xa_out, xb_out, ya_out, yb_out = rest
    start, end = step == 0, step == steps - 1

    @pl.when(start & x_even)
    def _():
        xb_out[...] = out[0]

    @pl.when(start & ~x_even)
    def _():
        xa_out[...] = out[0]

    @pl.when(end & x_even)
    def _():
        xa_out[...] = out[many - 1]

    @pl.when(end & ~x_even)
    def _():
        xb_out[...] = out[many - 1]

    for i in range(many):
        one = pl.ds(step * many + i, 1)
        low, high = out[i, :1, :], out[i, ny - 1 :, :]
        if not y_out:
            low, high = jnp.where(y_even, high, low), jnp.where(y_even, low, high)
        ya_out[one, :] = low
        yb_out[one, :] = high


def sweep(
    at,
    p,
    halo,
    faces,
    trans,
    rhs,
    cell=None,
    weight=None,
    last=False,
    got=None,
    values=(),
    gather=False,
    y_in=False,
    y_out=False,
    many=4,
):
    nx, ny, nz = p.shape
    part = pl.BlockSpec((many, ny, nz), lambda i: (i, 0, 0))
    x_face = pl.BlockSpec((ny, nz), lambda i: (0, 0))
    y_face = pl.BlockSpec((nx, nz), lambda i: (0, 0))
    first = weight is None
    out_shape, out_specs = [shape(nx, ny, nz)], [part]
    if first:
        out_shape.append(shape(nx, ny, nz))
        out_specs.append(part)
    scratch = [pltpu.VMEM((ny, nz), F32)] * (2 if first else 1)
    if gather:
        out_shape += [sent(LANES, LANES), sent(2 * LANES, LANES)]
        out_specs += [whole((LANES, LANES)), whole((2 * LANES, LANES))]
        scratch.append(pltpu.VMEM((CAP * LANES, nz), F32))
    elif values:
        out_shape.append(shape(nx, ny, nz))
        out_specs.append(part)
        scratch += [
            pltpu.VMEM((1, CAP * LANES), jnp.int32),
            pltpu.VMEM((CAP * LANES, 2 * nz), BF16),
            pltpu.VMEM((many * ny, nz), F32),
        ]
    if not last:
        out_shape += [sent(ny, nz)] * 2 + [sent(nx, nz)] * 2
        out_specs += [x_face, x_face, y_face, y_face]
    after = pl.BlockSpec(
        (1, ny, nz), lambda i: (jnp.minimum((i + 1) * many, nx - 1), 0, 0)
    )
    if y_in:
        halo = (*halo[:2], *(in_hbm(v, 1) for v in halo[2:]))
    operands = [*halo, *faces, p, p, trans, rhs, cell if first else weight]
    operands += [in_hbm(v, 1) for v in (got, *values)] if values else []
    return pl.pallas_call(
        functools.partial(
            sweep_body,
            first=first,
            last=last,
            fluxes=0 if gather else len(values),
            gather=gather,
            y_in=y_in,
            y_out=y_out,
        ),
        grid=(nx // many,),
        out_shape=tuple(out_shape),
        in_specs=[SMEM]
        + [whole(v.shape) for v in (*halo, *faces)]
        + [part, after]
        + [pl.BlockSpec((3, many, ny, nz), lambda i: (0, i, 0, 0)), part, part]
        + ([whole(v.shape) for v in (got, *values)] if values else []),
        out_specs=tuple(out_specs),
        scratch_shapes=scratch,
        compiler_params=params(),
        cost_estimate=pl.CostEstimate(flops=6_000_000, bytes_accessed=8 << 20, transcendentals=0),
        name="sweep",
    )(at, *(in_hbm(v) for v in operands))


def swap(v, axis, count, low):
    pairs = [(i, i + 1) for i in range(low, count - 1, 2)]
    return lax.ppermute(v, axis, pairs + [(b, a) for a, b in pairs])


def swapped(xa, xb, ya, yb, mats, shards):
    return (
        swap(xa, "mat", mats, 0),
        swap(xb, "mat", mats, 1),
        swap(ya, "frac", shards, 0),
        swap(yb, "frac", shards, 1),
    )


def body(
    pressure_start,
    face_trans,
    cell_coef,
    matrix_source,
    mortar_owner,
    mortar_cell,
    mortar_frac,
    mortar_kappa,
    tiles,
    tile_cols,
    frac_diag,
    frac_source,
    fracture_start,
):
    nx, ny, nz = pressure_start.shape
    mats, shards = lax.axis_size("mat"), lax.axis_size("frac")
    rows, per_row = tile_cols.shape
    count = mortar_cell.shape[0]
    size = rows * (1 + per_row)
    at = jnp.stack([lax.axis_index("mat"), lax.axis_index("frac")]).astype(jnp.int32)
    everyone = functools.partial(
        lax.all_to_all, axis_name=("mat", "frac"), split_axis=0, concat_axis=0, tiled=True
    )
    over_frac = functools.partial(
        lax.all_to_all, axis_name="frac", split_axis=0, concat_axis=0, tiled=True
    )
    over_mat = functools.partial(
        lax.all_to_all, axis_name="mat", split_axis=0, concat_axis=0, tiled=True
    )
    square = shape(LANES, LANES)
    owner = mortar_owner.reshape(1, count)
    frac, kappa = mortar_frac.reshape(1, count), mortar_kappa.reshape(1, count)
    flat = (nx * ny, nz)
    tile_list = tiles.reshape(rows * per_row, LANES, LANES)
    diag = frac_diag.reshape(rows, LANES)
    square_scratch = pltpu.VMEM((LANES, LANES), F32)
    gathered = pltpu.VMEM((CAP * LANES, nz), F32)
    block = pltpu.VMEM((size, LANES), F32)
    scalars = (at, tile_cols.T)
    fetch_scratch = [pltpu.VMEM(flat, F32), pltpu.SemaphoreType.DMA((8,))]

    send, slot = call(
        pack_body,
        (sent(2 * LANES, LANES), pltpu.HBM((1, count), jnp.int32)),
        owner,
        mortar_cell.reshape(1, count),
        frac,
        kappa,
        fracture_start.reshape(rows, LANES),
        scalars=scalars,
        scratch=[square_scratch],
        name="pack",
        least=1,
    )
    send, edges_at = lax.optimization_barrier((send, at))
    got = everyone(send)

    faces = swapped(*edges(edges_at, pressure_start, face_trans), mats, shards)

    send, x_start, trace, flux, message = call(
        first_body,
        (sent(2 * LANES, LANES), *[sent(LANES, LANES)] * 4),
        got,
        diag,
        frac_source.reshape(rows, LANES),
        scalars=scalars,
        raw=(tile_list, pressure_start.reshape(flat)),
        scratch=[
            gathered,
            square_scratch,
            pltpu.VMEM((per_row, LANES, LANES), F32),
            pltpu.SemaphoreType.DMA(()),
            *fetch_scratch,
        ],
        flops=2e9,
        name="first",
    )
    send, *faces = lax.optimization_barrier((send, *faces))
    reduced = everyone(send)
    pressure, weight, rhs, *sides = sweep(
        at, pressure_start, faces, faces, face_trans, matrix_source, cell_coef, got=message, values=(flux,)
    )
    sides = swapped(*sides, mats, shards)

    send = call(sum_body, sent(2 * LANES, LANES), reduced, name="sums")
    send, pressure = lax.optimization_barrier((send, pressure))
    residuals = everyone(send)
    chosen = call(
        functools.partial(columns_body, shards=shards, rows=rows, tiles=per_row),
        shape(LANES, shards * rows * per_row, dtype=BF16),
        got,
        name="columns",
    )
    r, sums, send = call(
        start_body,
        (*[sent(LANES, LANES)] * 2, sent(shards * size, LANES)),
        residuals,
        diag,
        scalars=scalars,
        resident=(tile_list,),
        scratch=[block],
        name="start",
    )
    x, d = x_start, r
    send, pressure, *sides = lax.optimization_barrier((send, pressure, *sides))
    arrived = over_frac(send)
    pressure, trace, change, *sides = sweep(
        at,
        pressure,
        sides,
        faces,
        face_trans,
        rhs,
        weight=weight,
        got=message,
        values=(trace,),
        gather=True,
        y_out=True,
    )

    arrived, change = lax.optimization_barrier((arrived, change))
    change = over_mat(change)
    arrived, change = lax.optimization_barrier((arrived, change))

    def step(arrived, x, r, d, *more, ride=None, last=False, faces_in=False, faces=(), side=()):
        length = size + (shards + mats if ride == "reduce" else 0) + (2 * nx if faces else 0)
        outs = [*[sent(LANES, LANES)] * 3, sent(shards * (1 if last else length), LANES)]
        if ride == "gather":
            outs += [sent(shards, LANES), sent(LANES, LANES)]
        if faces_in:
            outs += [sent(nx, nz)] * 2
        return call(
            functools.partial(
                step_body, ride=ride, last=last, faces_in=faces_in, faces_out=bool(faces)
            ),
            tuple(outs),
            arrived,
            chosen,
            diag,
            *more,
            side=(x, r, d, *side, *faces),
            scalars=scalars,
            resident=(tile_list,),
            scratch=([square_scratch] if ride == "next" else []) + [block],
            name="step",
        )

    def swapped_mat(xa, xb):
        return swap(xa, "mat", mats, 0), swap(xb, "mat", mats, 1)

    x, r, d, send = step(arrived, x, r, d, change, ride="reduce")
    send, trace, *x_sides = lax.optimization_barrier((send, trace, *sides[:2]))
    arrived = over_frac(send)
    x_sides = swapped_mat(*x_sides)
    arrived, *x_sides = lax.optimization_barrier((arrived, *x_sides))

    x, r, d, send, change, home = step(arrived, x, r, d, ride="gather", faces=sides[2:])
    arrived = over_frac(send)
    parts = [change, lax.ppermute(change, "mat", [(i, i ^ 1) for i in range(mats)])]
    pair = jnp.concatenate(parts, axis=0)
    for hop in range(2, mats, 2):
        parts.append(lax.ppermute(pair, "mat", [(i, i ^ hop) for i in range(mats)]))

    x, r, d, send, *y_sides = step(
        arrived, x, r, d, *parts[1:], faces_in=True, ride="next", side=(change, x_start, sums)
    )
    x_flux = x
    arrived = over_frac(send)
    pressure, rhs, *sides = sweep(
        at,
        pressure,
        (*x_sides, *y_sides),
        faces,
        face_trans,
        matrix_source,
        weight=weight,
        got=message,
        values=(trace, x_flux),
        y_in=True,
        y_out=True,
    )
    arrived, pressure, *sides = lax.optimization_barrier((arrived, pressure, *sides))
    x, r, d, send = step(arrived, x, r, d, faces=sides[2:])
    send, home, *sides = lax.optimization_barrier((send, home, *sides[:2]))
    arrived = over_frac(send)
    x_sides = swapped_mat(*sides)
    flux = call(
        functools.partial(home_body, mats=mats),
        shape(1, count),
        side=(home, owner, slot, frac, kappa, x_flux),
        name="home",
    )
    arrived, flux, *x_sides = lax.optimization_barrier((arrived, flux, *x_sides))
    x, r, d, send, *y_sides = step(arrived, x, r, d, last=True, faces_in=True)
    send, pressure, flux = lax.optimization_barrier((send, pressure, flux))
    arrived = over_frac(send)
    [pressure] = sweep(
        at,
        pressure,
        (*x_sides, *y_sides),
        faces,
        face_trans,
        rhs,
        weight=weight,
        last=True,
        y_in=True,
    )
    fracture = call(
        final_body, shape(rows, LANES), arrived, side=(x, r, d), scalars=(at,), name="final"
    )
    return pressure, fracture.reshape(rows * LANES), flux.reshape(count)


def solution(mesh):
    in_specs = (
        P("mat", "frac", None),
        P(None, "mat", "frac", None),
        P("mat", "frac", None),
        P("mat", "frac", None),
        P(("mat", "frac"), None),
        P(("mat", "frac")),
        P(("mat", "frac")),
        P(("mat", "frac")),
        P("frac", None, None, None),
        P("frac", None),
        P("frac"),
        P("frac"),
        P("frac"),
    )
    out_specs = (P("mat", "frac", None), P("frac"), P(("mat", "frac")))
    return jax.shard_map(body, mesh=mesh, in_specs=in_specs, out_specs=out_specs, check_vma=False)
```

```python
import functools
import math

import jax
import jax.numpy as jnp
from jax import lax
from jax.experimental import pallas as pl
from jax.experimental.pallas import tpu as pltpu
from jax.sharding import PartitionSpec as P

WEIGHT = 0.8
CAP = 8
LANES = 128
LARGE = 1 << 18
F32 = jnp.float32
BF16 = jnp.bfloat16
SMEM = pl.BlockSpec(memory_space=pltpu.SMEM)
VMEM = pl.BlockSpec(memory_space=pltpu.VMEM)
RAW = pl.BlockSpec(memory_space=pltpu.HBM)
X, Y, Z, HI, LO, KAPPA, COLS = (CAP * i for i in range(7))


def shape(*dims, dtype=F32):
    if math.prod(dims) >= LARGE:
        return pltpu.HBM(dims, dtype)
    return jax.ShapeDtypeStruct(dims, dtype)


def sent(*dims):
    return pltpu.HBM(dims, F32)


def in_hbm(x, least=LARGE):
    if x.size < least:
        return x
    return pltpu.with_memory_space_constraint(x, pltpu.HBM)


def on_chip(v):
    return isinstance(v, jax.ShapeDtypeStruct) and math.prod(v.shape) < LARGE


def whole(dims):
    return pl.BlockSpec(dims, lambda i: (0,) * len(dims), pipeline_mode=pl.Buffered(1))


def params():
    return pltpu.CompilerParams(vmem_limit_bytes=32 << 20)


def call(
    body, outs, *operands, scalars=(), raw=(), resident=(), side=(), scratch=(), flops=1e6, nbytes=1e6, name=None, least=LARGE
):
    single = not isinstance(outs, tuple)
    outs = (outs,) if single else outs
    result = pl.pallas_call(
        body,
        grid=(1,),
        out_shape=outs,
        in_specs=[SMEM] * len(scalars) + [RAW] * len(raw) + [VMEM] * len(resident) + [VMEM if v.size < least else whole(v.shape) for v in operands]
        + [whole(v.shape) for v in side],
        out_specs=tuple(
            VMEM if on_chip(v) else pl.BlockSpec(v.shape, lambda i, n=len(v.shape): (0,) * n)
            for v in outs
        ),
        scratch_shapes=scratch,
        compiler_params=params(),
        cost_estimate=pl.CostEstimate(
            flops=int(flops), bytes_accessed=int(nbytes), transcendentals=0
        ),
        name=name,
    )(
        *scalars,
        *(in_hbm(v, least) for v in raw),
        *resident,
        *(in_hbm(v, least) for v in operands),
        *(in_hbm(v, 1) for v in side),
    )
    return result[0] if single else result


def iota(dims, dim):
    return lax.broadcasted_iota(jnp.int32, dims, dim)


def ones_where(mask):
    return jnp.where(mask, 1.0, 0.0).astype(BF16)


def halves(v):
    top = v.astype(BF16)
    return jnp.concatenate([top, (v - top.astype(F32)).astype(BF16)], axis=1)


def pick_rounded(chosen, v):
    width = v.shape[1]
    out = jnp.dot(chosen, halves(v), preferred_element_type=F32)
    return out[:, :width] + out[:, width:]


def split(v):
    top = v.astype(BF16)
    rest = v - top.astype(F32)
    middle = rest.astype(BF16)
    low = (rest - middle.astype(F32)).astype(BF16)
    return jnp.concatenate([top, middle, low], axis=1)


def pick(chosen, v):
    width = v.shape[1]
    out = jnp.dot(chosen, split(v), preferred_element_type=F32)
    return out[:, :width] + out[:, width : 2 * width] + out[:, 2 * width :]


def total(v):
    return jnp.sum(jnp.sum(v, axis=1, keepdims=True), axis=0, keepdims=True)


def row_sums(v):
    return jnp.sum(v.T, axis=0, keepdims=True)


def as_column(row):
    return jnp.broadcast_to(row, (LANES, LANES)).T


def pack_body(at, cols, owner, cell, frac, kappa, x_own, send, slot_out, blocks):
    count = owner.shape[1]
    mine = at[0]
    own = owner[...]
    slot = jnp.zeros((1, count), jnp.int32)
    for first in range(0, count, LANES):
        column = jnp.broadcast_to(own[:, first : first + LANES], (LANES, LANES)).T
        column = jnp.concatenate([column] * (count // LANES), axis=1)
        before = iota((LANES, count), 0) + first < iota((LANES, count), 1)
        slot += jnp.sum(jnp.where((column == own) & before, 1, 0), axis=0, keepdims=True)
    slot_out[...] = slot
    here = iota((CAP, count), 0) == slot
    c, f = cell[...], frac[...]
    k = kappa[...]
    top = k.astype(BF16).astype(F32)
    middle = (k - top).astype(BF16).astype(F32)
    low = k - top - middle
    whole = [c >> 14, (c >> 8) & 63, c & 255, f >> 7, f & 127]
    rows = [jnp.where(here, v.astype(F32), 0.0) for v in whole]
    rows = jnp.concatenate([*rows, jnp.where(here, top, 0.0), jnp.zeros((LANES - 6 * CAP, count), F32)], axis=0)
    chosen = ones_where(iota((LANES, count), 0) == own)
    nt = functools.partial(
        lax.dot_general,
        dimension_numbers=(((1,), (1,)), ((), ())),
        preferred_element_type=F32,
    )

    def kappas(v):
        return jnp.concatenate(
            [
                jnp.zeros((KAPPA, count), F32),
                jnp.where(here, v, 0.0),
                jnp.zeros((LANES - 6 * CAP, count), F32),
            ],
            axis=0,
        ).astype(BF16)

    message = nt(chosen, rows.astype(BF16)) + nt(chosen, kappas(middle)) + nt(chosen, kappas(low))
    lane = iota((1, LANES), 1)
    extra = jnp.zeros((1, LANES), F32)
    for t in range(cols.shape[0]):
        column = jnp.where(iota((1, cols.shape[1]), 1) == mine, cols[t : t + 1, :], 0)
        column = jnp.sum(column, axis=1, keepdims=True).astype(F32)
        extra = jnp.where(lane == COLS + t, column, extra)
    blocks[...] = jnp.broadcast_to(x_own[pl.ds(mine, 1), :], (LANES, LANES))
    send[pl.ds(0, LANES, stride=2), :] = blocks[...]
    send[pl.ds(1, LANES, stride=2), :] = message + extra


def by_slot(message, k):
    x = message[:, X + k : X + k + 1].astype(jnp.int32)
    y = message[:, Y + k : Y + k + 1].astype(jnp.int32)
    z = message[:, Z + k : Z + k + 1].astype(jnp.int32)
    hi = message[:, HI + k : HI + k + 1].astype(jnp.int32)
    lo = message[:, LO + k : LO + k + 1].astype(jnp.int32)
    return x * 64 + y, z, hi, lo, message[:, KAPPA + k : KAPPA + k + 1]


def in_parts(source, target, arrived):
    parts = arrived.shape[0]
    each = source.shape[0] // parts
    copies = []
    for i in range(parts):
        part = pl.ds(i * each, each)
        copies.append(
            pltpu.make_async_copy(source.at[part], target.at[part], arrived.at[i])
        )
        copies[-1].start()
    return copies


def traces(message, pressure_all, pressure, here, gathered):
    copies = in_parts(pressure_all, pressure, here)
    rows, depth = pressure.shape
    chosen = jnp.concatenate(
        [ones_where(iota((LANES, rows), 1) == by_slot(message, k)[0]) for k in range(CAP)], axis=0
    )
    for copy in copies:
        copy.wait()
    gathered[...] = pick_rounded(chosen, pressure[...])
    return at_depth(message, gathered)


def at_depth(message, gathered):
    depth = gathered.shape[1]
    lane = iota((LANES, LANES), 1)
    out = jnp.zeros((LANES, LANES), F32)
    for k in range(CAP):
        z = by_slot(message, k)[1]
        part = gathered[k * LANES : (k + 1) * LANES, :]
        value = jnp.sum(jnp.where(iota((LANES, depth), 1) == z, part, 0.0), axis=1, keepdims=True)
        out = jnp.where(lane == k, value, out)
    return out


def at_mortar(message, x):
    chosen = jnp.concatenate(
        [ones_where(iota((LANES, LANES), 1) == by_slot(message, k)[2]) for k in range(CAP)], axis=0
    )
    found = pick(chosen, x)
    lane = iota((LANES, LANES), 1)
    out = jnp.zeros((LANES, LANES), F32)
    for k in range(CAP):
        part = found[k * LANES : (k + 1) * LANES, :]
        value = jnp.sum(jnp.where(lane == by_slot(message, k)[3], part, 0.0), axis=1, keepdims=True)
        out = jnp.where(lane == k, value, out)
    return out


def onto_fracture(message, *values):
    flipped = message.T
    hi = jnp.concatenate([flipped[HI + k : HI + k + 1, :] for k in range(CAP)], axis=1)
    chosen = ones_where(iota((LANES, CAP * LANES), 0) == hi.astype(jnp.int32))
    lane = iota((LANES, LANES), 1)
    wide = []
    for v in values:
        spread = [
            jnp.where(lane == by_slot(message, k)[3], v[:, k : k + 1], 0.0) for k in range(CAP)
        ]
        wide.append(jnp.concatenate(spread, axis=0))
    return [pick(chosen, v) for v in wide]


def kappa_of(message):
    lane = iota((LANES, LANES), 1)
    out = jnp.zeros((LANES, LANES), F32)
    for k in range(CAP):
        out = jnp.where(lane == k, message[:, KAPPA + k : KAPPA + k + 1], out)
    return out


def first_body(
    at,
    cols,
    tiles_all,
    pressure_all,
    got,
    diag,
    source,
    send,
    x_out,
    trace_out,
    flux_out,
    message_out,
    gathered,
    part,
    tiles,
    arrived,
    pressure,
    here,
):
    mine, shard = at[0], at[1]
    per_row = cols.shape[0]
    fetch = pltpu.make_async_copy(tiles_all.at[pl.ds(per_row * mine, per_row)], tiles, arrived)
    fetch.start()
    groups = LANES // CAP
    for m in range(CAP):
        x_out[pl.ds(m, groups, stride=CAP), :] = got[
            pl.ds(2 * m * groups, groups, stride=2), :
        ]
    message = got[pl.ds(1, LANES, stride=2), :]
    message_out[...] = message
    trace = traces(message, pressure_all, pressure, here, gathered)
    kappa = kappa_of(message)
    flux = kappa * (trace - at_mortar(message, x_out[...]))
    load, weight = onto_fracture(message, flux, kappa)
    part[...] = load
    row = CAP * shard + mine
    x_row = x_out[pl.ds(row, 1), :]
    x_col = as_column(x_row)
    mixed = jnp.zeros((LANES, LANES), F32)
    fetch.wait()
    for t in range(per_row):
        tile = tiles[t]
        mixed += tile * x_out[pl.ds(cols[t, mine], 1), :]
        back = jnp.sum(tile * x_col, axis=0, keepdims=True)
        part[pl.ds(cols[t, mine], 1), :] -= 0.5 * back
    part[pl.ds(row, 1), :] += source[pl.ds(mine, 1), :] - (
        diag[pl.ds(mine, 1), :] * x_row + 0.5 * row_sums(mixed)
    )
    send[pl.ds(0, LANES, stride=2), :] = part[...]
    send[pl.ds(1, LANES, stride=2), :] = weight
    trace_out[...] = trace
    flux_out[...] = flux


def spread_flux(message, values, spread, cell_row, depth):
    flipped = message.T
    for k in range(CAP):
        z = by_slot(message, k)[1]
        placed = jnp.where(iota((LANES, depth), 1) == z, values[:, k : k + 1], 0.0)
        spread[k * LANES : (k + 1) * LANES, :] = halves(placed)
        cell_row[:, k * LANES : (k + 1) * LANES] = (
            flipped[X + k : X + k + 1, :] * 64 + flipped[Y + k : Y + k + 1, :]
        ).astype(jnp.int32)


def sources(rows, step, spread, cell_row):
    depth = spread.shape[1] // 2
    row = iota((rows, CAP * LANES), 0) + step * rows
    chosen = ones_where(row == cell_row[...])
    out = jnp.dot(chosen, spread[...], preferred_element_type=F32)
    return out[:, :depth] + out[:, depth:]


def second_traces(message, trace, gathered, trace_out, send):
    now = at_depth(message, gathered)
    trace_out[...] = now
    [change] = onto_fracture(message, kappa_of(message) * (now - trace))
    mats = CAP
    each = LANES // mats
    for m in range(mats):
        part = slice(m * each, (m + 1) * each)
        send[2 * m * each : (2 * m + 1) * each, :] = change[part, :]
        send[(2 * m + 1) * each : (2 * m + 2) * each, :] = now[part, :]


def home_body(got, owner, slot, frac, kappa, x, flux, *, mats):
    count = owner.shape[1]

    def found(values, chosen):
        top = values.astype(BF16).astype(F32)
        middle = (values - top).astype(BF16).astype(F32)
        parts = jnp.concatenate([top, middle, values - top - middle], axis=0)
        if parts.shape[0] % 16:
            parts = jnp.concatenate([parts, jnp.zeros_like(top)], axis=0)
        out = jnp.dot(parts.astype(BF16), chosen, preferred_element_type=F32)
        n = values.shape[0]
        return out[:n] + out[n : 2 * n] + out[2 * n : 3 * n]

    shards = LANES // mats
    own = owner[...]
    source = (own & (shards - 1)) * mats + own // shards
    traces_all = found(got[...].T[:CAP, :], ones_where(iota((LANES, count), 0) == source))
    here = iota((CAP, count), 0) == slot[...]
    trace = jnp.sum(jnp.where(here, traces_all, 0.0), axis=0, keepdims=True)
    f = frac[...]
    x_all = found(x[...].T, ones_where(iota((LANES, count), 0) == f >> 7))
    here = iota((LANES, count), 0) == (f & 127)
    x_there = jnp.sum(jnp.where(here, x_all, 0.0), axis=0, keepdims=True)
    flux[...] = kappa[...] * (trace - x_there)


def sum_body(got, send):
    for i in range(2):
        mine = jnp.sum(got[pl.ds(i, LANES, stride=2), :], axis=0, keepdims=True)
        send[pl.ds(i, LANES, stride=2), :] = jnp.broadcast_to(mine, (LANES, LANES))


def columns_body(got, chosen, *, shards, rows, tiles):
    flipped = got[pl.ds(1, LANES, stride=2), :].T[COLS : COLS + CAP, :]
    count = shards * rows * tiles
    tile = iota((LANES, count), 1)
    sender = (tile // tiles) % rows * shards + tile // (rows * tiles)
    moved = jnp.dot(
        jnp.concatenate([flipped, flipped], axis=0).astype(BF16),
        ones_where(iota((LANES, count), 0) == sender),
        preferred_element_type=F32,
    )[:CAP]
    here = iota((CAP, count), 0) == iota((CAP, count), 1) % tiles
    column = jnp.sum(jnp.where(here, moved, 0.0), axis=0, keepdims=True).astype(jnp.int32)
    chosen[...] = ones_where(iota((LANES, count), 0) == column)


def products(at, cols, d, tiles, diag, block):
    shard = at[1]
    per_row, rows = cols.shape
    for r in range(rows):
        d_row = d[pl.ds(CAP * shard + r, 1), :]
        d_col = as_column(d_row)
        mixed = jnp.zeros((LANES, LANES), F32)
        for t in range(per_row):
            tile = tiles[per_row * r + t]
            mixed += tile * d[pl.ds(cols[t, r], 1), :]
            back = jnp.sum(tile * d_col, axis=0, keepdims=True)
            block[rows + per_row * r + t : rows + per_row * r + t + 1, :] = 0.5 * back
        block[r : r + 1, :] = diag[r : r + 1, :] * d_row + 0.5 * row_sums(mixed)


def image_of(got, chosen, step, rows, tiles):
    shards = got.shape[0] // step
    own = jnp.concatenate([got[s * step : s * step + rows, :] for s in range(shards)], axis=0)
    back = jnp.concatenate(
        [got[s * step + rows : s * step + rows + tiles, :] for s in range(shards)], axis=0
    )
    return own + pick(chosen[...], back)


def start_body(at, cols, tiles, got, diag, r_out, weight_out, send, block):
    r_out[...] = got[pl.ds(0, LANES, stride=2), :]
    weight_out[...] = got[pl.ds(1, LANES, stride=2), :]
    products(at, cols, r_out, tiles, diag, block)
    size = block.shape[0]
    for s in range(send.shape[0] // size):
        send[s * size : (s + 1) * size, :] = block[...]


def step_body(
    at, cols, tiles, got, chosen, diag, *rest, ride, last, faces_in, faces_out
):
    per_row, rows = cols.shape
    size = rows * (1 + per_row)
    shards = LANES // rows
    mats = rows
    extra = list(rest)
    change = extra.pop(0) if ride == "reduce" else None
    parts = [extra.pop(0) for _ in range(mats // 2)] if ride == "next" else None
    x, r, d = (extra.pop(0) for _ in range(3))
    if ride == "next":
        parts.insert(0, extra.pop(0))
    x_before, weight = (extra.pop(0), extra.pop(0)) if ride == "next" else (None, None)
    y_faces = (extra.pop(0), extra.pop(0)) if faces_out else None
    x_out, r_out, d_out, send = (extra.pop(0) for _ in range(4))
    change_out, home = (extra.pop(0), extra.pop(0)) if ride == "gather" else (None, None)
    y_halo = (extra.pop(0), extra.pop(0)) if faces_in else None
    block = extra.pop()
    got_step = got.shape[0] // shards
    shard = at[1]
    image = image_of(got, chosen, got_step, rows, rows * per_row)
    old = d[...]
    norm = total(r[...] * r[...])
    alpha = norm / total(old * image)
    x_new = x[...] + alpha * old
    r_new = r[...] - alpha * image
    x_out[...] = x_new
    if ride == "next":
        [whole_change] = extra
        k = 0
        for part in parts:
            for i in range(part.shape[0] // shards):
                place = pl.multiple_of((at[0] ^ k) * shards, shards)
                whole_change[pl.ds(place, shards), :] = part[i * shards : (i + 1) * shards, :]
                k += 1
        r_new = r_new + whole_change[...] - weight[...] * (x_new - x_before[...])
        d_out[...] = r_new
    else:
        d_out[...] = r_new + (total(r_new * r_new) / norm) * old
    r_out[...] = r_new
    if last:
        lanes = jnp.zeros((1, LANES), F32)
        for i in range(rows):
            d_row = d_out[pl.ds(CAP * shard + i, 1), :]
            mixed = jnp.zeros((LANES, LANES), F32)
            for t in range(per_row):
                mixed += tiles[per_row * i + t] * d_out[pl.ds(cols[t, i], 1), :]
            lanes += diag[i : i + 1, :] * d_row * d_row
            lanes += jnp.sum(mixed * as_column(d_row), axis=0, keepdims=True)
        send[...] = jnp.broadcast_to(lanes, send.shape)
    else:
        products(at, cols, d_out, tiles, diag, block)
        send_step = send.shape[0] // shards
        if ride == "reduce":
            found = change[:shards, :]
            for m in range(1, mats):
                found = found + change[2 * m * shards : (2 * m + 1) * shards, :]
        for s in range(shards):
            first = s * send_step
            send[first : first + size, :] = block[...]
            first += size
            if ride == "reduce":
                send[first : first + shards, :] = found
                for m in range(mats):
                    row = (2 * m + 1) * shards + s
                    send[first + shards + m : first + shards + m + 1, :] = change[row : row + 1, :]
                first += shards + mats
            if faces_out:
                face = jnp.where(shard < s, y_faces[1][...], y_faces[0][...])
                deep = face.shape[0]
                send[first : first + deep, :] = face[:, :LANES]
                send[first + deep : first + 2 * deep, :] = face[:, LANES:]
    first = size
    if ride == "gather":
        found = jnp.zeros((shards, LANES), F32)
        for s in range(shards):
            row = s * got_step + size
            found += got[row : row + shards, :]
            home[s * mats : (s + 1) * mats, :] = got[row + shards : row + shards + mats, :]
        change_out[...] = found
        first += shards + mats
    if faces_in:
        deep = y_halo[0].shape[0]
        for halo, other, there in (
            (y_halo[0], jnp.maximum(shard - 1, 0), shard > 0),
            (y_halo[1], jnp.minimum(shard + 1, shards - 1), shard < shards - 1),
        ):
            row = pl.multiple_of(other * got_step + first, 8)
            for half in range(2):
                values = got[pl.ds(row + half * deep, deep), :]
                halo[:, half * LANES : (half + 1) * LANES] = jnp.where(there, values, 0.0)


def final_body(at, got, x, r, d, out):
    alpha = total(r[...] * r[...]) / total(got[...])
    here = pl.ds(pl.multiple_of(CAP * at[1], CAP), CAP)
    out[...] = x[here, :] + alpha * d[here, :]


def even(at, dim):
    return (at[dim] & 1) == 0


def edges_body(at, px0, px1, py0, py1, tx1, ty1, xa, xb, ya, yb):
    wide, deep = px0.shape[1], py0.shape[0]
    low, high = px0[0], px1[0]
    xa[:wide, :] = jnp.where(even(at, 0), high, low)
    xb[:wide, :] = jnp.where(even(at, 0), low, high)
    xa[wide:, :] = tx1[0, 0]
    xb[wide:, :] = tx1[0, 0]
    low, high = py0[:, 0, :], py1[:, 7, :]
    ya[:deep, :] = jnp.where(even(at, 1), high, low)
    yb[:deep, :] = jnp.where(even(at, 1), low, high)
    ya[deep:, :] = ty1[0, :, 7, :]
    yb[deep:, :] = ty1[0, :, 7, :]


def edges(at, pressure, trans):
    nx, ny, nz = pressure.shape
    y_last = ny // 8 - 1
    out = [(2 * ny, nz)] * 2 + [(2 * nx, nz)] * 2
    pressure, trans = in_hbm(pressure), in_hbm(trans)
    return pl.pallas_call(
        edges_body,
        grid=(1,),
        out_shape=tuple(sent(*v) for v in out),
        in_specs=[
            SMEM,
            pl.BlockSpec((1, ny, nz), lambda i: (0, 0, 0)),
            pl.BlockSpec((1, ny, nz), lambda i: (nx - 1, 0, 0)),
            pl.BlockSpec((nx, 8, nz), lambda i: (0, 0, 0)),
            pl.BlockSpec((nx, 8, nz), lambda i: (0, y_last, 0)),
            pl.BlockSpec((1, 1, ny, nz), lambda i: (0, nx - 1, 0, 0)),
            pl.BlockSpec((1, nx, 8, nz), lambda i: (1, 0, y_last, 0)),
        ],
        out_specs=tuple(pl.BlockSpec(v, lambda i: (0, 0)) for v in out),
        compiler_params=params(),
        name="edges",
    )(at, pressure, pressure, pressure, pressure, trans, trans)


def sweep_body(
    at,
    xa,
    xb,
    ya,
    yb,
    cxa,
    cxb,
    cya,
    cyb,
    p,
    p_after,
    trans,
    rhs,
    *rest,
    first,
    last,
    fluxes,
    gather,
    y_in,
    y_out,
):
    rest = list(rest)
    cell = rest.pop(0) if first else None
    weight = None if first else rest.pop(0)
    if fluxes or gather:
        got, values = rest.pop(0), [rest.pop(0) for _ in range(fluxes + gather)]
    out = rest.pop(0)
    weight_out = rest.pop(0) if first else None
    rhs_out = rest.pop(0) if fluxes else None
    trace_out, cuts = (rest.pop(0), rest.pop(0)) if gather else (None, None)
    gathered = rest.pop() if gather else None
    if fluxes:
        found, spread, cell_row = rest.pop(), rest.pop(), rest.pop()
    carry_t = rest.pop() if first else None
    carry = rest.pop()
    step = pl.program_id(0)
    steps = pl.num_programs(0)
    many, ny, nz = out.shape
    nx = ya.shape[0] if not first else ya.shape[0] // 2
    row = iota((ny, nz), 0)
    lane = iota((ny, nz), 1)
    x_even, y_even = even(at, 0), even(at, 1)

    @pl.when(step == 0)
    def _():
        if fluxes == 1:
            spread_flux(got[...], values[0][...], spread, cell_row, nz)
        if fluxes == 2:
            message = got[...]
            flux = values[0][...] - at_mortar(message, values[1][...])
            spread_flux(message, kappa_of(message) * flux, spread, cell_row, nz)
        tx_low = jnp.where(x_even, cxb[ny:, :], cxa[ny:, :])
        carry[...] = tx_low * jnp.where(x_even, xb[:ny, :], xa[:ny, :])
        if first:
            carry_t[...] = tx_low

    if fluxes:
        found[...] = sources(many * ny, step, spread, cell_row)
    for i in range(many):
        here_at = step * many + i
        right = rhs[i]
        if fluxes:
            right = right + found[i * ny : (i + 1) * ny, :]
            rhs_out[i] = right
        here = p[i]
        if i + 1 < many:
            after = p[i + 1]
        else:
            x_high = jnp.where(x_even, xa[:ny, :], xb[:ny, :])
            after = jnp.where(step + 1 < steps, p_after[0], x_high)
        one = pl.ds(here_at, 1)
        edge = pl.ds(nx + here_at, 1)
        y_low, y_high = ya[one, :], yb[one, :]
        if not y_in:
            y_low, y_high = jnp.where(y_even, y_high, y_low), jnp.where(y_even, y_low, y_high)
        ty_edge = jnp.where(y_even, cyb[edge, :], cya[edge, :])
        tx, ty, tz = trans[0, i], trans[1, i], trans[2, i]
        y_next = jnp.where(row == ny - 1, y_high, pltpu.roll(here, ny - 1, 0))
        y_prev = jnp.where(row == 0, ty_edge * y_low, pltpu.roll(ty * here, 1, 0))
        z_next = jnp.where(lane == nz - 1, 0.0, pltpu.roll(here, nz - 1, 1))
        z_prev = jnp.where(lane == 0, 0.0, pltpu.roll(tz * here, 1, 1))
        if first:
            ty_before = jnp.where(row == 0, ty_edge, pltpu.roll(ty, 1, 0))
            tz_before = jnp.where(lane == 0, 0.0, pltpu.roll(tz, 1, 1))
            diagonal = cell[i] + tx + carry_t[...] + ty + ty_before + tz + tz_before
            w = WEIGHT / diagonal
            weight_out[i] = w
            carry_t[...] = tx
        else:
            w = weight[i]
        around = (tx * after + carry[...]) + (ty * y_next + y_prev) + (tz * z_next + z_prev)
        carry[...] = tx * here
        out[i] = (1.0 - WEIGHT) * here + w * (right + around)
    if gather:
        message = got[...]
        rows = iota((LANES, many * ny), 1) + step * (many * ny)
        chosen = jnp.concatenate(
            [ones_where(rows == by_slot(message, k)[0]) for k in range(CAP)], axis=0
        )
        planes = jnp.concatenate([out[i] for i in range(many)], axis=0)
        found = pick_rounded(chosen, planes)

        @pl.when(step == 0)
        def _():
            gathered[...] = found

        @pl.when(step > 0)
        def _():
            gathered[...] += found

        @pl.when(step == steps - 1)
        def _():
            second_traces(message, values[0][...], gathered, trace_out, cuts)

    if last:
        return
    xa_out, xb_out, ya_out, yb_out = rest
    start, end = step == 0, step == steps - 1

    @pl.when(start & x_even)
    def _():
        xb_out[...] = out[0]

    @pl.when(start & ~x_even)
    def _():
        xa_out[...] = out[0]

    @pl.when(end & x_even)
    def _():
        xa_out[...] = out[many - 1]

    @pl.when(end & ~x_even)
    def _():
        xb_out[...] = out[many - 1]

    for i in range(many):
        one = pl.ds(step * many + i, 1)
        low, high = out[i, :1, :], out[i, ny - 1 :, :]
        if not y_out:
            low, high = jnp.where(y_even, high, low), jnp.where(y_even, low, high)
        ya_out[one, :] = low
        yb_out[one, :] = high


def sweep(
    at,
    p,
    halo,
    faces,
    trans,
    rhs,
    cell=None,
    weight=None,
    last=False,
    got=None,
    values=(),
    gather=False,
    y_in=False,
    y_out=False,
    many=8,
):
    nx, ny, nz = p.shape
    part = pl.BlockSpec((many, ny, nz), lambda i: (i, 0, 0))
    x_face = pl.BlockSpec((ny, nz), lambda i: (0, 0))
    y_face = pl.BlockSpec((nx, nz), lambda i: (0, 0))
    first = weight is None
    out_shape, out_specs = [shape(nx, ny, nz)], [part]
    if first:
        out_shape.append(shape(nx, ny, nz))
        out_specs.append(part)
    scratch = [pltpu.VMEM((ny, nz), F32)] * (2 if first else 1)
    if gather:
        out_shape += [sent(LANES, LANES), sent(2 * LANES, LANES)]
        out_specs += [whole((LANES, LANES)), whole((2 * LANES, LANES))]
        scratch.append(pltpu.VMEM((CAP * LANES, nz), F32))
    elif values:
        out_shape.append(shape(nx, ny, nz))
        out_specs.append(part)
        scratch += [
            pltpu.VMEM((1, CAP * LANES), jnp.int32),
            pltpu.VMEM((CAP * LANES, 2 * nz), BF16),
            pltpu.VMEM((many * ny, nz), F32),
        ]
    if not last:
        out_shape += [sent(ny, nz)] * 2 + [sent(nx, nz)] * 2
        out_specs += [x_face, x_face, y_face, y_face]
    after = pl.BlockSpec(
        (1, ny, nz), lambda i: (jnp.minimum((i + 1) * many, nx - 1), 0, 0)
    )
    if y_in:
        halo = (*halo[:2], *(in_hbm(v, 1) for v in halo[2:]))
    operands = [*halo, *faces, p, p, trans, rhs, cell if first else weight]
    operands += [in_hbm(v, 1) for v in (got, *values)] if values else []
    return pl.pallas_call(
        functools.partial(
            sweep_body,
            first=first,
            last=last,
            fluxes=0 if gather else len(values),
            gather=gather,
            y_in=y_in,
            y_out=y_out,
        ),
        grid=(nx // many,),
        out_shape=tuple(out_shape),
        in_specs=[SMEM]
        + [whole(v.shape) for v in (*halo, *faces)]
        + [part, after]
        + [pl.BlockSpec((3, many, ny, nz), lambda i: (0, i, 0, 0)), part, part]
        + ([whole(v.shape) for v in (got, *values)] if values else []),
        out_specs=tuple(out_specs),
        scratch_shapes=scratch,
        compiler_params=params(),
        cost_estimate=pl.CostEstimate(flops=6_000_000, bytes_accessed=8 << 20, transcendentals=0),
        name="sweep",
    )(at, *(in_hbm(v) for v in operands))


def swap(v, axis, count, low):
    pairs = [(i, i + 1) for i in range(low, count - 1, 2)]
    return lax.ppermute(v, axis, pairs + [(b, a) for a, b in pairs])


def swapped(xa, xb, ya, yb, mats, shards):
    return (
        swap(xa, "mat", mats, 0),
        swap(xb, "mat", mats, 1),
        swap(ya, "frac", shards, 0),
        swap(yb, "frac", shards, 1),
    )


def body(
    pressure_start,
    face_trans,
    cell_coef,
    matrix_source,
    mortar_owner,
    mortar_cell,
    mortar_frac,
    mortar_kappa,
    tiles,
    tile_cols,
    frac_diag,
    frac_source,
    fracture_start,
):
    nx, ny, nz = pressure_start.shape
    mats, shards = lax.axis_size("mat"), lax.axis_size("frac")
    rows, per_row = tile_cols.shape
    count = mortar_cell.shape[0]
    size = rows * (1 + per_row)
    at = jnp.stack([lax.axis_index("mat"), lax.axis_index("frac")]).astype(jnp.int32)
    everyone = functools.partial(
        lax.all_to_all, axis_name=("mat", "frac"), split_axis=0, concat_axis=0, tiled=True
    )
    over_frac = functools.partial(
        lax.all_to_all, axis_name="frac", split_axis=0, concat_axis=0, tiled=True
    )
    over_mat = functools.partial(
        lax.all_to_all, axis_name="mat", split_axis=0, concat_axis=0, tiled=True
    )
    square = shape(LANES, LANES)
    owner = mortar_owner.reshape(1, count)
    frac, kappa = mortar_frac.reshape(1, count), mortar_kappa.reshape(1, count)
    flat = (nx * ny, nz)
    tile_list = tiles.reshape(rows * per_row, LANES, LANES)
    diag = frac_diag.reshape(rows, LANES)
    square_scratch = pltpu.VMEM((LANES, LANES), F32)
    gathered = pltpu.VMEM((CAP * LANES, nz), F32)
    block = pltpu.VMEM((size, LANES), F32)
    scalars = (at, tile_cols.T)
    fetch_scratch = [pltpu.VMEM(flat, F32), pltpu.SemaphoreType.DMA((8,))]

    send, slot = call(
        pack_body,
        (sent(2 * LANES, LANES), pltpu.HBM((1, count), jnp.int32)),
        tile_cols.T,
        owner,
        mortar_cell.reshape(1, count),
        frac,
        kappa,
        fracture_start.reshape(rows, LANES),
        scalars=(at,),
        scratch=[square_scratch],
        name="pack",
        least=1,
    )
    send, edges_at = lax.optimization_barrier((send, at))
    got = everyone(send)

    faces = swapped(*edges(edges_at, pressure_start, face_trans), mats, shards)

    send, x_start, trace, flux, message = call(
        first_body,
        (sent(2 * LANES, LANES), *[sent(LANES, LANES)] * 4),
        got,
        diag,
        frac_source.reshape(rows, LANES),
        scalars=scalars,
        raw=(tile_list, pressure_start.reshape(flat)),
        scratch=[
            gathered,
            square_scratch,
            pltpu.VMEM((per_row, LANES, LANES), F32),
            pltpu.SemaphoreType.DMA(()),
            *fetch_scratch,
        ],
        flops=2e9,
        name="first",
    )
    send, *faces = lax.optimization_barrier((send, *faces))
    reduced = everyone(send)
    pressure, weight, rhs, *sides = sweep(
        at, pressure_start, faces, faces, face_trans, matrix_source, cell_coef, got=message, values=(flux,)
    )
    sides = swapped(*sides, mats, shards)

    send = call(sum_body, sent(2 * LANES, LANES), reduced, name="sums")
    send, pressure = lax.optimization_barrier((send, pressure))
    residuals = everyone(send)
    chosen = call(
        functools.partial(columns_body, shards=shards, rows=rows, tiles=per_row),
        shape(LANES, shards * rows * per_row, dtype=BF16),
        got,
        name="columns",
    )
    r, sums, send = call(
        start_body,
        (*[sent(LANES, LANES)] * 2, sent(shards * size, LANES)),
        residuals,
        diag,
        scalars=scalars,
        resident=(tile_list,),
        scratch=[block],
        name="start",
    )
    x, d = x_start, r
    send, pressure, *sides = lax.optimization_barrier((send, pressure, *sides))
    arrived = over_frac(send)
    pressure, trace, change, *sides = sweep(
        at,
        pressure,
        sides,
        faces,
        face_trans,
        rhs,
        weight=weight,
        got=message,
        values=(trace,),
        gather=True,
        y_out=True,
    )

    arrived, change = lax.optimization_barrier((arrived, change))
    change = over_mat(change)
    arrived, change = lax.optimization_barrier((arrived, change))

    def step(arrived, x, r, d, *more, ride=None, last=False, faces_in=False, faces=(), side=()):
        length = size + (shards + mats if ride == "reduce" else 0) + (2 * nx if faces else 0)
        outs = [*[sent(LANES, LANES)] * 3, sent(shards * (1 if last else length), LANES)]
        if ride == "gather":
            outs += [sent(shards, LANES), sent(LANES, LANES)]
        if faces_in:
            outs += [sent(nx, nz)] * 2
        return call(
            functools.partial(
                step_body, ride=ride, last=last, faces_in=faces_in, faces_out=bool(faces)
            ),
            tuple(outs),
            arrived,
            chosen,
            diag,
            *more,
            side=(x, r, d, *side, *faces),
            scalars=scalars,
            resident=(tile_list,),
            scratch=([square_scratch] if ride == "next" else []) + [block],
            name="step",
        )

    def swapped_mat(xa, xb):
        return swap(xa, "mat", mats, 0), swap(xb, "mat", mats, 1)

    x, r, d, send = step(arrived, x, r, d, change, ride="reduce")
    send, trace, *x_sides = lax.optimization_barrier((send, trace, *sides[:2]))
    arrived = over_frac(send)
    x_sides = swapped_mat(*x_sides)
    arrived, *x_sides = lax.optimization_barrier((arrived, *x_sides))

    x, r, d, send, change, home = step(arrived, x, r, d, ride="gather", faces=sides[2:])
    arrived = over_frac(send)
    parts = [change, lax.ppermute(change, "mat", [(i, i ^ 1) for i in range(mats)])]
    pair = jnp.concatenate(parts, axis=0)
    for hop in range(2, mats, 2):
        parts.append(lax.ppermute(pair, "mat", [(i, i ^ hop) for i in range(mats)]))

    x, r, d, send, *y_sides = step(
        arrived, x, r, d, *parts[1:], faces_in=True, ride="next", side=(change, x_start, sums)
    )
    x_flux = x
    arrived = over_frac(send)
    pressure, rhs, *sides = sweep(
        at,
        pressure,
        (*x_sides, *y_sides),
        faces,
        face_trans,
        matrix_source,
        weight=weight,
        got=message,
        values=(trace, x_flux),
        y_in=True,
        y_out=True,
    )
    arrived, pressure, *sides = lax.optimization_barrier((arrived, pressure, *sides))
    x, r, d, send = step(arrived, x, r, d, faces=sides[2:])
    send, home, *sides = lax.optimization_barrier((send, home, *sides[:2]))
    arrived = over_frac(send)
    x_sides = swapped_mat(*sides)
    flux = call(
        functools.partial(home_body, mats=mats),
        shape(1, count),
        side=(home, owner, slot, frac, kappa, x_flux),
        name="home",
    )
    arrived, flux, *x_sides = lax.optimization_barrier((arrived, flux, *x_sides))
    x, r, d, send, *y_sides = step(arrived, x, r, d, last=True, faces_in=True)
    send, pressure, flux = lax.optimization_barrier((send, pressure, flux))
    arrived = over_frac(send)
    [pressure] = sweep(
        at,
        pressure,
        (*x_sides, *y_sides),
        faces,
        face_trans,
        rhs,
        weight=weight,
        last=True,
        y_in=True,
    )
    fracture = call(
        final_body, shape(rows, LANES), arrived, side=(x, r, d), scalars=(at,), name="final"
    )
    return pressure, fracture.reshape(rows * LANES), flux.reshape(count)


def solution(mesh):
    in_specs = (
        P("mat", "frac", None),
        P(None, "mat", "frac", None),
        P("mat", "frac", None),
        P("mat", "frac", None),
        P(("mat", "frac"), None),
        P(("mat", "frac")),
        P(("mat", "frac")),
        P(("mat", "frac")),
        P("frac", None, None, None),
        P("frac", None),
        P("frac"),
        P("frac"),
        P("frac"),
    )
    out_specs = (P("mat", "frac", None), P("frac"), P(("mat", "frac")))
    return jax.shard_map(body, mesh=mesh, in_specs=in_specs, out_specs=out_specs, check_vma=False)
```

```python
import functools
import math

import jax
import jax.numpy as jnp
from jax import lax
from jax.experimental import pallas as pl
from jax.experimental.pallas import tpu as pltpu
from jax.sharding import PartitionSpec as P

WEIGHT = 0.8
CAP = 8
LANES = 128
LARGE = 1 << 18
F32 = jnp.float32
BF16 = jnp.bfloat16
SMEM = pl.BlockSpec(memory_space=pltpu.SMEM)
VMEM = pl.BlockSpec(memory_space=pltpu.VMEM)
RAW = pl.BlockSpec(memory_space=pltpu.HBM)
X, Y, Z, HI, LO, KAPPA, COLS = (CAP * i for i in range(7))


def shape(*dims, dtype=F32):
    if math.prod(dims) >= LARGE:
        return pltpu.HBM(dims, dtype)
    return jax.ShapeDtypeStruct(dims, dtype)


def sent(*dims):
    return pltpu.HBM(dims, F32)


def in_hbm(x, least=LARGE):
    if x.size < least:
        return x
    return pltpu.with_memory_space_constraint(x, pltpu.HBM)


def on_chip(v):
    return isinstance(v, jax.ShapeDtypeStruct) and math.prod(v.shape) < LARGE


def whole(dims):
    return pl.BlockSpec(dims, lambda i: (0,) * len(dims), pipeline_mode=pl.Buffered(1))


def params():
    return pltpu.CompilerParams(vmem_limit_bytes=32 << 20)


def call(
    body, outs, *operands, scalars=(), raw=(), resident=(), side=(), scratch=(), flops=1e6, nbytes=1e6, name=None, least=LARGE
):
    single = not isinstance(outs, tuple)
    outs = (outs,) if single else outs
    result = pl.pallas_call(
        body,
        grid=(1,),
        out_shape=outs,
        in_specs=[SMEM] * len(scalars) + [RAW] * len(raw) + [VMEM] * len(resident) + [VMEM if v.size < least else whole(v.shape) for v in operands]
        + [whole(v.shape) for v in side],
        out_specs=tuple(
            VMEM if on_chip(v) else pl.BlockSpec(v.shape, lambda i, n=len(v.shape): (0,) * n)
            for v in outs
        ),
        scratch_shapes=scratch,
        compiler_params=params(),
        cost_estimate=pl.CostEstimate(
            flops=int(flops), bytes_accessed=int(nbytes), transcendentals=0
        ),
        name=name,
    )(
        *scalars,
        *(in_hbm(v, least) for v in raw),
        *resident,
        *(in_hbm(v, least) for v in operands),
        *(in_hbm(v, 1) for v in side),
    )
    return result[0] if single else result


def iota(dims, dim):
    return lax.broadcasted_iota(jnp.int32, dims, dim)


def ones_where(mask):
    return jnp.where(mask, 1.0, 0.0).astype(BF16)


def halves(v):
    top = v.astype(BF16)
    return jnp.concatenate([top, (v - top.astype(F32)).astype(BF16)], axis=1)


def pick_rounded(chosen, v):
    width = v.shape[1]
    out = jnp.dot(chosen, halves(v), preferred_element_type=F32)
    return out[:, :width] + out[:, width:]


def total(v):
    return jnp.sum(jnp.sum(v, axis=1, keepdims=True), axis=0, keepdims=True)


def row_sums(v):
    return jnp.sum(v.T, axis=0, keepdims=True)


def as_column(row):
    return jnp.broadcast_to(row, (LANES, LANES)).T


def pack_body(at, cols, owner, cell, frac, kappa, x_own, send, slot_out, blocks):
    count = owner.shape[1]
    mine = at[0]
    own = owner[...]
    slot = jnp.zeros((1, count), jnp.int32)
    for first in range(0, count, LANES):
        column = jnp.broadcast_to(own[:, first : first + LANES], (LANES, LANES)).T
        column = jnp.concatenate([column] * (count // LANES), axis=1)
        before = iota((LANES, count), 0) + first < iota((LANES, count), 1)
        slot += jnp.sum(jnp.where((column == own) & before, 1, 0), axis=0, keepdims=True)
    slot_out[...] = slot
    here = iota((CAP, count), 0) == slot
    c, f = cell[...], frac[...]
    k = kappa[...]
    top = k.astype(BF16).astype(F32)
    middle = (k - top).astype(BF16).astype(F32)
    low = k - top - middle
    whole = [c >> 14, (c >> 8) & 63, c & 255, f >> 7, f & 127]
    rows = [jnp.where(here, v.astype(F32), 0.0) for v in whole]
    rows = jnp.concatenate([*rows, jnp.where(here, top, 0.0), jnp.zeros((LANES - 6 * CAP, count), F32)], axis=0)
    chosen = ones_where(iota((LANES, count), 0) == own)
    nt = functools.partial(
        lax.dot_general,
        dimension_numbers=(((1,), (1,)), ((), ())),
        preferred_element_type=F32,
    )

    def kappas(v):
        return jnp.concatenate(
            [
                jnp.zeros((KAPPA, count), F32),
                jnp.where(here, v, 0.0),
                jnp.zeros((LANES - 6 * CAP, count), F32),
            ],
            axis=0,
        ).astype(BF16)

    message = nt(chosen, rows.astype(BF16)) + nt(chosen, kappas(middle)) + nt(chosen, kappas(low))
    lane = iota((1, LANES), 1)
    extra = jnp.zeros((1, LANES), F32)
    for t in range(cols.shape[0]):
        column = jnp.where(iota((1, cols.shape[1]), 1) == mine, cols[t : t + 1, :], 0)
        column = jnp.sum(column, axis=1, keepdims=True).astype(F32)
        extra = jnp.where(lane == COLS + t, column, extra)
    blocks[...] = jnp.broadcast_to(x_own[pl.ds(mine, 1), :], (LANES, LANES))
    send[pl.ds(0, LANES, stride=2), :] = blocks[...]
    send[pl.ds(1, LANES, stride=2), :] = message + extra


def by_slot(message, k):
    x = message[:, X + k : X + k + 1].astype(jnp.int32)
    y = message[:, Y + k : Y + k + 1].astype(jnp.int32)
    z = message[:, Z + k : Z + k + 1].astype(jnp.int32)
    hi = message[:, HI + k : HI + k + 1].astype(jnp.int32)
    lo = message[:, LO + k : LO + k + 1].astype(jnp.int32)
    return x * 64 + y, z, hi, lo, message[:, KAPPA + k : KAPPA + k + 1]


def in_parts(source, target, arrived):
    parts = arrived.shape[0]
    each = source.shape[0] // parts
    copies = []
    for i in range(parts):
        part = pl.ds(i * each, each)
        copies.append(
            pltpu.make_async_copy(source.at[part], target.at[part], arrived.at[i])
        )
        copies[-1].start()
    return copies


def traces(message, pressure_all, pressure, here, gathered):
    copies = in_parts(pressure_all, pressure, here)
    rows, depth = pressure.shape
    chosen = jnp.concatenate(
        [ones_where(iota((LANES, rows), 1) == by_slot(message, k)[0]) for k in range(CAP)], axis=0
    )
    for copy in copies:
        copy.wait()
    gathered[...] = pick_rounded(chosen, pressure[...])
    return at_depth(message, gathered)


def at_depth(message, gathered):
    depth = gathered.shape[1]
    lane = iota((LANES, LANES), 1)
    out = jnp.zeros((LANES, LANES), F32)
    for k in range(CAP):
        z = by_slot(message, k)[1]
        part = gathered[k * LANES : (k + 1) * LANES, :]
        value = jnp.sum(jnp.where(iota((LANES, depth), 1) == z, part, 0.0), axis=1, keepdims=True)
        out = jnp.where(lane == k, value, out)
    return out


def at_mortar(message, x):
    chosen = jnp.concatenate(
        [ones_where(iota((LANES, LANES), 1) == by_slot(message, k)[2]) for k in range(CAP)], axis=0
    )
    found = pick_rounded(chosen, x)
    lane = iota((LANES, LANES), 1)
    out = jnp.zeros((LANES, LANES), F32)
    for k in range(CAP):
        part = found[k * LANES : (k + 1) * LANES, :]
        value = jnp.sum(jnp.where(lane == by_slot(message, k)[3], part, 0.0), axis=1, keepdims=True)
        out = jnp.where(lane == k, value, out)
    return out


def onto_fracture(message, *values):
    flipped = message.T
    hi = jnp.concatenate([flipped[HI + k : HI + k + 1, :] for k in range(CAP)], axis=1)
    chosen = ones_where(iota((LANES, CAP * LANES), 0) == hi.astype(jnp.int32))
    lane = iota((LANES, LANES), 1)
    wide = []
    for v in values:
        spread = [
            jnp.where(lane == by_slot(message, k)[3], v[:, k : k + 1], 0.0) for k in range(CAP)
        ]
        wide.append(jnp.concatenate(spread, axis=0))
    return [pick_rounded(chosen, v) for v in wide]


def kappa_of(message):
    lane = iota((LANES, LANES), 1)
    out = jnp.zeros((LANES, LANES), F32)
    for k in range(CAP):
        out = jnp.where(lane == k, message[:, KAPPA + k : KAPPA + k + 1], out)
    return out


def first_body(
    at,
    cols,
    tiles_all,
    pressure_all,
    got,
    diag,
    source,
    send,
    x_out,
    trace_out,
    flux_out,
    message_out,
    gathered,
    part,
    tiles,
    arrived,
    pressure,
    here,
):
    mine, shard = at[0], at[1]
    per_row = cols.shape[0]
    fetch = pltpu.make_async_copy(tiles_all.at[pl.ds(per_row * mine, per_row)], tiles, arrived)
    fetch.start()
    groups = LANES // CAP
    for m in range(CAP):
        x_out[pl.ds(m, groups, stride=CAP), :] = got[
            pl.ds(2 * m * groups, groups, stride=2), :
        ]
    message = got[pl.ds(1, LANES, stride=2), :]
    message_out[...] = message
    trace = traces(message, pressure_all, pressure, here, gathered)
    kappa = kappa_of(message)
    flux = kappa * (trace - at_mortar(message, x_out[...]))
    load, weight = onto_fracture(message, flux, kappa)
    part[...] = load
    row = CAP * shard + mine
    x_row = x_out[pl.ds(row, 1), :]
    x_col = as_column(x_row)
    mixed = jnp.zeros((LANES, LANES), F32)
    fetch.wait()
    for t in range(per_row):
        tile = tiles[t]
        mixed += tile * x_out[pl.ds(cols[t, mine], 1), :]
        back = jnp.sum(tile * x_col, axis=0, keepdims=True)
        part[pl.ds(cols[t, mine], 1), :] -= 0.5 * back
    part[pl.ds(row, 1), :] += source[pl.ds(mine, 1), :] - (
        diag[pl.ds(mine, 1), :] * x_row + 0.5 * row_sums(mixed)
    )
    send[pl.ds(0, LANES, stride=2), :] = part[...]
    send[pl.ds(1, LANES, stride=2), :] = weight
    trace_out[...] = trace
    flux_out[...] = flux


def spread_flux(message, values, spread, cell_row, depth):
    flipped = message.T
    for k in range(CAP):
        z = by_slot(message, k)[1]
        placed = jnp.where(iota((LANES, depth), 1) == z, values[:, k : k + 1], 0.0)
        spread[k * LANES : (k + 1) * LANES, :] = halves(placed)
        cell_row[:, k * LANES : (k + 1) * LANES] = (
            flipped[X + k : X + k + 1, :] * 64 + flipped[Y + k : Y + k + 1, :]
        ).astype(jnp.int32)


def sources(rows, step, spread, cell_row):
    depth = spread.shape[1] // 2
    row = iota((rows, CAP * LANES), 0) + step * rows
    chosen = ones_where(row == cell_row[...])
    out = jnp.dot(chosen, spread[...], preferred_element_type=F32)
    return out[:, :depth] + out[:, depth:]


def second_traces(message, trace, gathered, trace_out, send):
    now = at_depth(message, gathered)
    trace_out[...] = now
    [change] = onto_fracture(message, kappa_of(message) * (now - trace))
    mats = CAP
    each = LANES // mats
    for m in range(mats):
        part = slice(m * each, (m + 1) * each)
        send[2 * m * each : (2 * m + 1) * each, :] = change[part, :]
        send[(2 * m + 1) * each : (2 * m + 2) * each, :] = now[part, :]


def home_body(got, owner, slot, frac, kappa, x, flux, *, mats):
    count = owner.shape[1]

    def found(values, chosen):
        top = values.astype(BF16).astype(F32)
        middle = (values - top).astype(BF16).astype(F32)
        parts = jnp.concatenate([top, middle, values - top - middle], axis=0)
        if parts.shape[0] % 16:
            parts = jnp.concatenate([parts, jnp.zeros_like(top)], axis=0)
        out = jnp.dot(parts.astype(BF16), chosen, preferred_element_type=F32)
        n = values.shape[0]
        return out[:n] + out[n : 2 * n] + out[2 * n : 3 * n]

    shards = LANES // mats
    own = owner[...]
    source = (own & (shards - 1)) * mats + own // shards
    traces_all = found(got[...].T[:CAP, :], ones_where(iota((LANES, count), 0) == source))
    here = iota((CAP, count), 0) == slot[...]
    trace = jnp.sum(jnp.where(here, traces_all, 0.0), axis=0, keepdims=True)
    f = frac[...]
    x_all = found(x[...].T, ones_where(iota((LANES, count), 0) == f >> 7))
    here = iota((LANES, count), 0) == (f & 127)
    x_there = jnp.sum(jnp.where(here, x_all, 0.0), axis=0, keepdims=True)
    flux[...] = kappa[...] * (trace - x_there)


def sum_body(got, send):
    for i in range(2):
        mine = jnp.sum(got[pl.ds(i, LANES, stride=2), :], axis=0, keepdims=True)
        send[pl.ds(i, LANES, stride=2), :] = jnp.broadcast_to(mine, (LANES, LANES))


def columns_body(got, chosen, *, shards, rows, tiles):
    flipped = got[pl.ds(1, LANES, stride=2), :].T[COLS : COLS + CAP, :]
    count = shards * rows * tiles
    tile = iota((LANES, count), 1)
    sender = (tile // tiles) % rows * shards + tile // (rows * tiles)
    moved = jnp.dot(
        jnp.concatenate([flipped, flipped], axis=0).astype(BF16),
        ones_where(iota((LANES, count), 0) == sender),
        preferred_element_type=F32,
    )[:CAP]
    here = iota((CAP, count), 0) == iota((CAP, count), 1) % tiles
    column = jnp.sum(jnp.where(here, moved, 0.0), axis=0, keepdims=True).astype(jnp.int32)
    chosen[...] = ones_where(iota((LANES, count), 0) == column)


def products(at, cols, d, tiles, diag, block):
    shard = at[1]
    per_row, rows = cols.shape
    for r in range(rows):
        d_row = d[pl.ds(CAP * shard + r, 1), :]
        d_col = as_column(d_row)
        mixed = jnp.zeros((LANES, LANES), F32)
        for t in range(per_row):
            tile = tiles[per_row * r + t]
            mixed += tile * d[pl.ds(cols[t, r], 1), :]
            back = jnp.sum(tile * d_col, axis=0, keepdims=True)
            block[rows + per_row * r + t : rows + per_row * r + t + 1, :] = 0.5 * back
        block[r : r + 1, :] = diag[r : r + 1, :] * d_row + 0.5 * row_sums(mixed)


def image_of(got, chosen, step, rows, tiles):
    shards = got.shape[0] // step
    own = jnp.concatenate([got[s * step : s * step + rows, :] for s in range(shards)], axis=0)
    back = jnp.concatenate(
        [got[s * step + rows : s * step + rows + tiles, :] for s in range(shards)], axis=0
    )
    return own + pick_rounded(chosen[...], back)


def start_body(at, cols, tiles, got, diag, r_out, weight_out, send, block):
    r_out[...] = got[pl.ds(0, LANES, stride=2), :]
    weight_out[...] = got[pl.ds(1, LANES, stride=2), :]
    products(at, cols, r_out, tiles, diag, block)
    size = block.shape[0]
    for s in range(send.shape[0] // size):
        send[s * size : (s + 1) * size, :] = block[...]


def step_body(
    at, cols, tiles, got, chosen, diag, *rest, ride, last, faces_in, faces_out
):
    per_row, rows = cols.shape
    size = rows * (1 + per_row)
    shards = LANES // rows
    mats = rows
    extra = list(rest)
    change = extra.pop(0) if ride == "reduce" else None
    parts = [extra.pop(0) for _ in range(mats // 2)] if ride == "next" else None
    x, r, d = (extra.pop(0) for _ in range(3))
    if ride == "next":
        parts.insert(0, extra.pop(0))
    x_before, weight = (extra.pop(0), extra.pop(0)) if ride == "next" else (None, None)
    y_faces = (extra.pop(0), extra.pop(0)) if faces_out else None
    x_out, r_out, d_out, send = (extra.pop(0) for _ in range(4))
    change_out, home = (extra.pop(0), extra.pop(0)) if ride == "gather" else (None, None)
    y_halo = (extra.pop(0), extra.pop(0)) if faces_in else None
    block = extra.pop()
    got_step = got.shape[0] // shards
    shard = at[1]
    image = image_of(got, chosen, got_step, rows, rows * per_row)
    old = d[...]
    norm = total(r[...] * r[...])
    alpha = norm / total(old * image)
    x_new = x[...] + alpha * old
    r_new = r[...] - alpha * image
    x_out[...] = x_new
    if ride == "next":
        [whole_change] = extra
        k = 0
        for part in parts:
            for i in range(part.shape[0] // shards):
                place = pl.multiple_of((at[0] ^ k) * shards, shards)
                whole_change[pl.ds(place, shards), :] = part[i * shards : (i + 1) * shards, :]
                k += 1
        r_new = r_new + whole_change[...] - weight[...] * (x_new - x_before[...])
        d_out[...] = r_new
    else:
        d_out[...] = r_new + (total(r_new * r_new) / norm) * old
    r_out[...] = r_new
    if last:
        lanes = jnp.zeros((1, LANES), F32)
        for i in range(rows):
            d_row = d_out[pl.ds(CAP * shard + i, 1), :]
            mixed = jnp.zeros((LANES, LANES), F32)
            for t in range(per_row):
                mixed += tiles[per_row * i + t] * d_out[pl.ds(cols[t, i], 1), :]
            lanes += diag[i : i + 1, :] * d_row * d_row
            lanes += jnp.sum(mixed * as_column(d_row), axis=0, keepdims=True)
        send[...] = jnp.broadcast_to(lanes, send.shape)
    else:
        products(at, cols, d_out, tiles, diag, block)
        send_step = send.shape[0] // shards
        if ride == "reduce":
            found = change[:shards, :]
            for m in range(1, mats):
                found = found + change[2 * m * shards : (2 * m + 1) * shards, :]
        for s in range(shards):
            first = s * send_step
            send[first : first + size, :] = block[...]
            first += size
            if ride == "reduce":
                send[first : first + shards, :] = found
                for m in range(mats):
                    row = (2 * m + 1) * shards + s
                    send[first + shards + m : first + shards + m + 1, :] = change[row : row + 1, :]
                first += shards + mats
            if faces_out:
                face = jnp.where(shard < s, y_faces[1][...], y_faces[0][...])
                deep = face.shape[0]
                send[first : first + deep, :] = face[:, :LANES]
                send[first + deep : first + 2 * deep, :] = face[:, LANES:]
    first = size
    if ride == "gather":
        found = jnp.zeros((shards, LANES), F32)
        for s in range(shards):
            row = s * got_step + size
            found += got[row : row + shards, :]
            home[s * mats : (s + 1) * mats, :] = got[row + shards : row + shards + mats, :]
        change_out[...] = found
        first += shards + mats
    if faces_in:
        deep = y_halo[0].shape[0]
        for halo, other, there in (
            (y_halo[0], jnp.maximum(shard - 1, 0), shard > 0),
            (y_halo[1], jnp.minimum(shard + 1, shards - 1), shard < shards - 1),
        ):
            row = pl.multiple_of(other * got_step + first, 8)
            for half in range(2):
                values = got[pl.ds(row + half * deep, deep), :]
                halo[:, half * LANES : (half + 1) * LANES] = jnp.where(there, values, 0.0)


def final_body(at, got, x, r, d, out):
    alpha = total(r[...] * r[...]) / total(got[...])
    here = pl.ds(pl.multiple_of(CAP * at[1], CAP), CAP)
    out[...] = x[here, :] + alpha * d[here, :]


def even(at, dim):
    return (at[dim] & 1) == 0


def edges_body(at, px0, px1, py0, py1, tx1, ty1, xa, xb, ya, yb):
    wide, deep = px0.shape[1], py0.shape[0]
    low, high = px0[0], px1[0]
    xa[:wide, :] = jnp.where(even(at, 0), high, low)
    xb[:wide, :] = jnp.where(even(at, 0), low, high)
    xa[wide:, :] = tx1[0, 0]
    xb[wide:, :] = tx1[0, 0]
    low, high = py0[:, 0, :], py1[:, 7, :]
    ya[:deep, :] = jnp.where(even(at, 1), high, low)
    yb[:deep, :] = jnp.where(even(at, 1), low, high)
    ya[deep:, :] = ty1[0, :, 7, :]
    yb[deep:, :] = ty1[0, :, 7, :]


def edges(at, pressure, trans):
    nx, ny, nz = pressure.shape
    y_last = ny // 8 - 1
    out = [(2 * ny, nz)] * 2 + [(2 * nx, nz)] * 2
    pressure, trans = in_hbm(pressure), in_hbm(trans)
    return pl.pallas_call(
        edges_body,
        grid=(1,),
        out_shape=tuple(sent(*v) for v in out),
        in_specs=[
            SMEM,
            pl.BlockSpec((1, ny, nz), lambda i: (0, 0, 0)),
            pl.BlockSpec((1, ny, nz), lambda i: (nx - 1, 0, 0)),
            pl.BlockSpec((nx, 8, nz), lambda i: (0, 0, 0)),
            pl.BlockSpec((nx, 8, nz), lambda i: (0, y_last, 0)),
            pl.BlockSpec((1, 1, ny, nz), lambda i: (0, nx - 1, 0, 0)),
            pl.BlockSpec((1, nx, 8, nz), lambda i: (1, 0, y_last, 0)),
        ],
        out_specs=tuple(pl.BlockSpec(v, lambda i: (0, 0)) for v in out),
        compiler_params=params(),
        name="edges",
    )(at, pressure, pressure, pressure, pressure, trans, trans)


def sweep_body(
    at,
    xa,
    xb,
    ya,
    yb,
    cxa,
    cxb,
    cya,
    cyb,
    p,
    p_after,
    trans,
    rhs,
    *rest,
    first,
    last,
    fluxes,
    gather,
    y_in,
    y_out,
):
    rest = list(rest)
    cell = rest.pop(0) if first else None
    weight = None if first else rest.pop(0)
    if fluxes or gather:
        got, values = rest.pop(0), [rest.pop(0) for _ in range(fluxes + gather)]
    out = rest.pop(0)
    weight_out = rest.pop(0) if first else None
    rhs_out = rest.pop(0) if fluxes else None
    trace_out, cuts = (rest.pop(0), rest.pop(0)) if gather else (None, None)
    gathered = rest.pop() if gather else None
    if fluxes:
        found, spread, cell_row = rest.pop(), rest.pop(), rest.pop()
    carry_t = rest.pop() if first else None
    carry = rest.pop()
    step = pl.program_id(0)
    steps = pl.num_programs(0)
    many, ny, nz = out.shape
    nx = ya.shape[0] if not first else ya.shape[0] // 2
    row = iota((ny, nz), 0)
    lane = iota((ny, nz), 1)
    x_even, y_even = even(at, 0), even(at, 1)

    @pl.when(step == 0)
    def _():
        if fluxes == 1:
            spread_flux(got[...], values[0][...], spread, cell_row, nz)
        if fluxes == 2:
            message = got[...]
            flux = values[0][...] - at_mortar(message, values[1][...])
            spread_flux(message, kappa_of(message) * flux, spread, cell_row, nz)
        tx_low = jnp.where(x_even, cxb[ny:, :], cxa[ny:, :])
        carry[...] = tx_low * jnp.where(x_even, xb[:ny, :], xa[:ny, :])
        if first:
            carry_t[...] = tx_low

    if fluxes:
        found[...] = sources(many * ny, step, spread, cell_row)
    for i in range(many):
        here_at = step * many + i
        right = rhs[i]
        if fluxes:
            right = right + found[i * ny : (i + 1) * ny, :]
            rhs_out[i] = right
        here = p[i]
        if i + 1 < many:
            after = p[i + 1]
        else:
            x_high = jnp.where(x_even, xa[:ny, :], xb[:ny, :])
            after = jnp.where(step + 1 < steps, p_after[0], x_high)
        one = pl.ds(here_at, 1)
        edge = pl.ds(nx + here_at, 1)
        y_low, y_high = ya[one, :], yb[one, :]
        if not y_in:
            y_low, y_high = jnp.where(y_even, y_high, y_low), jnp.where(y_even, y_low, y_high)
        ty_edge = jnp.where(y_even, cyb[edge, :], cya[edge, :])
        tx, ty, tz = trans[0, i], trans[1, i], trans[2, i]
        y_next = jnp.where(row == ny - 1, y_high, pltpu.roll(here, ny - 1, 0))
        y_prev = jnp.where(row == 0, ty_edge * y_low, pltpu.roll(ty * here, 1, 0))
        z_next = jnp.where(lane == nz - 1, 0.0, pltpu.roll(here, nz - 1, 1))
        z_prev = jnp.where(lane == 0, 0.0, pltpu.roll(tz * here, 1, 1))
        if first:
            ty_before = jnp.where(row == 0, ty_edge, pltpu.roll(ty, 1, 0))
            tz_before = jnp.where(lane == 0, 0.0, pltpu.roll(tz, 1, 1))
            diagonal = cell[i] + tx + carry_t[...] + ty + ty_before + tz + tz_before
            w = WEIGHT / diagonal
            weight_out[i] = w
            carry_t[...] = tx
        else:
            w = weight[i]
        around = (tx * after + carry[...]) + (ty * y_next + y_prev) + (tz * z_next + z_prev)
        carry[...] = tx * here
        out[i] = (1.0 - WEIGHT) * here + w * (right + around)
    if gather:
        message = got[...]
        rows = iota((LANES, many * ny), 1) + step * (many * ny)
        chosen = jnp.concatenate(
            [ones_where(rows == by_slot(message, k)[0]) for k in range(CAP)], axis=0
        )
        planes = jnp.concatenate([out[i] for i in range(many)], axis=0)
        found = pick_rounded(chosen, planes)

        @pl.when(step == 0)
        def _():
            gathered[...] = found

        @pl.when(step > 0)
        def _():
            gathered[...] += found

        @pl.when(step == steps - 1)
        def _():
            second_traces(message, values[0][...], gathered, trace_out, cuts)

    if last:
        return
    xa_out, xb_out, ya_out, yb_out = rest
    start, end = step == 0, step == steps - 1

    @pl.when(start & x_even)
    def _():
        xb_out[...] = out[0]

    @pl.when(start & ~x_even)
    def _():
        xa_out[...] = out[0]

    @pl.when(end & x_even)
    def _():
        xa_out[...] = out[many - 1]

    @pl.when(end & ~x_even)
    def _():
        xb_out[...] = out[many - 1]

    for i in range(many):
        one = pl.ds(step * many + i, 1)
        low, high = out[i, :1, :], out[i, ny - 1 :, :]
        if not y_out:
            low, high = jnp.where(y_even, high, low), jnp.where(y_even, low, high)
        ya_out[one, :] = low
        yb_out[one, :] = high


def sweep(
    at,
    p,
    halo,
    faces,
    trans,
    rhs,
    cell=None,
    weight=None,
    last=False,
    got=None,
    values=(),
    gather=False,
    y_in=False,
    y_out=False,
    many=8,
):
    nx, ny, nz = p.shape
    part = pl.BlockSpec((many, ny, nz), lambda i: (i, 0, 0))
    x_face = pl.BlockSpec((ny, nz), lambda i: (0, 0))
    y_face = pl.BlockSpec((nx, nz), lambda i: (0, 0))
    first = weight is None
    out_shape, out_specs = [shape(nx, ny, nz)], [part]
    if first:
        out_shape.append(shape(nx, ny, nz))
        out_specs.append(part)
    scratch = [pltpu.VMEM((ny, nz), F32)] * (2 if first else 1)
    if gather:
        out_shape += [sent(LANES, LANES), sent(2 * LANES, LANES)]
        out_specs += [whole((LANES, LANES)), whole((2 * LANES, LANES))]
        scratch.append(pltpu.VMEM((CAP * LANES, nz), F32))
    elif values:
        out_shape.append(shape(nx, ny, nz))
        out_specs.append(part)
        scratch += [
            pltpu.VMEM((1, CAP * LANES), jnp.int32),
            pltpu.VMEM((CAP * LANES, 2 * nz), BF16),
            pltpu.VMEM((many * ny, nz), F32),
        ]
    if not last:
        out_shape += [sent(ny, nz)] * 2 + [sent(nx, nz)] * 2
        out_specs += [x_face, x_face, y_face, y_face]
    after = pl.BlockSpec(
        (1, ny, nz), lambda i: (jnp.minimum((i + 1) * many, nx - 1), 0, 0)
    )
    if y_in:
        halo = (*halo[:2], *(in_hbm(v, 1) for v in halo[2:]))
    operands = [*halo, *faces, p, p, trans, rhs, cell if first else weight]
    operands += [in_hbm(v, 1) for v in (got, *values)] if values else []
    return pl.pallas_call(
        functools.partial(
            sweep_body,
            first=first,
            last=last,
            fluxes=0 if gather else len(values),
            gather=gather,
            y_in=y_in,
            y_out=y_out,
        ),
        grid=(nx // many,),
        out_shape=tuple(out_shape),
        in_specs=[SMEM]
        + [whole(v.shape) for v in (*halo, *faces)]
        + [part, after]
        + [pl.BlockSpec((3, many, ny, nz), lambda i: (0, i, 0, 0)), part, part]
        + ([whole(v.shape) for v in (got, *values)] if values else []),
        out_specs=tuple(out_specs),
        scratch_shapes=scratch,
        compiler_params=params(),
        cost_estimate=pl.CostEstimate(flops=6_000_000, bytes_accessed=8 << 20, transcendentals=0),
        name="sweep",
    )(at, *(in_hbm(v) for v in operands))


def swap(v, axis, count, low):
    pairs = [(i, i + 1) for i in range(low, count - 1, 2)]
    return lax.ppermute(v, axis, pairs + [(b, a) for a, b in pairs])


def swapped(xa, xb, ya, yb, mats, shards):
    return (
        swap(xa, "mat", mats, 0),
        swap(xb, "mat", mats, 1),
        swap(ya, "frac", shards, 0),
        swap(yb, "frac", shards, 1),
    )


def body(
    pressure_start,
    face_trans,
    cell_coef,
    matrix_source,
    mortar_owner,
    mortar_cell,
    mortar_frac,
    mortar_kappa,
    tiles,
    tile_cols,
    frac_diag,
    frac_source,
    fracture_start,
):
    nx, ny, nz = pressure_start.shape
    mats, shards = lax.axis_size("mat"), lax.axis_size("frac")
    rows, per_row = tile_cols.shape
    count = mortar_cell.shape[0]
    size = rows * (1 + per_row)
    at = jnp.stack([lax.axis_index("mat"), lax.axis_index("frac")]).astype(jnp.int32)
    everyone = functools.partial(
        lax.all_to_all, axis_name=("mat", "frac"), split_axis=0, concat_axis=0, tiled=True
    )
    over_frac = functools.partial(
        lax.all_to_all, axis_name="frac", split_axis=0, concat_axis=0, tiled=True
    )
    over_mat = functools.partial(
        lax.all_to_all, axis_name="mat", split_axis=0, concat_axis=0, tiled=True
    )
    square = shape(LANES, LANES)
    owner = mortar_owner.reshape(1, count)
    frac, kappa = mortar_frac.reshape(1, count), mortar_kappa.reshape(1, count)
    flat = (nx * ny, nz)
    tile_list = tiles.reshape(rows * per_row, LANES, LANES)
    diag = frac_diag.reshape(rows, LANES)
    square_scratch = pltpu.VMEM((LANES, LANES), F32)
    gathered = pltpu.VMEM((CAP * LANES, nz), F32)
    block = pltpu.VMEM((size, LANES), F32)
    scalars = (at, tile_cols.T)
    fetch_scratch = [pltpu.VMEM(flat, F32), pltpu.SemaphoreType.DMA((8,))]

    send, slot = call(
        pack_body,
        (sent(2 * LANES, LANES), pltpu.HBM((1, count), jnp.int32)),
        tile_cols.T,
        owner,
        mortar_cell.reshape(1, count),
        frac,
        kappa,
        fracture_start.reshape(rows, LANES),
        scalars=(at,),
        scratch=[square_scratch],
        name="pack",
        least=1,
    )
    send, edges_at = lax.optimization_barrier((send, at))
    got = everyone(send)

    faces = swapped(*edges(edges_at, pressure_start, face_trans), mats, shards)

    send, x_start, trace, flux, message = call(
        first_body,
        (sent(2 * LANES, LANES), *[sent(LANES, LANES)] * 4),
        got,
        diag,
        frac_source.reshape(rows, LANES),
        scalars=scalars,
        raw=(tile_list, pressure_start.reshape(flat)),
        scratch=[
            gathered,
            square_scratch,
            pltpu.VMEM((per_row, LANES, LANES), F32),
            pltpu.SemaphoreType.DMA(()),
            *fetch_scratch,
        ],
        flops=2e9,
        name="first",
    )
    send, *faces = lax.optimization_barrier((send, *faces))
    reduced = everyone(send)
    pressure, weight, rhs, *sides = sweep(
        at, pressure_start, faces, faces, face_trans, matrix_source, cell_coef, got=message, values=(flux,)
    )
    sides = swapped(*sides, mats, shards)

    send = call(sum_body, sent(2 * LANES, LANES), reduced, name="sums")
    send, pressure = lax.optimization_barrier((send, pressure))
    residuals = everyone(send)
    chosen = call(
        functools.partial(columns_body, shards=shards, rows=rows, tiles=per_row),
        shape(LANES, shards * rows * per_row, dtype=BF16),
        got,
        name="columns",
    )
    r, sums, send = call(
        start_body,
        (*[sent(LANES, LANES)] * 2, sent(shards * size, LANES)),
        residuals,
        diag,
        scalars=scalars,
        resident=(tile_list,),
        scratch=[block],
        name="start",
    )
    x, d = x_start, r
    send, pressure, *sides = lax.optimization_barrier((send, pressure, *sides))
    arrived = over_frac(send)
    pressure, trace, change, *sides = sweep(
        at,
        pressure,
        sides,
        faces,
        face_trans,
        rhs,
        weight=weight,
        got=message,
        values=(trace,),
        gather=True,
        y_out=True,
    )

    arrived, change = lax.optimization_barrier((arrived, change))
    change = over_mat(change)
    arrived, change = lax.optimization_barrier((arrived, change))

    def step(arrived, x, r, d, *more, ride=None, last=False, faces_in=False, faces=(), side=()):
        length = size + (shards + mats if ride == "reduce" else 0) + (2 * nx if faces else 0)
        outs = [*[sent(LANES, LANES)] * 3, sent(shards * (1 if last else length), LANES)]
        if ride == "gather":
            outs += [sent(shards, LANES), sent(LANES, LANES)]
        if faces_in:
            outs += [sent(nx, nz)] * 2
        return call(
            functools.partial(
                step_body, ride=ride, last=last, faces_in=faces_in, faces_out=bool(faces)
            ),
            tuple(outs),
            arrived,
            chosen,
            diag,
            *more,
            side=(x, r, d, *side, *faces),
            scalars=scalars,
            resident=(tile_list,),
            scratch=([square_scratch] if ride == "next" else []) + [block],
            name="step",
        )

    def swapped_mat(xa, xb):
        return swap(xa, "mat", mats, 0), swap(xb, "mat", mats, 1)

    x, r, d, send = step(arrived, x, r, d, change, ride="reduce")
    send, trace, *x_sides = lax.optimization_barrier((send, trace, *sides[:2]))
    arrived = over_frac(send)
    x_sides = swapped_mat(*x_sides)
    arrived, *x_sides = lax.optimization_barrier((arrived, *x_sides))

    x, r, d, send, change, home = step(arrived, x, r, d, ride="gather", faces=sides[2:])
    arrived = over_frac(send)
    parts = [change, lax.ppermute(change, "mat", [(i, i ^ 1) for i in range(mats)])]
    pair = jnp.concatenate(parts, axis=0)
    for hop in range(2, mats, 2):
        parts.append(lax.ppermute(pair, "mat", [(i, i ^ hop) for i in range(mats)]))

    x, r, d, send, *y_sides = step(
        arrived, x, r, d, *parts[1:], faces_in=True, ride="next", side=(change, x_start, sums)
    )
    x_flux = x
    arrived = over_frac(send)
    pressure, rhs, *sides = sweep(
        at,
        pressure,
        (*x_sides, *y_sides),
        faces,
        face_trans,
        matrix_source,
        weight=weight,
        got=message,
        values=(trace, x_flux),
        y_in=True,
        y_out=True,
    )
    arrived, pressure, *sides = lax.optimization_barrier((arrived, pressure, *sides))
    x, r, d, send = step(arrived, x, r, d, faces=sides[2:])
    send, home, *sides = lax.optimization_barrier((send, home, *sides[:2]))
    arrived = over_frac(send)
    x_sides = swapped_mat(*sides)
    flux = call(
        functools.partial(home_body, mats=mats),
        shape(1, count),
        side=(home, owner, slot, frac, kappa, x_flux),
        name="home",
    )
    arrived, flux, *x_sides = lax.optimization_barrier((arrived, flux, *x_sides))
    x, r, d, send, *y_sides = step(arrived, x, r, d, last=True, faces_in=True)
    send, pressure, flux = lax.optimization_barrier((send, pressure, flux))
    arrived = over_frac(send)
    [pressure] = sweep(
        at,
        pressure,
        (*x_sides, *y_sides),
        faces,
        face_trans,
        rhs,
        weight=weight,
        last=True,
        y_in=True,
    )
    fracture = call(
        final_body, shape(rows, LANES), arrived, side=(x, r, d), scalars=(at,), name="final"
    )
    return pressure, fracture.reshape(rows * LANES), flux.reshape(count)


def solution(mesh):
    in_specs = (
        P("mat", "frac", None),
        P(None, "mat", "frac", None),
        P("mat", "frac", None),
        P("mat", "frac", None),
        P(("mat", "frac"), None),
        P(("mat", "frac")),
        P(("mat", "frac")),
        P(("mat", "frac")),
        P("frac", None, None, None),
        P("frac", None),
        P("frac"),
        P("frac"),
        P("frac"),
    )
    out_specs = (P("mat", "frac", None), P("frac"), P(("mat", "frac")))
    return jax.shard_map(body, mesh=mesh, in_specs=in_specs, out_specs=out_specs, check_vma=False)
```

```python
import functools
import math

import jax
import jax.numpy as jnp
from jax import lax
from jax.experimental import pallas as pl
from jax.experimental.pallas import tpu as pltpu
from jax.sharding import PartitionSpec as P

WEIGHT = 0.8
CAP = 8
LANES = 128
LARGE = 1 << 18
F32 = jnp.float32
BF16 = jnp.bfloat16
SMEM = pl.BlockSpec(memory_space=pltpu.SMEM)
VMEM = pl.BlockSpec(memory_space=pltpu.VMEM)
RAW = pl.BlockSpec(memory_space=pltpu.HBM)
X, Y, Z, HI, LO, KAPPA, COLS = (CAP * i for i in range(7))


def shape(*dims, dtype=F32):
    if math.prod(dims) >= LARGE:
        return pltpu.HBM(dims, dtype)
    return jax.ShapeDtypeStruct(dims, dtype)


def sent(*dims):
    return pltpu.HBM(dims, F32)


def in_hbm(x, least=LARGE):
    if x.size < least:
        return x
    return pltpu.with_memory_space_constraint(x, pltpu.HBM)


def on_chip(v):
    return isinstance(v, jax.ShapeDtypeStruct) and math.prod(v.shape) < LARGE


def whole(dims):
    return pl.BlockSpec(dims, lambda i: (0,) * len(dims), pipeline_mode=pl.Buffered(1))


def params():
    return pltpu.CompilerParams(vmem_limit_bytes=32 << 20)


def call(
    body, outs, *operands, scalars=(), raw=(), resident=(), side=(), scratch=(), flops=1e6, nbytes=1e6, name=None, least=LARGE
):
    single = not isinstance(outs, tuple)
    outs = (outs,) if single else outs
    result = pl.pallas_call(
        body,
        grid=(1,),
        out_shape=outs,
        in_specs=[SMEM] * len(scalars) + [RAW] * len(raw) + [VMEM] * len(resident) + [VMEM if v.size < least else whole(v.shape) for v in operands]
        + [whole(v.shape) for v in side],
        out_specs=tuple(
            VMEM if on_chip(v) else pl.BlockSpec(v.shape, lambda i, n=len(v.shape): (0,) * n)
            for v in outs
        ),
        scratch_shapes=scratch,
        compiler_params=params(),
        cost_estimate=pl.CostEstimate(
            flops=int(flops), bytes_accessed=int(nbytes), transcendentals=0
        ),
        name=name,
    )(
        *scalars,
        *(in_hbm(v, least) for v in raw),
        *resident,
        *(in_hbm(v, least) for v in operands),
        *(in_hbm(v, 1) for v in side),
    )
    return result[0] if single else result


def iota(dims, dim):
    return lax.broadcasted_iota(jnp.int32, dims, dim)


def ones_where(mask):
    return jnp.where(mask, 1.0, 0.0).astype(BF16)


def halves(v):
    top = v.astype(BF16)
    return jnp.concatenate([top, (v - top.astype(F32)).astype(BF16)], axis=1)


def pick_rounded(chosen, v):
    width = v.shape[1]
    out = jnp.dot(chosen, halves(v), preferred_element_type=F32)
    return out[:, :width] + out[:, width:]


def split(v):
    top = v.astype(BF16)
    rest = v - top.astype(F32)
    middle = rest.astype(BF16)
    low = (rest - middle.astype(F32)).astype(BF16)
    return jnp.concatenate([top, middle, low], axis=1)


def pick(chosen, v):
    width = v.shape[1]
    out = jnp.dot(chosen, split(v), preferred_element_type=F32)
    return out[:, :width] + out[:, width : 2 * width] + out[:, 2 * width :]


def total(v):
    return jnp.sum(jnp.sum(v, axis=1, keepdims=True), axis=0, keepdims=True)


def row_sums(v):
    return jnp.sum(v.T, axis=0, keepdims=True)


def as_column(row):
    return jnp.broadcast_to(row, (LANES, LANES)).T


def pack_body(at, cols, owner, cell, frac, kappa, x_own, send, slot_out, blocks):
    count = owner.shape[1]
    mine = at[0]
    own = owner[...]
    slot = jnp.zeros((1, count), jnp.int32)
    for first in range(0, count, LANES):
        column = jnp.broadcast_to(own[:, first : first + LANES], (LANES, LANES)).T
        column = jnp.concatenate([column] * (count // LANES), axis=1)
        before = iota((LANES, count), 0) + first < iota((LANES, count), 1)
        slot += jnp.sum(jnp.where((column == own) & before, 1, 0), axis=0, keepdims=True)
    slot_out[...] = slot
    here = iota((CAP, count), 0) == slot
    c, f = cell[...], frac[...]
    k = kappa[...]
    top = k.astype(BF16).astype(F32)
    middle = (k - top).astype(BF16).astype(F32)
    low = k - top - middle
    whole = [c >> 14, (c >> 8) & 63, c & 255, f >> 7, f & 127]
    rows = [jnp.where(here, v.astype(F32), 0.0) for v in whole]
    rows = jnp.concatenate([*rows, jnp.where(here, top, 0.0), jnp.zeros((LANES - 6 * CAP, count), F32)], axis=0)
    chosen = ones_where(iota((LANES, count), 0) == own)
    nt = functools.partial(
        lax.dot_general,
        dimension_numbers=(((1,), (1,)), ((), ())),
        preferred_element_type=F32,
    )

    def kappas(v):
        return jnp.concatenate(
            [
                jnp.zeros((KAPPA, count), F32),
                jnp.where(here, v, 0.0),
                jnp.zeros((LANES - 6 * CAP, count), F32),
            ],
            axis=0,
        ).astype(BF16)

    message = nt(chosen, rows.astype(BF16)) + nt(chosen, kappas(middle)) + nt(chosen, kappas(low))
    lane = iota((1, LANES), 1)
    extra = jnp.zeros((1, LANES), F32)
    for t in range(cols.shape[0]):
        column = jnp.where(iota((1, cols.shape[1]), 1) == mine, cols[t : t + 1, :], 0)
        column = jnp.sum(column, axis=1, keepdims=True).astype(F32)
        extra = jnp.where(lane == COLS + t, column, extra)
    blocks[...] = jnp.broadcast_to(x_own[pl.ds(mine, 1), :], (LANES, LANES))
    send[pl.ds(0, LANES, stride=2), :] = blocks[...]
    send[pl.ds(1, LANES, stride=2), :] = message + extra


def by_slot(message, k):
    x = message[:, X + k : X + k + 1].astype(jnp.int32)
    y = message[:, Y + k : Y + k + 1].astype(jnp.int32)
    z = message[:, Z + k : Z + k + 1].astype(jnp.int32)
    hi = message[:, HI + k : HI + k + 1].astype(jnp.int32)
    lo = message[:, LO + k : LO + k + 1].astype(jnp.int32)
    return x * 64 + y, z, hi, lo, message[:, KAPPA + k : KAPPA + k + 1]


def in_parts(source, target, arrived):
    parts = arrived.shape[0]
    each = source.shape[0] // parts
    copies = []
    for i in range(parts):
        part = pl.ds(i * each, each)
        copies.append(
            pltpu.make_async_copy(source.at[part], target.at[part], arrived.at[i])
        )
        copies[-1].start()
    return copies


def traces(message, pressure_all, pressure, here, gathered):
    copies = in_parts(pressure_all, pressure, here)
    rows, depth = pressure.shape
    chosen = jnp.concatenate(
        [ones_where(iota((LANES, rows), 1) == by_slot(message, k)[0]) for k in range(CAP)], axis=0
    )
    for copy in copies:
        copy.wait()
    gathered[...] = pick_rounded(chosen, pressure[...])
    return at_depth(message, gathered)


def at_depth(message, gathered):
    depth = gathered.shape[1]
    lane = iota((LANES, LANES), 1)
    out = jnp.zeros((LANES, LANES), F32)
    for k in range(CAP):
        z = by_slot(message, k)[1]
        part = gathered[k * LANES : (k + 1) * LANES, :]
        value = jnp.sum(jnp.where(iota((LANES, depth), 1) == z, part, 0.0), axis=1, keepdims=True)
        out = jnp.where(lane == k, value, out)
    return out


def at_mortar(message, x):
    chosen = jnp.concatenate(
        [ones_where(iota((LANES, LANES), 1) == by_slot(message, k)[2]) for k in range(CAP)], axis=0
    )
    found = pick(chosen, x)
    lane = iota((LANES, LANES), 1)
    out = jnp.zeros((LANES, LANES), F32)
    for k in range(CAP):
        part = found[k * LANES : (k + 1) * LANES, :]
        value = jnp.sum(jnp.where(lane == by_slot(message, k)[3], part, 0.0), axis=1, keepdims=True)
        out = jnp.where(lane == k, value, out)
    return out


def onto_fracture(message, *values):
    flipped = message.T
    hi = jnp.concatenate([flipped[HI + k : HI + k + 1, :] for k in range(CAP)], axis=1)
    chosen = ones_where(iota((LANES, CAP * LANES), 0) == hi.astype(jnp.int32))
    lane = iota((LANES, LANES), 1)
    wide = []
    for v in values:
        spread = [
            jnp.where(lane == by_slot(message, k)[3], v[:, k : k + 1], 0.0) for k in range(CAP)
        ]
        wide.append(jnp.concatenate(spread, axis=0))
    return [pick(chosen, v) for v in wide]


def kappa_of(message):
    lane = iota((LANES, LANES), 1)
    out = jnp.zeros((LANES, LANES), F32)
    for k in range(CAP):
        out = jnp.where(lane == k, message[:, KAPPA + k : KAPPA + k + 1], out)
    return out


def first_body(
    at,
    cols,
    tiles_all,
    pressure_all,
    got,
    diag,
    source,
    send,
    x_out,
    trace_out,
    flux_out,
    message_out,
    gathered,
    part,
    tiles,
    arrived,
    pressure,
    here,
):
    mine, shard = at[0], at[1]
    per_row = cols.shape[0]
    fetch = pltpu.make_async_copy(tiles_all.at[pl.ds(per_row * mine, per_row)], tiles, arrived)
    fetch.start()
    groups = LANES // CAP
    for m in range(CAP):
        x_out[pl.ds(m, groups, stride=CAP), :] = got[
            pl.ds(2 * m * groups, groups, stride=2), :
        ]
    message = got[pl.ds(1, LANES, stride=2), :]
    message_out[...] = message
    trace = traces(message, pressure_all, pressure, here, gathered)
    kappa = kappa_of(message)
    flux = kappa * (trace - at_mortar(message, x_out[...]))
    load, weight = onto_fracture(message, flux, kappa)
    part[...] = load
    row = CAP * shard + mine
    x_row = x_out[pl.ds(row, 1), :]
    x_col = as_column(x_row)
    mixed = jnp.zeros((LANES, LANES), F32)
    fetch.wait()
    for t in range(per_row):
        tile = tiles[t]
        mixed += tile * x_out[pl.ds(cols[t, mine], 1), :]
        back = jnp.sum(tile * x_col, axis=0, keepdims=True)
        part[pl.ds(cols[t, mine], 1), :] -= 0.5 * back
    part[pl.ds(row, 1), :] += source[pl.ds(mine, 1), :] - (
        diag[pl.ds(mine, 1), :] * x_row + 0.5 * row_sums(mixed)
    )
    send[pl.ds(0, LANES, stride=2), :] = part[...]
    send[pl.ds(1, LANES, stride=2), :] = weight
    trace_out[...] = trace
    flux_out[...] = flux


def spread_flux(message, values, spread, cell_row, depth):
    flipped = message.T
    for k in range(CAP):
        z = by_slot(message, k)[1]
        placed = jnp.where(iota((LANES, depth), 1) == z, values[:, k : k + 1], 0.0)
        spread[k * LANES : (k + 1) * LANES, :] = halves(placed)
        cell_row[:, k * LANES : (k + 1) * LANES] = (
            flipped[X + k : X + k + 1, :] * 64 + flipped[Y + k : Y + k + 1, :]
        ).astype(jnp.int32)


def sources(rows, step, spread, cell_row):
    depth = spread.shape[1] // 2
    row = iota((rows, CAP * LANES), 0) + step * rows
    chosen = ones_where(row == cell_row[...])
    out = jnp.dot(chosen, spread[...], preferred_element_type=F32)
    return out[:, :depth] + out[:, depth:]


def second_traces(message, trace, gathered, trace_out, send):
    now = at_depth(message, gathered)
    trace_out[...] = now
    [change] = onto_fracture(message, kappa_of(message) * (now - trace))
    mats = CAP
    each = LANES // mats
    for m in range(mats):
        part = slice(m * each, (m + 1) * each)
        send[2 * m * each : (2 * m + 1) * each, :] = change[part, :]
        send[(2 * m + 1) * each : (2 * m + 2) * each, :] = now[part, :]


def home_body(got, owner, slot, frac, kappa, x, flux, *, mats):
    count = owner.shape[1]

    def found(values, chosen):
        top = values.astype(BF16).astype(F32)
        middle = (values - top).astype(BF16).astype(F32)
        parts = jnp.concatenate([top, middle, values - top - middle], axis=0)
        if parts.shape[0] % 16:
            parts = jnp.concatenate([parts, jnp.zeros_like(top)], axis=0)
        out = jnp.dot(parts.astype(BF16), chosen, preferred_element_type=F32)
        n = values.shape[0]
        return out[:n] + out[n : 2 * n] + out[2 * n : 3 * n]

    shards = LANES // mats
    own = owner[...]
    source = (own & (shards - 1)) * mats + own // shards
    traces_all = found(got[...].T[:CAP, :], ones_where(iota((LANES, count), 0) == source))
    here = iota((CAP, count), 0) == slot[...]
    trace = jnp.sum(jnp.where(here, traces_all, 0.0), axis=0, keepdims=True)
    f = frac[...]
    x_all = found(x[...].T, ones_where(iota((LANES, count), 0) == f >> 7))
    here = iota((LANES, count), 0) == (f & 127)
    x_there = jnp.sum(jnp.where(here, x_all, 0.0), axis=0, keepdims=True)
    flux[...] = kappa[...] * (trace - x_there)


def sum_body(got, send):
    for i in range(2):
        mine = jnp.sum(got[pl.ds(i, LANES, stride=2), :], axis=0, keepdims=True)
        send[pl.ds(i, LANES, stride=2), :] = jnp.broadcast_to(mine, (LANES, LANES))


def columns_body(got, chosen, *, shards, rows, tiles):
    flipped = got[pl.ds(1, LANES, stride=2), :].T[COLS : COLS + CAP, :]
    count = shards * rows * tiles
    tile = iota((LANES, count), 1)
    sender = (tile // tiles) % rows * shards + tile // (rows * tiles)
    moved = jnp.dot(
        jnp.concatenate([flipped, flipped], axis=0).astype(BF16),
        ones_where(iota((LANES, count), 0) == sender),
        preferred_element_type=F32,
    )[:CAP]
    here = iota((CAP, count), 0) == iota((CAP, count), 1) % tiles
    column = jnp.sum(jnp.where(here, moved, 0.0), axis=0, keepdims=True).astype(jnp.int32)
    chosen[...] = ones_where(iota((LANES, count), 0) == column)


def products(at, cols, d, tiles, diag, block):
    shard = at[1]
    per_row, rows = cols.shape
    for r in range(rows):
        d_row = d[pl.ds(CAP * shard + r, 1), :]
        d_col = as_column(d_row)
        mixed = jnp.zeros((LANES, LANES), F32)
        for t in range(per_row):
            tile = tiles[per_row * r + t]
            mixed += tile * d[pl.ds(cols[t, r], 1), :]
            back = jnp.sum(tile * d_col, axis=0, keepdims=True)
            block[rows + per_row * r + t : rows + per_row * r + t + 1, :] = 0.5 * back
        block[r : r + 1, :] = diag[r : r + 1, :] * d_row + 0.5 * row_sums(mixed)


def image_of(got, chosen, step, rows, tiles):
    shards = got.shape[0] // step
    own = jnp.concatenate([got[s * step : s * step + rows, :] for s in range(shards)], axis=0)
    back = jnp.concatenate(
        [got[s * step + rows : s * step + rows + tiles, :] for s in range(shards)], axis=0
    )
    return own + pick(chosen[...], back)


def start_body(at, cols, tiles, got, diag, r_out, weight_out, send, block):
    r_out[...] = got[pl.ds(0, LANES, stride=2), :]
    weight_out[...] = got[pl.ds(1, LANES, stride=2), :]
    products(at, cols, r_out, tiles, diag, block)
    size = block.shape[0]
    for s in range(send.shape[0] // size):
        send[s * size : (s + 1) * size, :] = block[...]


def step_body(
    at, cols, tiles, got, chosen, diag, *rest, ride, last, faces_in, faces_out
):
    per_row, rows = cols.shape
    size = rows * (1 + per_row)
    shards = LANES // rows
    mats = rows
    extra = list(rest)
    change = extra.pop(0) if ride == "reduce" else None
    parts = [extra.pop(0) for _ in range(mats // 2)] if ride == "next" else None
    x, r, d = (extra.pop(0) for _ in range(3))
    if ride == "next":
        parts.insert(0, extra.pop(0))
    x_before, weight = (extra.pop(0), extra.pop(0)) if ride == "next" else (None, None)
    y_faces = (extra.pop(0), extra.pop(0)) if faces_out else None
    x_out, r_out, d_out, send = (extra.pop(0) for _ in range(4))
    change_out, home = (extra.pop(0), extra.pop(0)) if ride == "gather" else (None, None)
    y_halo = (extra.pop(0), extra.pop(0)) if faces_in else None
    block = extra.pop()
    got_step = got.shape[0] // shards
    shard = at[1]
    image = image_of(got, chosen, got_step, rows, rows * per_row)
    old = d[...]
    norm = total(r[...] * r[...])
    alpha = norm / total(old * image)
    x_new = x[...] + alpha * old
    r_new = r[...] - alpha * image
    x_out[...] = x_new
    if ride == "next":
        [whole_change] = extra
        k = 0
        for part in parts:
            for i in range(part.shape[0] // shards):
                place = pl.multiple_of((at[0] ^ k) * shards, shards)
                whole_change[pl.ds(place, shards), :] = part[i * shards : (i + 1) * shards, :]
                k += 1
        r_new = r_new + whole_change[...] - weight[...] * (x_new - x_before[...])
        d_out[...] = r_new
    else:
        d_out[...] = r_new + (total(r_new * r_new) / norm) * old
    r_out[...] = r_new
    if last:
        lanes = jnp.zeros((1, LANES), F32)
        for i in range(rows):
            d_row = d_out[pl.ds(CAP * shard + i, 1), :]
            mixed = jnp.zeros((LANES, LANES), F32)
            for t in range(per_row):
                mixed += tiles[per_row * i + t] * d_out[pl.ds(cols[t, i], 1), :]
            lanes += diag[i : i + 1, :] * d_row * d_row
            lanes += jnp.sum(mixed * as_column(d_row), axis=0, keepdims=True)
        send[...] = jnp.broadcast_to(lanes, send.shape)
    else:
        products(at, cols, d_out, tiles, diag, block)
        send_step = send.shape[0] // shards
        if ride == "reduce":
            found = change[:shards, :]
            for m in range(1, mats):
                found = found + change[2 * m * shards : (2 * m + 1) * shards, :]
        for s in range(shards):
            first = s * send_step
            send[first : first + size, :] = block[...]
            first += size
            if ride == "reduce":
                send[first : first + shards, :] = found
                for m in range(mats):
                    row = (2 * m + 1) * shards + s
                    send[first + shards + m : first + shards + m + 1, :] = change[row : row + 1, :]
                first += shards + mats
            if faces_out:
                face = jnp.where(shard < s, y_faces[1][...], y_faces[0][...])
                deep = face.shape[0]
                send[first : first + deep, :] = face[:, :LANES]
                send[first + deep : first + 2 * deep, :] = face[:, LANES:]
    first = size
    if ride == "gather":
        found = jnp.zeros((shards, LANES), F32)
        for s in range(shards):
            row = s * got_step + size
            found += got[row : row + shards, :]
            home[s * mats : (s + 1) * mats, :] = got[row + shards : row + shards + mats, :]
        change_out[...] = found
        first += shards + mats
    if faces_in:
        deep = y_halo[0].shape[0]
        for halo, other, there in (
            (y_halo[0], jnp.maximum(shard - 1, 0), shard > 0),
            (y_halo[1], jnp.minimum(shard + 1, shards - 1), shard < shards - 1),
        ):
            row = pl.multiple_of(other * got_step + first, 8)
            for half in range(2):
                values = got[pl.ds(row + half * deep, deep), :]
                halo[:, half * LANES : (half + 1) * LANES] = jnp.where(there, values, 0.0)


def final_body(at, got, x, r, d, out):
    alpha = total(r[...] * r[...]) / total(got[pl.ds(0, LANES // CAP, stride=CAP), :])
    here = pl.ds(pl.multiple_of(CAP * at[1], CAP), CAP)
    out[...] = x[here, :] + alpha * d[here, :]


def even(at, dim):
    return (at[dim] & 1) == 0


def edges_body(at, px0, px1, py0, py1, tx1, ty1, xa, xb, ya, yb):
    wide, deep = px0.shape[1], py0.shape[0]
    low, high = px0[0], px1[0]
    xa[:wide, :] = jnp.where(even(at, 0), high, low)
    xb[:wide, :] = jnp.where(even(at, 0), low, high)
    xa[wide:, :] = tx1[0, 0]
    xb[wide:, :] = tx1[0, 0]
    low, high = py0[:, 0, :], py1[:, 7, :]
    ya[:deep, :] = jnp.where(even(at, 1), high, low)
    yb[:deep, :] = jnp.where(even(at, 1), low, high)
    ya[deep:, :] = ty1[0, :, 7, :]
    yb[deep:, :] = ty1[0, :, 7, :]


def edges(at, pressure, trans):
    nx, ny, nz = pressure.shape
    y_last = ny // 8 - 1
    out = [(2 * ny, nz)] * 2 + [(2 * nx, nz)] * 2
    pressure, trans = in_hbm(pressure), in_hbm(trans)
    return pl.pallas_call(
        edges_body,
        grid=(1,),
        out_shape=tuple(sent(*v) for v in out),
        in_specs=[
            SMEM,
            pl.BlockSpec((1, ny, nz), lambda i: (0, 0, 0)),
            pl.BlockSpec((1, ny, nz), lambda i: (nx - 1, 0, 0)),
            pl.BlockSpec((nx, 8, nz), lambda i: (0, 0, 0)),
            pl.BlockSpec((nx, 8, nz), lambda i: (0, y_last, 0)),
            pl.BlockSpec((1, 1, ny, nz), lambda i: (0, nx - 1, 0, 0)),
            pl.BlockSpec((1, nx, 8, nz), lambda i: (1, 0, y_last, 0)),
        ],
        out_specs=tuple(pl.BlockSpec(v, lambda i: (0, 0)) for v in out),
        compiler_params=params(),
        name="edges",
    )(at, pressure, pressure, pressure, pressure, trans, trans)


def sweep_body(
    at,
    xa,
    xb,
    ya,
    yb,
    cxa,
    cxb,
    cya,
    cyb,
    p,
    p_after,
    trans,
    rhs,
    *rest,
    first,
    last,
    fluxes,
    gather,
    y_in,
    y_out,
):
    rest = list(rest)
    cell = rest.pop(0) if first else None
    weight = None if first else rest.pop(0)
    if fluxes or gather:
        got, values = rest.pop(0), [rest.pop(0) for _ in range(fluxes + gather)]
    out = rest.pop(0)
    weight_out = rest.pop(0) if first else None
    rhs_out = rest.pop(0) if fluxes else None
    trace_out, cuts = (rest.pop(0), rest.pop(0)) if gather else (None, None)
    gathered = rest.pop() if gather else None
    if fluxes:
        found, spread, cell_row = rest.pop(), rest.pop(), rest.pop()
    carry_t = rest.pop() if first else None
    carry = rest.pop()
    step = pl.program_id(0)
    steps = pl.num_programs(0)
    many, ny, nz = out.shape
    nx = ya.shape[0] if not first else ya.shape[0] // 2
    row = iota((ny, nz), 0)
    lane = iota((ny, nz), 1)
    x_even, y_even = even(at, 0), even(at, 1)

    @pl.when(step == 0)
    def _():
        if fluxes == 1:
            spread_flux(got[...], values[0][...], spread, cell_row, nz)
        if fluxes == 2:
            message = got[...]
            flux = values[0][...] - at_mortar(message, values[1][...])
            spread_flux(message, kappa_of(message) * flux, spread, cell_row, nz)
        tx_low = jnp.where(x_even, cxb[ny:, :], cxa[ny:, :])
        carry[...] = tx_low * jnp.where(x_even, xb[:ny, :], xa[:ny, :])
        if first:
            carry_t[...] = tx_low

    if fluxes:
        found[...] = sources(many * ny, step, spread, cell_row)
    for i in range(many):
        here_at = step * many + i
        right = rhs[i]
        if fluxes:
            right = right + found[i * ny : (i + 1) * ny, :]
            rhs_out[i] = right
        here = p[i]
        if i + 1 < many:
            after = p[i + 1]
        else:
            x_high = jnp.where(x_even, xa[:ny, :], xb[:ny, :])
            after = jnp.where(step + 1 < steps, p_after[0], x_high)
        one = pl.ds(here_at, 1)
        edge = pl.ds(nx + here_at, 1)
        y_low, y_high = ya[one, :], yb[one, :]
        if not y_in:
            y_low, y_high = jnp.where(y_even, y_high, y_low), jnp.where(y_even, y_low, y_high)
        ty_edge = jnp.where(y_even, cyb[edge, :], cya[edge, :])
        tx, ty, tz = trans[0, i], trans[1, i], trans[2, i]
        y_next = jnp.where(row == ny - 1, y_high, pltpu.roll(here, ny - 1, 0))
        y_prev = jnp.where(row == 0, ty_edge * y_low, pltpu.roll(ty * here, 1, 0))
        z_next = jnp.where(lane == nz - 1, 0.0, pltpu.roll(here, nz - 1, 1))
        z_prev = jnp.where(lane == 0, 0.0, pltpu.roll(tz * here, 1, 1))
        if first:
            ty_before = jnp.where(row == 0, ty_edge, pltpu.roll(ty, 1, 0))
            tz_before = jnp.where(lane == 0, 0.0, pltpu.roll(tz, 1, 1))
            diagonal = cell[i] + tx + carry_t[...] + ty + ty_before + tz + tz_before
            w = WEIGHT / diagonal
            weight_out[i] = w
            carry_t[...] = tx
        else:
            w = weight[i]
        around = (tx * after + carry[...]) + (ty * y_next + y_prev) + (tz * z_next + z_prev)
        carry[...] = tx * here
        out[i] = (1.0 - WEIGHT) * here + w * (right + around)
    if gather:
        message = got[...]
        rows = iota((LANES, many * ny), 1) + step * (many * ny)
        chosen = jnp.concatenate(
            [ones_where(rows == by_slot(message, k)[0]) for k in range(CAP)], axis=0
        )
        planes = jnp.concatenate([out[i] for i in range(many)], axis=0)
        found = pick_rounded(chosen, planes)

        @pl.when(step == 0)
        def _():
            gathered[...] = found

        @pl.when(step > 0)
        def _():
            gathered[...] += found

        @pl.when(step == steps - 1)
        def _():
            second_traces(message, values[0][...], gathered, trace_out, cuts)

    if last:
        return
    xa_out, xb_out, ya_out, yb_out = rest
    start, end = step == 0, step == steps - 1

    @pl.when(start & x_even)
    def _():
        xb_out[...] = out[0]

    @pl.when(start & ~x_even)
    def _():
        xa_out[...] = out[0]

    @pl.when(end & x_even)
    def _():
        xa_out[...] = out[many - 1]

    @pl.when(end & ~x_even)
    def _():
        xb_out[...] = out[many - 1]

    for i in range(many):
        one = pl.ds(step * many + i, 1)
        low, high = out[i, :1, :], out[i, ny - 1 :, :]
        if not y_out:
            low, high = jnp.where(y_even, high, low), jnp.where(y_even, low, high)
        ya_out[one, :] = low
        yb_out[one, :] = high


def sweep(
    at,
    p,
    halo,
    faces,
    trans,
    rhs,
    cell=None,
    weight=None,
    last=False,
    got=None,
    values=(),
    gather=False,
    y_in=False,
    y_out=False,
    many=8,
):
    nx, ny, nz = p.shape
    part = pl.BlockSpec((many, ny, nz), lambda i: (i, 0, 0))
    x_face = pl.BlockSpec((ny, nz), lambda i: (0, 0))
    y_face = pl.BlockSpec((nx, nz), lambda i: (0, 0))
    first = weight is None
    out_shape, out_specs = [shape(nx, ny, nz)], [part]
    if first:
        out_shape.append(shape(nx, ny, nz))
        out_specs.append(part)
    scratch = [pltpu.VMEM((ny, nz), F32)] * (2 if first else 1)
    if gather:
        out_shape += [sent(LANES, LANES), sent(2 * LANES, LANES)]
        out_specs += [whole((LANES, LANES)), whole((2 * LANES, LANES))]
        scratch.append(pltpu.VMEM((CAP * LANES, nz), F32))
    elif values:
        out_shape.append(shape(nx, ny, nz))
        out_specs.append(part)
        scratch += [
            pltpu.VMEM((1, CAP * LANES), jnp.int32),
            pltpu.VMEM((CAP * LANES, 2 * nz), BF16),
            pltpu.VMEM((many * ny, nz), F32),
        ]
    if not last:
        out_shape += [sent(ny, nz)] * 2 + [sent(nx, nz)] * 2
        out_specs += [x_face, x_face, y_face, y_face]
    after = pl.BlockSpec(
        (1, ny, nz), lambda i: (jnp.minimum((i + 1) * many, nx - 1), 0, 0)
    )
    if y_in:
        halo = (*halo[:2], *(in_hbm(v, 1) for v in halo[2:]))
    operands = [*halo, *faces, p, p, trans, rhs, cell if first else weight]
    operands += [in_hbm(v, 1) for v in (got, *values)] if values else []
    return pl.pallas_call(
        functools.partial(
            sweep_body,
            first=first,
            last=last,
            fluxes=0 if gather else len(values),
            gather=gather,
            y_in=y_in,
            y_out=y_out,
        ),
        grid=(nx // many,),
        out_shape=tuple(out_shape),
        in_specs=[SMEM]
        + [whole(v.shape) for v in (*halo, *faces)]
        + [part, after]
        + [pl.BlockSpec((3, many, ny, nz), lambda i: (0, i, 0, 0)), part, part]
        + ([whole(v.shape) for v in (got, *values)] if values else []),
        out_specs=tuple(out_specs),
        scratch_shapes=scratch,
        compiler_params=params(),
        cost_estimate=pl.CostEstimate(flops=6_000_000, bytes_accessed=8 << 20, transcendentals=0),
        name="sweep",
    )(at, *(in_hbm(v) for v in operands))


def swap(v, axis, count, low):
    pairs = [(i, i + 1) for i in range(low, count - 1, 2)]
    return lax.ppermute(v, axis, pairs + [(b, a) for a, b in pairs])


def swapped(xa, xb, ya, yb, mats, shards):
    return (
        swap(xa, "mat", mats, 0),
        swap(xb, "mat", mats, 1),
        swap(ya, "frac", shards, 0),
        swap(yb, "frac", shards, 1),
    )


def body(
    pressure_start,
    face_trans,
    cell_coef,
    matrix_source,
    mortar_owner,
    mortar_cell,
    mortar_frac,
    mortar_kappa,
    tiles,
    tile_cols,
    frac_diag,
    frac_source,
    fracture_start,
):
    nx, ny, nz = pressure_start.shape
    mats, shards = lax.axis_size("mat"), lax.axis_size("frac")
    rows, per_row = tile_cols.shape
    count = mortar_cell.shape[0]
    size = rows * (1 + per_row)
    at = jnp.stack([lax.axis_index("mat"), lax.axis_index("frac")]).astype(jnp.int32)
    everyone = functools.partial(
        lax.all_to_all, axis_name=("mat", "frac"), split_axis=0, concat_axis=0, tiled=True
    )
    over_frac = functools.partial(
        lax.all_to_all, axis_name="frac", split_axis=0, concat_axis=0, tiled=True
    )
    over_mat = functools.partial(
        lax.all_to_all, axis_name="mat", split_axis=0, concat_axis=0, tiled=True
    )
    square = shape(LANES, LANES)
    owner = mortar_owner.reshape(1, count)
    frac, kappa = mortar_frac.reshape(1, count), mortar_kappa.reshape(1, count)
    flat = (nx * ny, nz)
    tile_list = tiles.reshape(rows * per_row, LANES, LANES)
    diag = frac_diag.reshape(rows, LANES)
    square_scratch = pltpu.VMEM((LANES, LANES), F32)
    gathered = pltpu.VMEM((CAP * LANES, nz), F32)
    block = pltpu.VMEM((size, LANES), F32)
    scalars = (at, tile_cols.T)
    fetch_scratch = [pltpu.VMEM(flat, F32), pltpu.SemaphoreType.DMA((8,))]

    send, slot = call(
        pack_body,
        (sent(2 * LANES, LANES), pltpu.HBM((1, count), jnp.int32)),
        tile_cols.T,
        owner,
        mortar_cell.reshape(1, count),
        frac,
        kappa,
        fracture_start.reshape(rows, LANES),
        scalars=(at,),
        scratch=[square_scratch],
        name="pack",
        least=1,
    )
    send, edges_at = lax.optimization_barrier((send, at))
    got = everyone(send)

    faces = swapped(*edges(edges_at, pressure_start, face_trans), mats, shards)

    send, x_start, trace, flux, message = call(
        first_body,
        (sent(2 * LANES, LANES), *[sent(LANES, LANES)] * 4),
        got,
        diag,
        frac_source.reshape(rows, LANES),
        scalars=scalars,
        raw=(tile_list, pressure_start.reshape(flat)),
        scratch=[
            gathered,
            square_scratch,
            pltpu.VMEM((per_row, LANES, LANES), F32),
            pltpu.SemaphoreType.DMA(()),
            *fetch_scratch,
        ],
        flops=2e9,
        name="first",
    )
    send, *faces = lax.optimization_barrier((send, *faces))
    reduced = everyone(send)
    pressure, weight, rhs, *sides = sweep(
        at, pressure_start, faces, faces, face_trans, matrix_source, cell_coef, got=message, values=(flux,)
    )
    sides = swapped(*sides, mats, shards)

    send = call(sum_body, sent(2 * LANES, LANES), reduced, name="sums")
    send, pressure = lax.optimization_barrier((send, pressure))
    residuals = everyone(send)
    chosen = call(
        functools.partial(columns_body, shards=shards, rows=rows, tiles=per_row),
        shape(LANES, shards * rows * per_row, dtype=BF16),
        got,
        name="columns",
    )
    r, sums, send = call(
        start_body,
        (*[sent(LANES, LANES)] * 2, sent(shards * size, LANES)),
        residuals,
        diag,
        scalars=scalars,
        resident=(tile_list,),
        scratch=[block],
        name="start",
    )
    x, d = x_start, r
    send, pressure, *sides = lax.optimization_barrier((send, pressure, *sides))
    arrived = over_frac(send)
    pressure, trace, change, *sides = sweep(
        at,
        pressure,
        sides,
        faces,
        face_trans,
        rhs,
        weight=weight,
        got=message,
        values=(trace,),
        gather=True,
        y_out=True,
    )

    arrived, change = lax.optimization_barrier((arrived, change))
    change = over_mat(change)
    arrived, change = lax.optimization_barrier((arrived, change))

    def step(arrived, x, r, d, *more, ride=None, last=False, faces_in=False, faces=(), side=()):
        length = size + (shards + mats if ride == "reduce" else 0) + (2 * nx if faces else 0)
        outs = [*[sent(LANES, LANES)] * 3, sent(shards * (rows if last else length), LANES)]
        if ride == "gather":
            outs += [sent(shards, LANES), sent(LANES, LANES)]
        if faces_in:
            outs += [sent(nx, nz)] * 2
        return call(
            functools.partial(
                step_body, ride=ride, last=last, faces_in=faces_in, faces_out=bool(faces)
            ),
            tuple(outs),
            arrived,
            chosen,
            diag,
            *more,
            side=(x, r, d, *side, *faces),
            scalars=scalars,
            resident=(tile_list,),
            scratch=([square_scratch] if ride == "next" else []) + [block],
            name="step",
        )

    def swapped_mat(xa, xb):
        return swap(xa, "mat", mats, 0), swap(xb, "mat", mats, 1)

    x, r, d, send = step(arrived, x, r, d, change, ride="reduce")
    send, trace, *x_sides = lax.optimization_barrier((send, trace, *sides[:2]))
    arrived = over_frac(send)
    x_sides = swapped_mat(*x_sides)
    arrived, *x_sides = lax.optimization_barrier((arrived, *x_sides))

    x, r, d, send, change, home = step(arrived, x, r, d, ride="gather", faces=sides[2:])
    arrived = over_frac(send)
    parts = [change, lax.ppermute(change, "mat", [(i, i ^ 1) for i in range(mats)])]
    pair = jnp.concatenate(parts, axis=0)
    for hop in range(2, mats, 2):
        parts.append(lax.ppermute(pair, "mat", [(i, i ^ hop) for i in range(mats)]))

    x, r, d, send, *y_sides = step(
        arrived, x, r, d, *parts[1:], faces_in=True, ride="next", side=(change, x_start, sums)
    )
    x_flux = x
    arrived = over_frac(send)
    pressure, rhs, *sides = sweep(
        at,
        pressure,
        (*x_sides, *y_sides),
        faces,
        face_trans,
        matrix_source,
        weight=weight,
        got=message,
        values=(trace, x_flux),
        y_in=True,
        y_out=True,
    )
    arrived, pressure, *sides = lax.optimization_barrier((arrived, pressure, *sides))
    x, r, d, send = step(arrived, x, r, d, faces=sides[2:])
    send, home, *sides = lax.optimization_barrier((send, home, *sides[:2]))
    arrived = over_frac(send)
    x_sides = swapped_mat(*sides)
    flux = call(
        functools.partial(home_body, mats=mats),
        shape(1, count),
        side=(home, owner, slot, frac, kappa, x_flux),
        name="home",
    )
    arrived, flux, *x_sides = lax.optimization_barrier((arrived, flux, *x_sides))
    x, r, d, send, *y_sides = step(arrived, x, r, d, last=True, faces_in=True)
    send, pressure, flux = lax.optimization_barrier((send, pressure, flux))
    arrived = over_frac(send)
    [pressure] = sweep(
        at,
        pressure,
        (*x_sides, *y_sides),
        faces,
        face_trans,
        rhs,
        weight=weight,
        last=True,
        y_in=True,
    )
    fracture = call(
        final_body, shape(rows, LANES), arrived, side=(x, r, d), scalars=(at,), name="final"
    )
    return pressure, fracture.reshape(rows * LANES), flux.reshape(count)


def solution(mesh):
    in_specs = (
        P("mat", "frac", None),
        P(None, "mat", "frac", None),
        P("mat", "frac", None),
        P("mat", "frac", None),
        P(("mat", "frac"), None),
        P(("mat", "frac")),
        P(("mat", "frac")),
        P(("mat", "frac")),
        P("frac", None, None, None),
        P("frac", None),
        P("frac"),
        P("frac"),
        P("frac"),
    )
    out_specs = (P("mat", "frac", None), P("frac"), P(("mat", "frac")))
    return jax.shard_map(body, mesh=mesh, in_specs=in_specs, out_specs=out_specs, check_vma=False)
```
